128 devices in a mesh: gz: 4 (over y_lo, core), gy: 32 (over z, y_hi, x).
Axes of the slice: x: 4, y: 4 (y_hi: 2, y_lo: 2; y = y_hi * 2 + y_lo), z: 4, core: 2. Of those that a mesh axis runs over, the one named last changes fastest.
Arguments:
- input_field: float32 [32, 16, 256, 256], P(None, 'gz', 'gy'), may hold values from -6 to 6
- pre_activation: float32 [32, 16, 256, 256], P(None, 'gz', 'gy'), may hold values from -8 to 8
- cotangent: float32 [32, 16, 256, 256], P(None, 'gz', 'gy'), may hold values from -6 to 6
- spectral_weights: float32 [2, 16, 32, 32, 32, 32], P(None, None, 'gz', 'gy'), may hold values from -4.2426405 to 4.2426405
- mix_weights: float32 [32, 32], replicated, may hold values from -1 to 1
- coefficients: float32 [5, 32], replicated, may hold values from -3 to 3
Outputs:
- grad_input: float32 [32, 16, 256, 256], P(None, 'gz', 'gy')
- grad_spectral: float32 [2, 16, 32, 32, 32, 32], P(None, None, 'gz', 'gy')
- grad_mix: float32 [32, 32], replicated
- grad_coef: float32 [5, 32], replicated
The draws below stay inside these ranges and needn't reach their ends.
All inputs are finite; a program needn't handle non-finite values.
Results may differ from the reference program's by a relative error of at most 0.00013.
Values sent between devices are 32-bit elements; how exact they have to be, the bound alone decides.
A program may use at most 192 MiB of HBM per device.

```python
import math
import jax
import jax.numpy as jnp
from jax import lax

C = 32
X = 256
KX = 32
KY = 32
KZ = 16
Y = 256
Z = 16
CELLS = 1048576


def block_scale(stream_key, dims, cuts, least, largest):
    factor_of, own = 1.0, jax.random.fold_in(stream_key, 6)
    for axis_at, parts in cuts:
        heights = jnp.exp(jax.random.uniform(jax.random.fold_in(own, axis_at), (parts,), jnp.float32, least / len(cuts), largest / len(cuts)))
        factor_of = factor_of * jnp.repeat(heights, dims[axis_at] // parts).reshape([-1 if axis == axis_at else 1 for axis in range(len(dims))])
    return factor_of


def scatter_about(own_key, dims, width, reach, split=(), kind=jnp.bfloat16):
    factor_of = block_scale(own_key, dims, split, -0.22, 0.18) if split else 1.0
    array = jax.random.normal(own_key, dims, jnp.float32) * width * factor_of
    return jnp.minimum(jnp.maximum(array, -reach), reach).astype(kind)


def setup_inputs(seed: int = 0) -> dict:
    streams_of = jax.random.split(jax.random.key(seed), 7)
    input_field = scatter_about(streams_of[0], (C, Z, Y, X), 1.0, 6.0, ((1, 4), (2, 32)), jnp.float32)
    pre_activation = scatter_about(streams_of[1], (C, Z, Y, X), 1.5, 8.0, ((1, 4), (2, 32)), jnp.float32)
    cotangent = scatter_about(streams_of[2], (C, Z, Y, X), 1.0, 6.0, ((1, 4), (2, 32)), jnp.float32)
    spectral_weights = scatter_about(streams_of[3], (2, KZ, KY, KX, C, C), (4.0 / C ** 0.5), 4.2426405, ((2, 4), (3, 32)), jnp.float32)
    mix_weights = scatter_about(streams_of[4], (C, C), C ** -0.5, 1.0, (), jnp.float32)
    coefficients = scatter_about(streams_of[5], (5, C), 0.5, 3.0, (), jnp.float32)
    return {"input_field": input_field, "pre_activation": pre_activation, "cotangent": cotangent, "spectral_weights": spectral_weights, "mix_weights": mix_weights, "coefficients": coefficients}


HIGHEST_PRECISION = lax.Precision.HIGHEST


def gelu_slope(values):
    normal_cdf = 0.5 * (1.0 + jax.scipy.special.erf(values * 0.7071067811865476))
    return normal_cdf + values * jnp.exp(-0.5 * values * values) * 0.3989422804014327


def mode_numbers(number):
    positions = jnp.arange(number, dtype=jnp.int32)
    return jnp.where(positions < number // 2, positions, positions - number).astype(jnp.int32)


def twiddle(cell_index, mode_index, period):
    product = jnp.remainder(cell_index[:, None] * mode_index[None, :], period).astype(jnp.float32)
    angles = product * (2.0 * math.pi / period)
    return jnp.cos(angles), jnp.sin(angles)


def rotate_pair(pair, cos_table, sin_table, formula, inverse):
    real_cos = jnp.einsum(formula, pair[0], cos_table, precision=HIGHEST_PRECISION)
    real_sin = jnp.einsum(formula, pair[0], sin_table, precision=HIGHEST_PRECISION)
    imag_cos = jnp.einsum(formula, pair[1], cos_table, precision=HIGHEST_PRECISION)
    imag_sin = jnp.einsum(formula, pair[1], sin_table, precision=HIGHEST_PRECISION)
    if inverse:
        return jnp.stack([real_cos - imag_sin, imag_cos + real_sin])
    return jnp.stack([real_cos + imag_sin, imag_cos - real_sin])


def mixing(hat_input, hat_slope, weights):
    outer = 'oljk,cljk->ljkoc'
    grad_re = jnp.einsum(outer, hat_slope[0], hat_input[0]) + jnp.einsum(outer, hat_slope[1], hat_input[1])
    grad_im = jnp.einsum(outer, hat_slope[1], hat_input[0]) - jnp.einsum(outer, hat_slope[0], hat_input[1])
    inner = 'ljkoc,oljk->cljk'
    dual_re = jnp.einsum(inner, weights[0], hat_slope[0], precision=HIGHEST_PRECISION) + jnp.einsum(inner, weights[1], hat_slope[1], precision=HIGHEST_PRECISION)
    dual_im = jnp.einsum(inner, weights[0], hat_slope[1], precision=HIGHEST_PRECISION) - jnp.einsum(inner, weights[1], hat_slope[0], precision=HIGHEST_PRECISION)
    return jnp.stack([grad_re, grad_im]), jnp.stack([dual_re, dual_im])


def neighbours(padded):
    return [padded[:, 1:-1, 1:-1], padded[:, 1:-1, 2:], padded[:, 1:-1, :-2], padded[:, 2:, 1:-1], padded[:, :-2, 1:-1]]


def adjoint_rims(padded):
    return [padded[:, 1:-1, 1:-1], padded[:, 1:-1, :-2], padded[:, 1:-1, 2:], padded[:, :-2, 1:-1], padded[:, 2:, 1:-1]]


def weighted(coefficients, pieces):
    total = coefficients[0][:, None, None, None] * pieces[0]
    for place in range(1, 5):
        total = total + coefficients[place][:, None, None, None] * pieces[place]
    return total


def tables():
    cos_x, sin_x = twiddle(jnp.arange(X, dtype=jnp.int32), mode_numbers(KX), X)
    cos_y, sin_y = twiddle(jnp.arange(Y, dtype=jnp.int32), mode_numbers(KY), Y)
    cos_z, sin_z = twiddle(jnp.arange(Z, dtype=jnp.int32), mode_numbers(KZ), Z)
    return cos_x, sin_x, cos_y, sin_y, cos_z, sin_z


def spectrum(values):
    cos_x, sin_x, cos_y, sin_y, cos_z, sin_z = tables()
    pair = jnp.stack([jnp.einsum('czyx,xk->czyk', values, cos_x, precision=HIGHEST_PRECISION),
                      -jnp.einsum('czyx,xk->czyk', values, sin_x, precision=HIGHEST_PRECISION)])
    pair = rotate_pair(pair, cos_y, sin_y, 'czyk,yj->czjk', False)
    return rotate_pair(pair, cos_z, sin_z, 'czjk,zl->cljk', False)


def reference(input_field, pre_activation, cotangent, spectral_weights, mix_weights, coefficients):
    slope_field = cotangent * gelu_slope(pre_activation)
    hat_input = spectrum(input_field)
    hat_slope = spectrum(slope_field) / CELLS
    grad_spectral, dual = mixing(hat_input, hat_slope, spectral_weights)
    cos_x, sin_x, cos_y, sin_y, cos_z, sin_z = tables()
    returned = rotate_pair(dual, cos_z, sin_z, 'cljk,zl->czjk', True)
    returned = rotate_pair(returned, cos_y, sin_y, 'czjk,yj->czyk', True)
    spectral_part = jnp.einsum('czyk,xk->czyx', returned[0], cos_x, precision=HIGHEST_PRECISION) - jnp.einsum('czyk,xk->czyx', returned[1], sin_x, precision=HIGHEST_PRECISION)
    pad_width = ((0, 0), (1, 1), (1, 1), (0, 0))
    pieces = neighbours(jnp.pad(input_field, pad_width))
    stencil = weighted(coefficients, pieces)
    hidden = jnp.einsum('oc,ozyx->czyx', mix_weights, slope_field, precision=HIGHEST_PRECISION)
    grad_mix = jnp.einsum('ozyx,czyx->oc', slope_field, stencil, precision=HIGHEST_PRECISION) / 1024.0
    grad_coef = jnp.stack([jnp.sum(hidden * piece, axis=(1, 2, 3)) for piece in pieces]) / 1024.0
    grad_input = weighted(coefficients, adjoint_rims(jnp.pad(hidden, pad_width))) + spectral_part
    return grad_input, grad_spectral, grad_mix, grad_coef
```

```python
import math

import jax
import jax.numpy as jnp
from jax import lax
from jax.sharding import PartitionSpec as P

HIGHEST_PRECISION = lax.Precision.HIGHEST


def padded_2(shard, sides, width):
    for axis, dim in sides:
        size, length = (lax.axis_size(axis), shard.shape[dim])
        up = [(i, (i + 1) % size) for i in range(size - 1)]
        down = [(j, i) for i, j in up]
        last = lax.slice_in_dim(shard, length - width, length, axis=dim)
        leading = lax.slice_in_dim(shard, 0, width, axis=dim)
        before = lax.ppermute(last, axis, up)
        after = lax.ppermute(leading, axis, down)
        shard = jnp.concatenate([before, shard, after], axis=dim)
    return shard


def gelu_slope(values):
    normal_cdf = 0.5 * (1.0 + jax.scipy.special.erf(values * 0.7071067811865476))
    return normal_cdf + values * jnp.exp(-0.5 * values * values) * 0.3989422804014327


def mode_numbers(number):
    positions = jnp.arange(number, dtype=jnp.int32)
    return jnp.where(positions < number // 2, positions, positions - number)


def twiddle(cell_index, mode_index, period):
    product = jnp.remainder(cell_index[:, None] * mode_index[None, :], period).astype(jnp.float32)
    angles = product * (2.0 * math.pi / period)
    return (jnp.cos(angles), jnp.sin(angles))


def rotate_pair(pair, cos_table, sin_table, formula, inverse):
    real_cos = jnp.einsum(formula, pair[0], cos_table, precision=HIGHEST_PRECISION)
    real_sin = jnp.einsum(formula, pair[0], sin_table, precision=HIGHEST_PRECISION)
    imag_cos = jnp.einsum(formula, pair[1], cos_table, precision=HIGHEST_PRECISION)
    imag_sin = jnp.einsum(formula, pair[1], sin_table, precision=HIGHEST_PRECISION)
    if inverse:
        return jnp.stack([real_cos - imag_sin, imag_cos + real_sin])
    return jnp.stack([real_cos + imag_sin, imag_cos - real_sin])


def mixing(hat_input, hat_slope, weights):
    outer = "oljk,cljk->ljkoc"
    grad_re = jnp.einsum(outer, hat_slope[0], hat_input[0]) + jnp.einsum(
        outer, hat_slope[1], hat_input[1]
    )
    grad_im = jnp.einsum(outer, hat_slope[1], hat_input[0]) - jnp.einsum(
        outer, hat_slope[0], hat_input[1]
    )
    inner = "ljkoc,oljk->cljk"
    dual_re = jnp.einsum(inner, weights[0], hat_slope[0], precision=HIGHEST_PRECISION) + jnp.einsum(
        inner, weights[1], hat_slope[1], precision=HIGHEST_PRECISION
    )
    dual_im = jnp.einsum(inner, weights[0], hat_slope[1], precision=HIGHEST_PRECISION) - jnp.einsum(
        inner, weights[1], hat_slope[0], precision=HIGHEST_PRECISION
    )
    return (jnp.stack([grad_re, grad_im]), jnp.stack([dual_re, dual_im]))


def neighbours(padded):
    return [
        padded[:, 1:-1, 1:-1],
        padded[:, 1:-1, 2:],
        padded[:, 1:-1, :-2],
        padded[:, 2:, 1:-1],
        padded[:, :-2, 1:-1],
    ]


def adjoint_rims(padded):
    return [
        padded[:, 1:-1, 1:-1],
        padded[:, 1:-1, :-2],
        padded[:, 1:-1, 2:],
        padded[:, :-2, 1:-1],
        padded[:, 2:, 1:-1],
    ]


def weighted(coefficients, pieces):
    total = coefficients[0][:, None, None, None] * pieces[0]
    for place in range(1, 5):
        total = total + coefficients[place][:, None, None, None] * pieces[place]
    return total


def per_device(input_field, pre_activation, cotangent, spectral_weights, mix_weights, coefficients):
    channels, depth_dev, rows_dev, length = input_field.shape
    groups_y = lax.axis_size("gy")
    groups_z = lax.axis_size("gz")
    grid_y = rows_dev * groups_y
    grid_z = depth_dev * groups_z
    cell_total = length * grid_y * grid_z
    modes_z = spectral_weights.shape[1]
    owned_y = spectral_weights.shape[2]
    owned_x = spectral_weights.shape[3]
    modes_y = owned_y * groups_z
    modes_x = owned_x * groups_y
    slope_field = cotangent * gelu_slope(pre_activation)
    cos_x, sin_x = twiddle(jnp.arange(length, dtype=jnp.int32), mode_numbers(modes_x), length)

    row_cells = jnp.arange(grid_y, dtype=jnp.int32)
    depth_cells = jnp.arange(grid_z, dtype=jnp.int32)
    cos_y, sin_y = twiddle(row_cells, mode_numbers(modes_y), grid_y)
    cos_z, sin_z = twiddle(depth_cells, mode_numbers(modes_z), grid_z)
    forward_x = jnp.stack([cos_x, -sin_x])
    fields = jnp.stack([input_field, slope_field])
    lines = jnp.einsum("fczyx,rxk->kyfrcz", fields, forward_x, precision=HIGHEST_PRECISION)
    lines = lax.all_to_all(lines, "gy", 0, 0, tiled=True)
    lines = lines.reshape(groups_y, owned_x * rows_dev, 2, 2, channels, depth_dev)
    lines = lines.reshape(grid_y, 2, 2, channels, depth_dev)
    turned = rotate_pair(
        jnp.moveaxis(lines, 2, 0), cos_y, sin_y, "yfcz,yj->jfcz", False
    )
    turned = lax.all_to_all(jnp.moveaxis(turned, 1, 0), "gz", 0, 0, tiled=True)
    turned = turned.reshape(groups_z, owned_y, 2, 2, channels, depth_dev)
    hats = rotate_pair(
        jnp.transpose(turned, (2, 3, 4, 0, 5, 1)).reshape(2, 2, channels, grid_z, owned_y),
        cos_z, sin_z, "fczj,zl->fclj", False,
    )[..., None]
    grad_spectral, dual = mixing(hats[:, 0], hats[:, 1] / cell_total, spectral_weights)
    returned = rotate_pair(dual[..., 0], cos_z, sin_z, "clj,zl->zjc", True)
    returned = lax.all_to_all(jnp.moveaxis(returned, 0, 1), "gz", 0, 0, tiled=True)
    returned = returned.reshape(groups_z, depth_dev, 2, owned_y, channels)
    returned = jnp.transpose(returned, (2, 0, 3, 1, 4)).reshape(2, modes_y, depth_dev, channels)
    returned = rotate_pair(returned, cos_y, sin_y, "jzc,yj->yzc", True)
    returned = lax.all_to_all(jnp.moveaxis(returned, 0, 1), "gy", 0, 0, tiled=True)
    returned = returned.reshape(modes_x, rows_dev, 2, depth_dev, channels)
    spectral_part = jnp.einsum("kyrzc,rxk->czyx", returned, forward_x, precision=HIGHEST_PRECISION)
    padded_input = padded_2(input_field, (("gz", 1), ("gy", 2)), 1)
    hidden = jnp.einsum("oc,ozyx->czyx", mix_weights, slope_field, precision=HIGHEST_PRECISION)
    padded_hidden = padded_2(hidden, (("gz", 1), ("gy", 2)), 1)
    pieces = neighbours(padded_input)
    stencil = weighted(coefficients, pieces)
    local_mix = jnp.einsum("ozyx,czyx->oc", slope_field, stencil, precision=HIGHEST_PRECISION)
    local_coef = jnp.stack([jnp.sum(hidden * piece, axis=(1, 2, 3)) for piece in pieces])
    total_mix, total_coef = lax.psum((local_mix, local_coef), ("gz", "gy"))
    grad_input = weighted(coefficients, adjoint_rims(padded_hidden)) + spectral_part
    return (grad_input, grad_spectral, total_mix / 1024.0, total_coef / 1024.0)


def solution(mesh):
    in_specs = (
        P(None, "gz", "gy", None),
        P(None, "gz", "gy", None),
        P(None, "gz", "gy", None),
        P(None, None, "gz", "gy", None, None),
        P(),
        P(),
    )
    out_specs = (P(None, "gz", "gy", None), P(None, None, "gz", "gy", None, None), P(), P())
    return jax.shard_map(
        per_device, mesh=mesh, in_specs=in_specs, out_specs=out_specs, check_vma=False
    )
```

```python
import functools
import math

import jax
import jax.numpy as jnp
import numpy as np
from jax import lax
from jax.experimental import pallas as pl
from jax.experimental.pallas import tpu as pltpu
from jax.sharding import PartitionSpec as P

F32 = jnp.float32
BF16 = jnp.bfloat16
MESH = pl.DeviceIdType.MESH
C = 32
ZL = 4
YL = 8
NX = 256
LANES = 128
NK = 128


def mode_numbers(number):
    positions = np.arange(number)
    return np.where(positions < number // 2, positions, positions - number)


def table(cells, modes):
    product = np.remainder(np.outer(mode_numbers(modes), np.arange(cells)), cells)
    angles = product * (2.0 * math.pi / cells)
    return np.cos(angles), np.sin(angles)


def split(a):
    high = a.astype(BF16)
    return high, (a - high.astype(F32)).astype(BF16)


def dot1(a, b, dims):
    return lax.dot_general(a, b, (dims, ((), ())), preferred_element_type=F32)


def dot3(a, b, dims):
    a_high, a_low = a if isinstance(a, tuple) else split(a)
    b_high, b_low = b if isinstance(b, tuple) else split(b)
    return dot1(a_high, b_low, dims) + dot1(a_low, b_high, dims) + dot1(a_high, b_high, dims)


NN = ((1,), (0,))
NT = ((1,), (1,))
TN = ((0,), (0,))


def gelu_slope(values):
    normal_cdf = 0.5 * (1.0 + lax.erf(values * 0.7071067811865476))
    return normal_cdf + values * jnp.exp(-0.5 * values * values) * 0.3989422804014327


def dft4(re, im, sign):
    ar, ai = re[0] + re[2], im[0] + im[2]
    br, bi = re[0] - re[2], im[0] - im[2]
    cr, ci = re[1] + re[3], im[1] + im[3]
    dr, di = re[1] - re[3], im[1] - im[3]
    if sign < 0:
        return [ar + cr, br + di, ar - cr, br - di], [ai + ci, bi - dr, ai - ci, bi + dr]
    return [ar + cr, br - di, ar - cr, br + di], [ai + ci, bi + dr, ai - ci, bi - dr]


def turn(re, im, cos, sin, sign):
    if sign < 0:
        return re * cos + im * sin, im * cos - re * sin
    return re * cos - im * sin, im * cos + re * sin


def plane(ref, start, size):
    return jnp.concatenate([ref[half, pl.ds(start, size), :] for half in range(2)], axis=1)


def put_plane(ref, start, value):
    for half in range(2):
        ref[half, pl.ds(start, value.shape[0]), :] = value[:, half * LANES : (half + 1) * LANES]


def iota(shape, axis):
    return lax.broadcasted_iota(jnp.int32, shape, axis)


def exchange_kernel(
    groups_y, groups_z, phases, cell_total,
    inp_hbm, pre_hbm, cot_hbm, wts_hbm, mix_ref, coef_ref, wx_ref, wy_ref, wyt_ref, tw_ref,
    lines_out, sten_out, hin_out, hsl_out, red_out,
    inp4, pre4, cot4, wts, inp2, slo2, sbuf, rbuf, zsend, zrecv, zsend2, zrecv2, sbuf2,
    hy_send, hy_recv, hz_recv, hid, sten, hin, hsl, hslt, dual, red_send, red_recv, red_sum,
    load_sem, s1, r1, s2, r2, sz, rz, sz2, rz2, hs_sem, hr_sem, sr, rr, out_sem,
):
    gz = lax.axis_index("gz")
    gy = lax.axis_index("gy")
    modes_x = wx_ref.shape[0] // 2

    def load(i, src, dst):
        return pltpu.make_async_copy(src, dst, load_sem.at[i])

    load(0, inp_hbm, inp4).start()
    load(1, pre_hbm, pre4).start()
    load(2, cot_hbm, cot4).start()

    barrier = pltpu.get_barrier_semaphore()

    def greet(i, carry):
        peer = lax.rem(gy + i, groups_y)
        pl.semaphore_signal(barrier, inc=1, device_id=(gz, peer), device_id_type=MESH)
        return carry

    lax.fori_loop(1, groups_y, greet, 0)
    for i in range(1, groups_z):
        peer = lax.rem(gz + i, groups_z)
        pl.semaphore_signal(barrier, inc=1, device_id=(peer, gy), device_id_type=MESH)

    wx = split(wx_ref[...])

    def along_x(source, field):
        cells = jnp.concatenate(
            [
                jnp.concatenate(
                    [source[half, pl.ds(y, LANES, stride=YL), :] for half in range(2)], axis=1
                )
                for y in range(YL)
            ],
            axis=0,
        )
        result = dot3(wx, cells, NT)
        for y in range(YL):
            for part in range(2):
                sbuf[pl.ds((2 * field + part) * YL + y, modes_x, stride=4 * YL), :] = (
                    result[part * modes_x : (part + 1) * modes_x, y * LANES : (y + 1) * LANES]
                )

    load(0, inp_hbm, inp4).wait()
    for z in range(ZL):
        put_plane(inp2, z * 256, inp4[:, z].reshape(256, NX))
    along_x(inp2, 0)
    load(1, pre_hbm, pre4).wait()
    load(2, cot_hbm, cot4).wait()
    load(3, wts_hbm, wts).start()

    def slope_step(step, carry):
        z = step // 4
        c = lax.rem(step, 4) * 8
        pre = pre4[pl.ds(c, 8), z].reshape(64, NX)
        cot = cot4[pl.ds(c, 8), z].reshape(64, NX)
        put_plane(slo2, pl.multiple_of(step * 64, 64), cot * gelu_slope(pre))
        return carry

    lax.fori_loop(0, 16, slope_step, 0)
    along_x(slo2, 1)
    for z in range(ZL):
        for side, y in enumerate((YL - 1, 0)):
            for half in range(2):
                hy_send[side, half, pl.ds(z * C, C), :] = slo2[
                    half, pl.ds(z * 256 + y, C, stride=YL), :
                ]

    pl.semaphore_wait(barrier, groups_y - 1 + groups_z - 1)

    def rows(ref, index, size=YL):
        return ref.at[pl.ds(pl.multiple_of(index * size, size), size), :]

    def first(i):
        peer = lax.rem(gy + i, groups_y)
        return pltpu.make_async_remote_copy(
            rows(sbuf, peer, 4 * YL), rows(rbuf, gy, 4 * YL), s1.at[peer], r1.at[gy],
            device_id=(gz, peer), device_id_type=MESH,
        )

    def first_in(i):
        peer = lax.rem(gy + i, groups_y)
        return pltpu.make_async_remote_copy(
            rows(sbuf, peer, 4 * YL), rows(rbuf, peer, 4 * YL), s1.at[peer], r1.at[peer],
            device_id=(gz, peer), device_id_type=MESH,
        )

    def second(i):
        peer = lax.rem(gy + i, groups_y)
        return pltpu.make_async_remote_copy(
            rows(sbuf2, peer, 2 * YL), rows(lines_out, gy, 2 * YL), s2.at[peer], r2.at[gy],
            device_id=(gz, peer), device_id_type=MESH,
        )

    def second_in(i):
        peer = lax.rem(gy + i, groups_y)
        return pltpu.make_async_remote_copy(
            rows(sbuf2, peer, 2 * YL), rows(lines_out, peer, 2 * YL), s2.at[peer], r2.at[peer],
            device_id=(gz, peer), device_id_type=MESH,
        )

    def across(source, target, send, recv, i, inward):
        peer = lax.rem(gz + i, groups_z)
        slot = peer if inward else gz
        return pltpu.make_async_remote_copy(
            rows(source, peer), rows(target, slot), send.at[peer], recv.at[slot],
            device_id=(peer, gy), device_id_type=MESH,
        )

    def each(make, action):
        def body(i, carry):
            getattr(make(i), action)()
            return carry

        lax.fori_loop(1, groups_y, body, 0)

    each(first, "start")
    own_lines = pl.ds(pl.multiple_of(gy * 4 * YL, 4 * YL), 4 * YL)
    rbuf[own_lines, :] = sbuf[own_lines, :]

    next_z, prev_z = lax.rem(gz + 1, groups_z), lax.rem(gz + groups_z - 1, groups_z)
    next_y, prev_y = lax.rem(gy + 1, groups_y), lax.rem(gy + groups_y - 1, groups_y)
    halos = []
    for i, (source, target, device) in enumerate(
        (
            (slo2.at[:, pl.ds(3 * 256, 256), :], hz_recv.at[0], (next_z, gy)),
            (slo2.at[:, pl.ds(0, 256), :], hz_recv.at[1], (prev_z, gy)),
            (hy_send.at[0], hy_recv.at[0], (gz, next_y)),
            (hy_send.at[1], hy_recv.at[1], (gz, prev_y)),
        )
    ):
        halos.append(
            pltpu.make_async_remote_copy(
                source, target, hs_sem.at[i], hr_sem.at[i], device_id=device, device_id_type=MESH
            )
        )
        halos[-1].start()

    has_before_z = jnp.where(gz > 0, 1.0, 0.0)
    has_after_z = jnp.where(gz < groups_z - 1, 1.0, 0.0)
    has_before_y = jnp.where(gy > 0, 1.0, 0.0)
    has_after_y = jnp.where(gy < groups_y - 1, 1.0, 0.0)
    mix = mix_ref[...]
    coef = coef_ref[...]
    expand = (lax.shift_right_logical(iota((256, C), 0), 3) == iota((256, C), 1)).astype(F32)
    gather = (lax.shift_right_logical(iota((C, 256), 1), 3) == iota((C, 256), 0)).astype(F32)
    row_y = lax.bitwise_and(iota((256, 256), 0), 7)
    col_y = lax.bitwise_and(iota((256, 256), 1), 7)

    for halo in halos:
        halo.wait_recv()
    def outside(which):
        if which < 2:
            return plane(hz_recv.at[which], 0, 256) * (has_before_z, has_after_z)[which]
        return plane(hy_recv.at[which - 2], 0, ZL * C) * (has_before_y, has_after_y)[which - 2]

    before_z, after_z, before_y, after_y = [outside(which) for which in range(4)]
    planes = [before_z] + [plane(slo2, z * 256, 256) for z in range(ZL)] + [after_z]
    for z in range(ZL):
        right = split(plane(inp2, z * 256, 256))
        left = split(
            jnp.concatenate(
                [planes[z + 1], planes[z], planes[z + 2],
                 before_y[z * C : (z + 1) * C], after_y[z * C : (z + 1) * C]], axis=0,
            )
        )
        term = dot3(left, right, NT)
        gram = term if z == 0 else gram + term
    gram_0, gram_up, gram_down = gram[0:256], gram[256:512], gram[512:768]
    same = row_y == col_y
    pieces = jnp.concatenate(
        [
            jnp.where(same, gram_0, 0.0),
            jnp.where(col_y == row_y + 1, gram_0, 0.0),
            jnp.where(col_y == row_y - 1, gram_0, 0.0),
            jnp.where(same, gram_up, 0.0),
            jnp.where(same, gram_down, 0.0),
        ],
        axis=1,
    )
    summed = dot3(gather, pieces, NN)
    edge_y = col_y[0:C]
    sums = [summed[:, j * 256 : (j + 1) * 256] for j in range(5)]
    sums[1] = sums[1] + jnp.where(edge_y == 0, gram[768 : 768 + C], 0.0)
    sums[2] = sums[2] + jnp.where(edge_y == YL - 1, gram[768 + C : 768 + 2 * C], 0.0)
    moments = [dot3(part, expand, NN) for part in sums]
    red_send[...] = jnp.zeros_like(red_send)
    local_mix = coef[0:1, :] * moments[0]
    for j in range(1, 5):
        local_mix = local_mix + coef[j : j + 1, :] * moments[j]
    red_send[0, 0:C, 0:C] = local_mix
    for j in range(5):
        red_send[0, C + j : C + j + 1, 0:C] = jnp.sum(mix * moments[j], axis=0, keepdims=True)

    def place(phase):
        stride, size = phases[phase]
        if stride == 0:
            return size, gz
        return size, lax.rem(gy // stride, size)

    def piece(phase, i, inward):
        stride, _ = phases[phase]
        size, mine = place(phase)
        peer = lax.rem(mine + i, size)
        slot = peer if inward else mine
        device = (peer, gy) if stride == 0 else (gz, gy + (peer - mine) * stride)
        return pltpu.make_async_remote_copy(
            red_send.at[phase], red_recv.at[phase, slot], sr.at[phase, i], rr.at[phase, slot],
            device_id=device, device_id_type=MESH,
        )

    def tree_send(phase):
        size, mine = place(phase)
        for i in range(1, size):
            piece(phase, i, False).start()
        red_recv[phase, mine] = red_send[phase]

    def tree_take(phase):
        size, _ = place(phase)
        for i in range(1, size):
            piece(phase, i, True).wait_recv()
        total = red_recv[phase, 0]
        for j in range(1, size):
            total = total + red_recv[phase, j]
        if phase + 1 < len(phases):
            red_send[phase + 1] = total
        else:
            red_sum[...] = total * (1.0 / 1024.0)

    tree_send(0)

    each(first_in, "wait_recv")
    received = rbuf[...].reshape(groups_y, 4, YL, LANES)
    received = jnp.concatenate(
        [received[:, part].reshape(groups_y * YL, LANES) for part in range(4)], axis=1
    )
    turned = dot3(wy_ref[...], received, NN)
    cos_part, sin_part = turned[0:32], turned[32:64]
    for field in range(2):
        re = slice(2 * field * LANES, (2 * field + 1) * LANES)
        im = slice((2 * field + 1) * LANES, (2 * field + 2) * LANES)
        zsend[:, re] = cos_part[:, re] + sin_part[:, im]
        zsend[:, im] = cos_part[:, im] - sin_part[:, re]
    for i in range(1, groups_z):
        across(zsend, zrecv, sz, rz, i, False).start()
    own = pl.ds(pl.multiple_of(gz * 8, 8), 8)
    zrecv[own, :] = zsend[own, :]
    tree_take(0)
    if len(phases) > 1:
        tree_send(1)
    for i in range(1, groups_z):
        across(zsend, zrecv, sz, rz, i, True).wait_recv()

    cos_z = [tw_ref[2 * k : 2 * k + 1, :] for k in range(4)]
    sin_z = [tw_ref[2 * k + 1 : 2 * k + 2, :] for k in range(4)]
    for field in range(2):
        base = 2 * field * LANES
        re = [zrecv[q * 8 : q * 8 + 8, base : base + LANES] for q in range(4)]
        im = [zrecv[q * 8 : q * 8 + 8, base + LANES : base + 2 * LANES] for q in range(4)]
        re, im = dft4(re, im, -1)
        for k in range(4):
            t_re, t_im = re[k], im[k]
            if k:
                t_re, t_im = turn(t_re, t_im, cos_z[k], sin_z[k], -1)
            f_re, f_im = dft4(
                [t_re] + [pltpu.roll(t_re, LANES - 32 * s, 1) for s in range(1, 4)],
                [t_im] + [pltpu.roll(t_im, LANES - 32 * s, 1) for s in range(1, 4)],
                -1,
            )
            for m in range(4):
                at = pl.ds((k + 4 * m) * 8, 8)
                if field == 0:
                    hin[0, at, :] = f_re[m]
                    hin[1, at, :] = f_im[m]
                else:
                    hsl[0, at, :] = f_re[m] * (1.0 / cell_total)
                    hsl[1, at, :] = f_im[m] * (1.0 / cell_total)
    for part in range(2):
        hslt[part] = hsl[part].T[0:C, :]

    load(3, wts_hbm, wts).wait()

    def dual_step(kz, carry):
        shift = lax.rem(NK - kz * 8, NK)
        slope_re = pltpu.roll(hslt[0], shift, 1)
        slope_im = pltpu.roll(hslt[1], shift, 1)
        for j in range(8):
            k = kz * 8 + j
            s_re = jnp.broadcast_to(slope_re[:, j : j + 1], (C, C))
            s_im = jnp.broadcast_to(slope_im[:, j : j + 1], (C, C))
            w_re, w_im = wts[0, k], wts[1, k]
            dual[0, pl.ds(k, 1), 0:C] = jnp.sum(w_re * s_re + w_im * s_im, axis=0, keepdims=True)
            dual[1, pl.ds(k, 1), 0:C] = jnp.sum(w_re * s_im - w_im * s_re, axis=0, keepdims=True)
        return carry

    lax.fori_loop(0, 16, dual_step, 0)

    block = lax.shift_right_logical(iota((8, LANES), 1), 5)
    v_re, v_im = [], []
    for k in range(4):
        u_re, u_im = dft4(
            [dual[0, pl.ds((k + 4 * m) * 8, 8), :] for m in range(4)],
            [dual[1, pl.ds((k + 4 * m) * 8, 8), :] for m in range(4)],
            1,
        )
        packed = []
        for u in (u_re, u_im):
            value = u[0]
            for s in range(1, 4):
                value = jnp.where(block == s, pltpu.roll(u[s], 32 * s, 1), value)
            packed.append(value)
        if k:
            packed = turn(packed[0], packed[1], cos_z[k], sin_z[k], 1)
        v_re.append(packed[0])
        v_im.append(packed[1])
    v_re, v_im = dft4(v_re, v_im, 1)
    for q in range(4):
        zsend2[q * 8 : q * 8 + 8, 0:LANES] = v_re[q]
        zsend2[q * 8 : q * 8 + 8, LANES : 2 * LANES] = v_im[q]
    for i in range(1, groups_z):
        across(zsend2, zrecv2, sz2, rz2, i, False).start()
    zrecv2[own, :] = zsend2[own, :]
    if len(phases) > 1:
        tree_take(1)
    if len(phases) > 2:
        tree_send(2)
    for i in range(1, groups_z):
        across(zsend2, zrecv2, sz2, rz2, i, True).wait_recv()

    upper = zrecv2[...]
    lower = jnp.concatenate([-upper[:, LANES:], upper[:, :LANES]], axis=1)
    back = dot3(wyt_ref[...], jnp.concatenate([upper, lower], axis=0), NN)
    sbuf2[...] = jnp.concatenate(
        [
            back[:, part * LANES : (part + 1) * LANES].reshape(groups_y, 1, YL, LANES)
            for part in range(2)
        ],
        axis=1,
    ).reshape(groups_y * 2 * YL, LANES)
    each(second, "start")
    own_rows = pltpu.make_async_copy(rows(sbuf2, gy, 2 * YL), rows(lines_out, gy, 2 * YL), out_sem.at[0])
    own_rows.start()
    if len(phases) > 2:
        tree_take(2)
    if len(phases) > 3:
        tree_send(3)

    coef_rows = dot3(expand, coef, NT)
    coef_col = [coef_rows[:, j : j + 1] for j in range(5)]
    full = dot3(dot3(expand, mix, NT), expand, NT)
    weight = jnp.concatenate(
        [
            full
            * (
                jnp.where(same, coef_col[0], 0.0)
                + jnp.where(row_y == col_y + 1, coef_col[1], 0.0)
                + jnp.where(row_y == col_y - 1, coef_col[2], 0.0)
            ),
            jnp.where(same, full, 0.0),
        ],
        axis=0,
    )
    weight = split(weight)
    for z in range(ZL):
        both = dot3(weight, plane(slo2, z * 256, 256), NN)
        put_plane(sten, z * 256, both[0:256])
        hid[z + 1] = both[256:512]
    plain = (weight[0][256:512], weight[1][256:512])
    hid[0] = dot3(plain, outside(0), NN)
    hid[5] = dot3(plain, outside(1), NN)
    for z in range(ZL):
        total = plane(sten, z * 256, 256) + coef_col[3] * hid[z] + coef_col[4] * hid[z + 2]
        put_plane(sten, z * 256, total)
    coef_small = dot3(
        (iota((C, C), 0) == iota((C, C), 1)).astype(F32), coef, NT
    )
    edges = jnp.concatenate(
        [outside(2)[z * C : (z + 1) * C] for z in range(ZL)]
        + [outside(3)[z * C : (z + 1) * C] for z in range(ZL)],
        axis=1,
    )
    edge_hidden = dot3(mix, edges, TN)
    for z in range(ZL):
        for side, y in enumerate((0, YL - 1)):
            at = pl.ds(z * 256 + y, C, stride=YL)
            for half in range(2):
                column = (side * ZL + z) * NX + half * LANES
                sten[half, at, :] = (
                    sten[half, at, :]
                    + coef_small[:, 1 + side : 2 + side]
                    * edge_hidden[:, column : column + LANES]
                )
    outs = [
        pltpu.make_async_copy(sten, sten_out, out_sem.at[1]),
        pltpu.make_async_copy(hin, hin_out, out_sem.at[2]),
        pltpu.make_async_copy(hslt, hsl_out, out_sem.at[3]),
    ]
    for out in outs:
        out.start()
    if len(phases) > 3:
        tree_take(3)
    total_out = pltpu.make_async_copy(red_sum, red_out, out_sem.at[4])
    total_out.start()

    each(second_in, "wait_recv")
    own_rows.wait()
    for out in outs:
        out.wait()
    total_out.wait()
    each(first, "wait_send")
    each(second, "wait_send")
    for halo in halos:
        halo.wait_send()
    for i in range(1, groups_z):
        across(zsend, zrecv, sz, rz, i, False).wait_send()
        across(zsend2, zrecv2, sz2, rz2, i, False).wait_send()
    for phase in range(len(phases)):
        for i in range(1, place(phase)[0]):
            piece(phase, i, False).wait_send()


def result_kernel(
    lines, sten, hin, hsl, red, wx_ref,
    grad_input, grad_spectral, grad_mix, grad_coef,
    cells, spectral, out_sem,
):
    modes_x = wx_ref.shape[0] // 2

    def part(kz):
        at = pl.ds(kz * 8, 8)
        return pltpu.make_async_copy(
            spectral.at[:, at], grad_spectral.at[:, at], out_sem.at[kz]
        )

    def outer_step(kz, carry):
        shift = lax.rem(NK - kz * 8, NK)
        slope_re = pltpu.roll(hsl[0], shift, 1)
        slope_im = pltpu.roll(hsl[1], shift, 1)
        for j in range(8):
            k = kz * 8 + j
            s_re = jnp.broadcast_to(slope_re[:, j : j + 1], (C, C))
            s_im = jnp.broadcast_to(slope_im[:, j : j + 1], (C, C))
            i_re = hin[0, pl.ds(k, 1), 0:C]
            i_im = hin[1, pl.ds(k, 1), 0:C]
            spectral[0, k] = s_re * i_re + s_im * i_im
            spectral[1, k] = s_im * i_re - s_re * i_im
        part(kz).start()
        return carry

    lax.fori_loop(0, 16, outer_step, 0)
    grad_mix[...] = red[0:C, 0:C]
    grad_coef[...] = red[C : C + 5, 0:C]
    spread = jnp.concatenate(
        [
            jnp.concatenate(
                [lines[pl.ds(part * YL + y, modes_x, stride=2 * YL), :] for y in range(YL)], axis=1
            )
            for part in range(2)
        ],
        axis=0,
    )
    result = dot3(spread, wx_ref[...], TN)
    for y in range(YL):
        for half in range(2):
            cells[half, pl.ds(y, LANES, stride=YL), :] = result[
                y * LANES : (y + 1) * LANES, half * LANES : (half + 1) * LANES
            ]
    for z in range(ZL):
        total = plane(cells, z * 256, 256) + plane(sten, z * 256, 256)
        grad_input[:, z] = total.reshape(C, YL, NX)

    def finish(kz, carry):
        part(kz).wait()
        return carry

    lax.fori_loop(0, 16, finish, 0)


def per_device(input_field, pre_activation, cotangent, spectral_weights, mix_weights, coefficients):
    groups_y = lax.axis_size("gy")
    groups_z = lax.axis_size("gz")
    grid_y = YL * groups_y
    modes_x = groups_y
    cell_total = NX * grid_y * ZL * groups_z
    phases = ((0, groups_z), (1, 4), (4, 2), (8, 4)) if groups_y == 32 else ((0, groups_z), (1, 4))
    rows_y = groups_y * YL
    cos_x, sin_x = table(NX, modes_x)
    cos_y, sin_y = table(grid_y, 32)
    wx = np.concatenate([cos_x, -sin_x]).astype(np.float32)
    wy = np.concatenate([cos_y, sin_y]).astype(np.float32)
    cell = np.arange(LANES) // C
    tw = np.stack(
        [fn(2.0 * math.pi * k * cell / 16.0) for k in range(4) for fn in (np.cos, np.sin)]
    ).astype(np.float32)
    weights = spectral_weights.reshape(2, NK, C, C)
    vmem = pl.BlockSpec(memory_space=pltpu.VMEM)
    anyspace = pl.BlockSpec(memory_space=pl.ANY)
    sds = jax.ShapeDtypeStruct
    dma = pltpu.SemaphoreType.DMA
    lines, sten, hin, hsl, red = pl.pallas_call(
        functools.partial(exchange_kernel, groups_y, groups_z, phases, cell_total),
        name="exchange",
        out_shape=(
            sds((2 * rows_y, LANES), F32),
            sds((2, ZL * 256, LANES), F32),
            sds((2, NK, LANES), F32),
            sds((2, C, NK), F32),
            sds((40, LANES), F32),
        ),
        in_specs=[anyspace] * 4 + [vmem] * 6,
        out_specs=(anyspace,) * 5,
        scratch_shapes=[
            pltpu.VMEM((C, ZL, YL, NX), F32),
            pltpu.VMEM((C, ZL, YL, NX), F32),
            pltpu.VMEM((C, ZL, YL, NX), F32),
            pltpu.VMEM((2, NK, C, C), F32),
            pltpu.VMEM((2, ZL * 256, LANES), F32),
            pltpu.VMEM((2, ZL * 256, LANES), F32),
            pltpu.VMEM((4 * rows_y, LANES), F32),
            pltpu.VMEM((4 * rows_y, LANES), F32),
            pltpu.VMEM((32, 4 * LANES), F32),
            pltpu.VMEM((32, 4 * LANES), F32),
            pltpu.VMEM((32, 2 * LANES), F32),
            pltpu.VMEM((32, 2 * LANES), F32),
            pltpu.VMEM((2 * rows_y, LANES), F32),
            pltpu.VMEM((2, 2, ZL * C, LANES), F32),
            pltpu.VMEM((2, 2, ZL * C, LANES), F32),
            pltpu.VMEM((2, 2, 256, LANES), F32),
            pltpu.VMEM((6, 256, NX), F32),
            pltpu.VMEM((2, ZL * 256, LANES), F32),
            pltpu.VMEM((2, NK, LANES), F32),
            pltpu.VMEM((2, NK, LANES), F32),
            pltpu.VMEM((2, C, NK), F32),
            pltpu.VMEM((2, NK, LANES), F32),
            pltpu.VMEM((len(phases), 40, LANES), F32),
            pltpu.VMEM((len(phases), 4, 40, LANES), F32),
            pltpu.VMEM((40, LANES), F32),
            dma((4,)),
            dma((groups_y,)), dma((groups_y,)), dma((groups_y,)), dma((groups_y,)),
            dma((groups_z,)), dma((groups_z,)), dma((groups_z,)), dma((groups_z,)),
            dma((4,)), dma((4,)),
            dma((len(phases), 4)), dma((len(phases), 4)),
            dma((5,)),
        ],
        compiler_params=pltpu.CompilerParams(collective_id=0, has_side_effects=True),
    )(
        input_field, pre_activation, cotangent, weights, mix_weights, coefficients,
        jnp.asarray(wx), jnp.asarray(wy), jnp.asarray(wy.T.copy()), jnp.asarray(tw),
    )
    grad_input, grad_spectral, grad_mix, grad_coef = pl.pallas_call(
        result_kernel,
        name="result",
        out_shape=(
            sds((C, ZL, YL, NX), F32),
            sds((2, NK, C, C), F32),
            sds((C, C), F32),
            sds((5, C), F32),
        ),
        in_specs=[vmem] * 6,
        out_specs=(vmem, anyspace, vmem, vmem),
        scratch_shapes=[
            pltpu.VMEM((2, ZL * 256, LANES), F32),
            pltpu.VMEM((2, NK, C, C), F32),
            dma((16,)),
        ],
    )(lines, sten, hin, hsl, red, jnp.asarray(wx))
    return (grad_input, grad_spectral.reshape(spectral_weights.shape), grad_mix, grad_coef)


def solution(mesh):
    in_specs = (
        P(None, "gz", "gy", None),
        P(None, "gz", "gy", None),
        P(None, "gz", "gy", None),
        P(None, None, "gz", "gy", None, None),
        P(),
        P(),
    )
    out_specs = (P(None, "gz", "gy", None), P(None, None, "gz", "gy", None, None), P(), P())
    return jax.shard_map(
        per_device, mesh=mesh, in_specs=in_specs, out_specs=out_specs, check_vma=False
    )
```

```python
import functools
import math

import jax
import jax.numpy as jnp
import numpy as np
from jax import lax
from jax.experimental import pallas as pl
from jax.experimental.pallas import tpu as pltpu
from jax.sharding import PartitionSpec as P

F32 = jnp.float32
BF16 = jnp.bfloat16
MESH = pl.DeviceIdType.MESH
C = 32
ZL = 4
YL = 8
NX = 256
LANES = 128
NK = 128


def mode_numbers(number):
    positions = np.arange(number)
    return np.where(positions < number // 2, positions, positions - number)


def table(cells, modes):
    product = np.remainder(np.outer(mode_numbers(modes), np.arange(cells)), cells)
    angles = product * (2.0 * math.pi / cells)
    return np.cos(angles), np.sin(angles)


def split(a):
    high = a.astype(BF16)
    return high, (a - high.astype(F32)).astype(BF16)


def dot1(a, b, dims):
    return lax.dot_general(a, b, (dims, ((), ())), preferred_element_type=F32)


def dot3(a, b, dims):
    a_high, a_low = a if isinstance(a, tuple) else split(a)
    b_high, b_low = b if isinstance(b, tuple) else split(b)
    return dot1(a_high, b_low, dims) + dot1(a_low, b_high, dims) + dot1(a_high, b_high, dims)


NN = ((1,), (0,))
NT = ((1,), (1,))
TN = ((0,), (0,))


def gelu_slope(values):
    normal_cdf = 0.5 * (1.0 + lax.erf(values * 0.7071067811865476))
    return normal_cdf + values * jnp.exp(-0.5 * values * values) * 0.3989422804014327


def dft4(re, im, sign):
    ar, ai = re[0] + re[2], im[0] + im[2]
    br, bi = re[0] - re[2], im[0] - im[2]
    cr, ci = re[1] + re[3], im[1] + im[3]
    dr, di = re[1] - re[3], im[1] - im[3]
    if sign < 0:
        return [ar + cr, br + di, ar - cr, br - di], [ai + ci, bi - dr, ai - ci, bi + dr]
    return [ar + cr, br - di, ar - cr, br + di], [ai + ci, bi + dr, ai - ci, bi - dr]


def turn(re, im, cos, sin, sign):
    if sign < 0:
        return re * cos + im * sin, im * cos - re * sin
    return re * cos - im * sin, im * cos + re * sin


def plane(ref, start, size):
    return jnp.concatenate([ref[half, pl.ds(start, size), :] for half in range(2)], axis=1)


def put_plane(ref, start, value):
    for half in range(2):
        ref[half, pl.ds(start, value.shape[0]), :] = value[:, half * LANES : (half + 1) * LANES]


def offsets(groups_y):
    sizes = (4, 2, 4) if groups_y == 32 else (4,)
    result = []
    for i in range(1, groups_y):
        moves, rest = [], i
        for size in sizes:
            moves.append((size, rest % size))
            rest //= size
        hops = sum(min(m, n - m) * (2 if n == 2 else 1) for n, m in moves)
        result.append((-hops, tuple(moves)))
    return [moves for _, moves in sorted(result)]


def iota(shape, axis):
    return lax.broadcasted_iota(jnp.int32, shape, axis)


def exchange_kernel(
    groups_y, groups_z, phases, cell_total,
    inp_hbm, pre_hbm, cot_hbm, wts_hbm, mix_ref, coef_ref, wx_ref, wy_ref, wyt_ref, tw_ref,
    lines_out, sten, spectral, red_sum,
    inp4, pre4, cot4, wts, inp2, slo2, sbuf, rbuf, zsend, zrecv, zsend2, zrecv2, sbuf2,
    hy_send, hy_recv, hz_recv, hid, gram, hin, hsl, hslt, dual, red_send, red_recv,
    load_sem, s1, r1, s2, r2, sz, rz, sz2, rz2, hs_sem, hr_sem, sr, rr, out_sem,
):
    gz = lax.axis_index("gz")
    gy = lax.axis_index("gy")
    modes_x = wx_ref.shape[0] // 2

    def load(i, src, dst):
        return pltpu.make_async_copy(src, dst, load_sem.at[i])

    load(0, inp_hbm, inp4).start()
    load(1, pre_hbm, pre4).start()
    load(2, cot_hbm, cot4).start()

    barrier = pltpu.get_barrier_semaphore()

    def greet(i, carry):
        peer = lax.rem(gy + i, groups_y)
        pl.semaphore_signal(barrier, inc=1, device_id=(gz, peer), device_id_type=MESH)
        return carry

    lax.fori_loop(1, groups_y, greet, 0)
    for i in range(1, groups_z):
        peer = lax.rem(gz + i, groups_z)
        pl.semaphore_signal(barrier, inc=1, device_id=(peer, gy), device_id_type=MESH)

    wx = split(wx_ref[...])

    def along_x(source, field):
        cells = jnp.concatenate(
            [
                jnp.concatenate(
                    [source[half, pl.ds(y, LANES, stride=YL), :] for half in range(2)], axis=1
                )
                for y in range(YL)
            ],
            axis=0,
        )
        result = dot3(wx, cells, NT)
        for y in range(YL):
            for part in range(2):
                sbuf[pl.ds((2 * field + part) * YL + y, modes_x, stride=4 * YL), :] = (
                    result[part * modes_x : (part + 1) * modes_x, y * LANES : (y + 1) * LANES]
                )

    load(0, inp_hbm, inp4).wait()
    for z in range(ZL):
        put_plane(inp2, z * 256, inp4[:, z].reshape(256, NX))
    along_x(inp2, 0)
    load(1, pre_hbm, pre4).wait()
    load(2, cot_hbm, cot4).wait()
    load(3, wts_hbm, wts).start()

    def slope_step(step, carry):
        z = step // 4
        c = lax.rem(step, 4) * 8
        pre = pre4[pl.ds(c, 8), z].reshape(64, NX)
        cot = cot4[pl.ds(c, 8), z].reshape(64, NX)
        put_plane(slo2, pl.multiple_of(step * 64, 64), cot * gelu_slope(pre))
        return carry

    lax.fori_loop(0, 16, slope_step, 0)
    along_x(slo2, 1)
    for z in range(ZL):
        for side, y in enumerate((YL - 1, 0)):
            for half in range(2):
                hy_send[side, half, pl.ds(z * C, C), :] = slo2[
                    half, pl.ds(z * 256 + y, C, stride=YL), :
                ]

    pl.semaphore_wait(barrier, groups_y - 1 + groups_z - 1)

    def rows(ref, index, size=YL):
        return ref.at[pl.ds(pl.multiple_of(index * size, size), size), :]

    def partner(i):
        if isinstance(i, tuple):
            digits, stride, peer = gy, 1, 0
            for size, move in i:
                peer = peer + lax.rem(lax.rem(digits, size) + move, size) * stride
                digits, stride = digits // size, stride * size
            return peer
        return lax.rem(gy + i, groups_y)

    def first(i):
        peer = partner(i)
        return pltpu.make_async_remote_copy(
            rows(sbuf, peer, 4 * YL), rows(rbuf, gy, 4 * YL), s1.at[peer], r1.at[gy],
            device_id=(gz, peer), device_id_type=MESH,
        )

    def first_in(i):
        peer = lax.rem(gy + i, groups_y)
        return pltpu.make_async_remote_copy(
            rows(sbuf, peer, 4 * YL), rows(rbuf, peer, 4 * YL), s1.at[peer], r1.at[peer],
            device_id=(gz, peer), device_id_type=MESH,
        )

    def second(i):
        peer = partner(i)
        return pltpu.make_async_remote_copy(
            rows(sbuf2, peer, 2 * YL), rows(lines_out, gy, 2 * YL), s2.at[peer], r2.at[gy],
            device_id=(gz, peer), device_id_type=MESH,
        )

    def second_in(i):
        peer = lax.rem(gy + i, groups_y)
        return pltpu.make_async_remote_copy(
            rows(sbuf2, peer, 2 * YL), rows(lines_out, peer, 2 * YL), s2.at[peer], r2.at[peer],
            device_id=(gz, peer), device_id_type=MESH,
        )

    def across(source, target, send, recv, i, inward):
        peer = lax.rem(gz + i, groups_z)
        slot = peer if inward else gz
        return pltpu.make_async_remote_copy(
            rows(source, peer), rows(target, slot), send.at[peer], recv.at[slot],
            device_id=(peer, gy), device_id_type=MESH,
        )

    def each_far(make):
        for i in offsets(groups_y):
            make(i).start()

    def each(make, action):
        def body(i, carry):
            getattr(make(i), action)()
            return carry

        lax.fori_loop(1, groups_y, body, 0)

    each_far(first)
    own_lines = pl.ds(pl.multiple_of(gy * 4 * YL, 4 * YL), 4 * YL)
    rbuf[own_lines, :] = sbuf[own_lines, :]

    next_z, prev_z = lax.rem(gz + 1, groups_z), lax.rem(gz + groups_z - 1, groups_z)
    next_y, prev_y = lax.rem(gy + 1, groups_y), lax.rem(gy + groups_y - 1, groups_y)
    halos = []
    for i, (source, target, device, sends, takes) in enumerate(
        (
            (slo2.at[:, pl.ds(3 * 256, 256), :], hz_recv.at[0], (next_z, gy),
             gz < groups_z - 1, gz > 0),
            (slo2.at[:, pl.ds(0, 256), :], hz_recv.at[1], (prev_z, gy),
             gz > 0, gz < groups_z - 1),
            (hy_send.at[0], hy_recv.at[0], (gz, next_y), gy < groups_y - 1, gy > 0),
            (hy_send.at[1], hy_recv.at[1], (gz, prev_y), gy > 0, gy < groups_y - 1),
        )
    ):
        copy = pltpu.make_async_remote_copy(
            source, target, hs_sem.at[i], hr_sem.at[i], device_id=device, device_id_type=MESH
        )
        halos.append((copy, sends, takes))
        pl.when(sends)(copy.start)

        @pl.when(jnp.logical_not(takes))
        def _():
            target[...] = jnp.zeros(target.shape, F32)

    mix = mix_ref[...]
    coef = coef_ref[...]
    expand = (lax.shift_right_logical(iota((256, C), 0), 3) == iota((256, C), 1)).astype(F32)
    gather = (lax.shift_right_logical(iota((C, 256), 1), 3) == iota((C, 256), 0)).astype(F32)
    row_y = lax.bitwise_and(iota((256, 256), 0), 7)
    col_y = lax.bitwise_and(iota((256, 256), 1), 7)

    def outside(which):
        if which < 2:
            return plane(hz_recv.at[which], 0, 256)
        return plane(hy_recv.at[which - 2], 0, ZL * C)

    def gram_of(left, z):
        return dot3(left, split(plane(inp2, z * 256, 256)), NT)

    same = row_y == col_y
    coef_rows = dot3(expand, coef, NT)
    coef_col = [coef_rows[:, j : j + 1] for j in range(5)]
    full = dot3(dot3(expand, mix, NT), expand, NT)
    weight = jnp.concatenate(
        [
            full
            * (
                jnp.where(same, coef_col[0], 0.0)
                + jnp.where(row_y == col_y + 1, coef_col[1], 0.0)
                + jnp.where(row_y == col_y - 1, coef_col[2], 0.0)
            ),
            jnp.where(same, full, 0.0),
        ],
        axis=0,
    )
    weight = split(weight)
    plain = (weight[0][256:512], weight[1][256:512])
    for z in range(ZL):
        both = dot3(weight, plane(slo2, z * 256, 256), NN)
        put_plane(sten, z * 256, both[0:256])
        hid[z + 1] = both[256:512]
    own = [split(plane(slo2, z * 256, 256)) for z in range(ZL)]
    for kind, shift in enumerate((0, -1, 1)):
        total = None
        for z in range(ZL):
            if 0 <= z + shift < ZL:
                term = gram_of(own[z + shift], z)
                total = term if total is None else total + term
        gram[kind] = total

    def moments():
        gram_0 = gram[0]
        gram_up = gram[1] + gram_of(outside(0), 0)
        gram_down = gram[2] + gram_of(outside(1), ZL - 1)
        before_y, after_y = outside(2), outside(3)
        edge = None
        for z in range(ZL):
            at = slice(z * C, (z + 1) * C)
            term = gram_of(jnp.concatenate([before_y[at], after_y[at]], axis=0), z)
            edge = term if z == 0 else edge + term
        pieces = jnp.concatenate(
            [
                jnp.where(same, gram_0, 0.0),
                jnp.where(col_y == row_y + 1, gram_0, 0.0),
                jnp.where(col_y == row_y - 1, gram_0, 0.0),
                jnp.where(same, gram_up, 0.0),
                jnp.where(same, gram_down, 0.0),
            ],
            axis=1,
        )
        summed = dot3(gather, pieces, NN)
        edge_y = col_y[0:C]
        sums = [summed[:, j * 256 : (j + 1) * 256] for j in range(5)]
        sums[1] = sums[1] + jnp.where(edge_y == 0, edge[0:C], 0.0)
        sums[2] = sums[2] + jnp.where(edge_y == YL - 1, edge[C : 2 * C], 0.0)
        every = dot3(jnp.concatenate(sums, axis=0), expand, NN)
        parts = [every[j * C : (j + 1) * C] for j in range(5)]
        red_send[0] = jnp.zeros((40, LANES), F32)
        local_mix = coef[0:1, :] * parts[0]
        for j in range(1, 5):
            local_mix = local_mix + coef[j : j + 1, :] * parts[j]
        red_send[0, 0:C, 0:C] = local_mix
        for j in range(5):
            red_send[0, C + j : C + j + 1, 0:C] = jnp.sum(mix * parts[j], axis=0, keepdims=True)

    def place(phase):
        stride, size = phases[phase]
        if stride == 0:
            return size, gz
        return size, lax.rem(gy // stride, size)

    def piece(phase, i, inward):
        stride, _ = phases[phase]
        size, mine = place(phase)
        peer = lax.rem(mine + i, size)
        slot = peer if inward else mine
        device = (peer, gy) if stride == 0 else (gz, gy + (peer - mine) * stride)
        return pltpu.make_async_remote_copy(
            red_send.at[phase], red_recv.at[phase, slot], sr.at[phase, i], rr.at[phase, slot],
            device_id=device, device_id_type=MESH,
        )

    def tree_send(phase):
        size, mine = place(phase)
        for i in range(1, size):
            piece(phase, i, False).start()
        red_recv[phase, mine] = red_send[phase]

    def tree_take(phase):
        size, _ = place(phase)
        for i in range(1, size):
            piece(phase, i, True).wait_recv()
        total = red_recv[phase, 0]
        for j in range(1, size):
            total = total + red_recv[phase, j]
        if phase + 1 < len(phases):
            red_send[phase + 1] = total
        else:
            red_sum[...] = total * (1.0 / 1024.0)

    each(first_in, "wait_recv")
    received = rbuf[...].reshape(groups_y, 4, YL, LANES)
    received = jnp.concatenate(
        [received[:, part].reshape(groups_y * YL, LANES) for part in range(4)], axis=1
    )
    turned = dot3(wy_ref[...], received, NN)
    cos_part, sin_part = turned[0:32], turned[32:64]
    for field in range(2):
        re = slice(2 * field * LANES, (2 * field + 1) * LANES)
        im = slice((2 * field + 1) * LANES, (2 * field + 2) * LANES)
        zsend[:, re] = cos_part[:, re] + sin_part[:, im]
        zsend[:, im] = cos_part[:, im] - sin_part[:, re]
    for i in range(1, groups_z):
        across(zsend, zrecv, sz, rz, i, False).start()
    mine = pl.ds(pl.multiple_of(gz * 8, 8), 8)
    zrecv[mine, :] = zsend[mine, :]
    for i in range(1, groups_z):
        across(zsend, zrecv, sz, rz, i, True).wait_recv()

    cos_z = [tw_ref[2 * k : 2 * k + 1, :] for k in range(4)]
    sin_z = [tw_ref[2 * k + 1 : 2 * k + 2, :] for k in range(4)]
    for field in range(2):
        base = 2 * field * LANES
        re = [zrecv[q * 8 : q * 8 + 8, base : base + LANES] for q in range(4)]
        im = [zrecv[q * 8 : q * 8 + 8, base + LANES : base + 2 * LANES] for q in range(4)]
        re, im = dft4(re, im, -1)
        for k in range(4):
            t_re, t_im = re[k], im[k]
            if k:
                t_re, t_im = turn(t_re, t_im, cos_z[k], sin_z[k], -1)
            f_re, f_im = dft4(
                [t_re] + [pltpu.roll(t_re, LANES - 32 * s, 1) for s in range(1, 4)],
                [t_im] + [pltpu.roll(t_im, LANES - 32 * s, 1) for s in range(1, 4)],
                -1,
            )
            for m in range(4):
                at = pl.ds((k + 4 * m) * 8, 8)
                if field == 0:
                    hin[0, at, :] = f_re[m]
                    hin[1, at, :] = f_im[m]
                else:
                    hsl[0, at, :] = f_re[m] * (1.0 / cell_total)
                    hsl[1, at, :] = f_im[m] * (1.0 / cell_total)
    for part in range(2):
        hslt[part] = hsl[part].T[0:C, :]

    load(3, wts_hbm, wts).wait()

    def dual_step(step, carry):
        shift = lax.rem(NK - step * 32, NK)
        slope_re = pltpu.roll(hslt[0], shift, 1)
        slope_im = pltpu.roll(hslt[1], shift, 1)
        for j in range(32):
            k = step * 32 + j
            s_re = jnp.broadcast_to(slope_re[:, j : j + 1], (C, C))
            s_im = jnp.broadcast_to(slope_im[:, j : j + 1], (C, C))
            w_re, w_im = wts[0, k], wts[1, k]
            dual[0, pl.ds(k, 1), 0:C] = jnp.sum(w_re * s_re + w_im * s_im, axis=0, keepdims=True)
            dual[1, pl.ds(k, 1), 0:C] = jnp.sum(w_re * s_im - w_im * s_re, axis=0, keepdims=True)
        return carry

    lax.fori_loop(0, 4, dual_step, 0)

    block = lax.shift_right_logical(iota((8, LANES), 1), 5)
    v_re, v_im = [], []
    for k in range(4):
        u_re, u_im = dft4(
            [dual[0, pl.ds((k + 4 * m) * 8, 8), :] for m in range(4)],
            [dual[1, pl.ds((k + 4 * m) * 8, 8), :] for m in range(4)],
            1,
        )
        packed = []
        for u in (u_re, u_im):
            value = u[0]
            for s in range(1, 4):
                value = jnp.where(block == s, pltpu.roll(u[s], 32 * s, 1), value)
            packed.append(value)
        if k:
            packed = turn(packed[0], packed[1], cos_z[k], sin_z[k], 1)
        v_re.append(packed[0])
        v_im.append(packed[1])
    v_re, v_im = dft4(v_re, v_im, 1)
    for q in range(4):
        zsend2[q * 8 : q * 8 + 8, 0:LANES] = v_re[q]
        zsend2[q * 8 : q * 8 + 8, LANES : 2 * LANES] = v_im[q]
    for i in range(1, groups_z):
        across(zsend2, zrecv2, sz2, rz2, i, False).start()
    zrecv2[mine, :] = zsend2[mine, :]
    for copy, _, takes in halos:
        pl.when(takes)(copy.wait_recv)
    moments()
    tree_send(0)
    for i in range(1, groups_z):
        across(zsend2, zrecv2, sz2, rz2, i, True).wait_recv()

    upper = zrecv2[...]
    lower = jnp.concatenate([-upper[:, LANES:], upper[:, :LANES]], axis=1)
    back = dot3(wyt_ref[...], jnp.concatenate([upper, lower], axis=0), NN)
    sbuf2[...] = jnp.concatenate(
        [
            back[:, part * LANES : (part + 1) * LANES].reshape(groups_y, 1, YL, LANES)
            for part in range(2)
        ],
        axis=1,
    ).reshape(groups_y * 2 * YL, LANES)
    each_far(second)
    own_rows = pltpu.make_async_copy(rows(sbuf2, gy, 2 * YL), rows(lines_out, gy, 2 * YL), out_sem.at[0])
    own_rows.start()

    tree_take(0)
    tree_send(1)

    def outer_step(step, carry):
        shift = lax.rem(NK - step * 32, NK)
        slope_re = pltpu.roll(hslt[0], shift, 1)
        slope_im = pltpu.roll(hslt[1], shift, 1)
        for j in range(32):
            k = step * 32 + j
            s_re = jnp.broadcast_to(slope_re[:, j : j + 1], (C, C))
            s_im = jnp.broadcast_to(slope_im[:, j : j + 1], (C, C))
            i_re = hin[0, pl.ds(k, 1), 0:C]
            i_im = hin[1, pl.ds(k, 1), 0:C]
            spectral[0, k] = s_re * i_re + s_im * i_im
            spectral[1, k] = s_im * i_re - s_re * i_im
        return carry

    lax.fori_loop(0, 4, outer_step, 0)
    tree_take(1)
    if len(phases) > 2:
        tree_send(2)
    hid[0] = dot3(plain, outside(0), NN)
    hid[5] = dot3(plain, outside(1), NN)
    for z in range(ZL):
        total = plane(sten, z * 256, 256) + coef_col[3] * hid[z] + coef_col[4] * hid[z + 2]
        put_plane(sten, z * 256, total)
    coef_small = dot3((iota((C, C), 0) == iota((C, C), 1)).astype(F32), coef, NT)
    before_y, after_y = outside(2), outside(3)
    edges = jnp.concatenate(
        [side[z * C : (z + 1) * C] for side in (before_y, after_y) for z in range(ZL)], axis=1
    )
    edge_hidden = dot3(mix, edges, TN)
    for z in range(ZL):
        for side, y in enumerate((0, YL - 1)):
            at = pl.ds(z * 256 + y, C, stride=YL)
            for half in range(2):
                column = (side * ZL + z) * NX + half * LANES
                sten[half, at, :] = (
                    sten[half, at, :]
                    + coef_small[:, 1 + side : 2 + side]
                    * edge_hidden[:, column : column + LANES]
                )
    if len(phases) > 2:
        tree_take(2)

    each(second_in, "wait_recv")
    own_rows.wait()
    each(first, "wait_send")
    each(second, "wait_send")
    for copy, sends, _ in halos:
        pl.when(sends)(copy.wait_send)
    for i in range(1, groups_z):
        across(zsend, zrecv, sz, rz, i, False).wait_send()
        across(zsend2, zrecv2, sz2, rz2, i, False).wait_send()
    for phase in range(len(phases)):
        for i in range(1, place(phase)[0]):
            piece(phase, i, False).wait_send()


def result_kernel(
    lines, sten, spectral, red, wx_ref,
    grad_input, grad_spectral, grad_mix, grad_coef,
    cells, out_sem,
):
    modes_x = wx_ref.shape[0] // 2
    out = pltpu.make_async_copy(spectral, grad_spectral, out_sem.at[0])
    out.start()
    grad_mix[...] = red[0:C, 0:C]
    grad_coef[...] = red[C : C + 5, 0:C]
    spread = jnp.concatenate(
        [
            jnp.concatenate(
                [lines[pl.ds(part * YL + y, modes_x, stride=2 * YL), :] for y in range(YL)], axis=1
            )
            for part in range(2)
        ],
        axis=0,
    )
    result = dot3(spread, wx_ref[...], TN)
    for y in range(YL):
        for half in range(2):
            cells[half, pl.ds(y, LANES, stride=YL), :] = result[
                y * LANES : (y + 1) * LANES, half * LANES : (half + 1) * LANES
            ]
    for z in range(ZL):
        total = plane(cells, z * 256, 256) + plane(sten, z * 256, 256)
        grad_input[:, z] = total.reshape(C, YL, NX)
    out.wait()


def per_device(input_field, pre_activation, cotangent, spectral_weights, mix_weights, coefficients):
    groups_y = lax.axis_size("gy")
    groups_z = lax.axis_size("gz")
    grid_y = YL * groups_y
    modes_x = groups_y
    cell_total = NX * grid_y * ZL * groups_z
    phases = ((0, groups_z), (1, 8), (8, 4)) if groups_y == 32 else ((0, groups_z), (1, 4))
    rows_y = groups_y * YL
    cos_x, sin_x = table(NX, modes_x)
    cos_y, sin_y = table(grid_y, 32)
    wx = np.concatenate([cos_x, -sin_x]).astype(np.float32)
    wy = np.concatenate([cos_y, sin_y]).astype(np.float32)
    cell = np.arange(LANES) // C
    tw = np.stack(
        [fn(2.0 * math.pi * k * cell / 16.0) for k in range(4) for fn in (np.cos, np.sin)]
    ).astype(np.float32)
    weights = spectral_weights.reshape(2, NK, C, C)
    vmem = pl.BlockSpec(memory_space=pltpu.VMEM)
    hbm = pl.BlockSpec(memory_space=pltpu.HBM)
    sds = jax.ShapeDtypeStruct
    dma = pltpu.SemaphoreType.DMA
    lines, sten, spectral, red = pl.pallas_call(
        functools.partial(exchange_kernel, groups_y, groups_z, phases, cell_total),
        name="exchange",
        out_shape=(
            pltpu.VMEM((2 * rows_y, LANES), F32),
            pltpu.VMEM((2, ZL * 256, LANES), F32),
            pltpu.VMEM((2, NK, C, C), F32),
            pltpu.VMEM((40, LANES), F32),
        ),
        in_specs=[hbm] * 4 + [vmem] * 6,
        out_specs=(vmem,) * 4,
        scratch_shapes=[
            pltpu.VMEM((C, ZL, YL, NX), F32),
            pltpu.VMEM((C, ZL, YL, NX), F32),
            pltpu.VMEM((C, ZL, YL, NX), F32),
            pltpu.VMEM((2, NK, C, C), F32),
            pltpu.VMEM((2, ZL * 256, LANES), F32),
            pltpu.VMEM((2, ZL * 256, LANES), F32),
            pltpu.VMEM((4 * rows_y, LANES), F32),
            pltpu.VMEM((4 * rows_y, LANES), F32),
            pltpu.VMEM((32, 4 * LANES), F32),
            pltpu.VMEM((32, 4 * LANES), F32),
            pltpu.VMEM((32, 2 * LANES), F32),
            pltpu.VMEM((32, 2 * LANES), F32),
            pltpu.VMEM((2 * rows_y, LANES), F32),
            pltpu.VMEM((2, 2, ZL * C, LANES), F32),
            pltpu.VMEM((2, 2, ZL * C, LANES), F32),
            pltpu.VMEM((2, 2, 256, LANES), F32),
            pltpu.VMEM((6, 256, NX), F32),
            pltpu.VMEM((3, 256, 256), F32),
            pltpu.VMEM((2, NK, LANES), F32),
            pltpu.VMEM((2, NK, LANES), F32),
            pltpu.VMEM((2, C, NK), F32),
            pltpu.VMEM((2, NK, LANES), F32),
            pltpu.VMEM((len(phases), 40, LANES), F32),
            pltpu.VMEM((len(phases), 8, 40, LANES), F32),
            dma((4,)),
            dma((groups_y,)), dma((groups_y,)), dma((groups_y,)), dma((groups_y,)),
            dma((groups_z,)), dma((groups_z,)), dma((groups_z,)), dma((groups_z,)),
            dma((4,)), dma((4,)),
            dma((len(phases), 8)), dma((len(phases), 8)),
            dma((1,)),
        ],
        compiler_params=pltpu.CompilerParams(
            collective_id=0, has_side_effects=True, vmem_limit_bytes=40 << 20
        ),
    )(
        *(
            pltpu.with_memory_space_constraint(operand, pltpu.HBM)
            for operand in (
                input_field, pre_activation, cotangent, weights, mix_weights, coefficients,
                jnp.asarray(wx), jnp.asarray(wy), jnp.asarray(wy.T.copy()), jnp.asarray(tw),
            )
        )
    )
    grad_input, grad_spectral, grad_mix, grad_coef = pl.pallas_call(
        result_kernel,
        name="result",
        out_shape=(
            sds((C, ZL, YL, NX), F32),
            sds((2, NK, C, C), F32),
            sds((C, C), F32),
            sds((5, C), F32),
        ),
        in_specs=[vmem] * 5,
        out_specs=(vmem, hbm, vmem, vmem),
        scratch_shapes=[
            pltpu.VMEM((2, ZL * 256, LANES), F32),
            dma((1,)),
        ],
        compiler_params=pltpu.CompilerParams(vmem_limit_bytes=24 << 20),
    )(lines, sten, spectral, red, jnp.asarray(wx))
    return (grad_input, grad_spectral.reshape(spectral_weights.shape), grad_mix, grad_coef)


def solution(mesh):
    in_specs = (
        P(None, "gz", "gy", None),
        P(None, "gz", "gy", None),
        P(None, "gz", "gy", None),
        P(None, None, "gz", "gy", None, None),
        P(),
        P(),
    )
    out_specs = (P(None, "gz", "gy", None), P(None, None, "gz", "gy", None, None), P(), P())
    return jax.shard_map(
        per_device, mesh=mesh, in_specs=in_specs, out_specs=out_specs, check_vma=False
    )
```

```python
import functools
import math

import jax
import jax.numpy as jnp
import numpy as np
from jax import lax
from jax.experimental import pallas as pl
from jax.experimental.pallas import tpu as pltpu
from jax.sharding import PartitionSpec as P

F32 = jnp.float32
BF16 = jnp.bfloat16
MESH = pl.DeviceIdType.MESH
C = 32
ZL = 4
YL = 8
NX = 256
LANES = 128
NK = 128


def mode_numbers(number):
    positions = np.arange(number)
    return np.where(positions < number // 2, positions, positions - number)


def table(cells, modes):
    product = np.remainder(np.outer(mode_numbers(modes), np.arange(cells)), cells)
    angles = product * (2.0 * math.pi / cells)
    return np.cos(angles), np.sin(angles)


def split(a):
    high = a.astype(BF16)
    return high, (a - high.astype(F32)).astype(BF16)


def dot1(a, b, dims):
    return lax.dot_general(a, b, (dims, ((), ())), preferred_element_type=F32)


def dot3(a, b, dims):
    a_high, a_low = a if isinstance(a, tuple) else split(a)
    b_high, b_low = b if isinstance(b, tuple) else split(b)
    return dot1(a_high, b_low, dims) + dot1(a_low, b_high, dims) + dot1(a_high, b_high, dims)


NN = ((1,), (0,))
NT = ((1,), (1,))
TN = ((0,), (0,))


def gelu_slope(values):
    normal_cdf = 0.5 * (1.0 + lax.erf(values * 0.7071067811865476))
    return normal_cdf + values * jnp.exp(-0.5 * values * values) * 0.3989422804014327


def dft4(re, im, sign):
    ar, ai = re[0] + re[2], im[0] + im[2]
    br, bi = re[0] - re[2], im[0] - im[2]
    cr, ci = re[1] + re[3], im[1] + im[3]
    dr, di = re[1] - re[3], im[1] - im[3]
    if sign < 0:
        return [ar + cr, br + di, ar - cr, br - di], [ai + ci, bi - dr, ai - ci, bi + dr]
    return [ar + cr, br - di, ar - cr, br + di], [ai + ci, bi + dr, ai - ci, bi - dr]


def turn(re, im, cos, sin, sign):
    if sign < 0:
        return re * cos + im * sin, im * cos - re * sin
    return re * cos - im * sin, im * cos + re * sin


def plane(ref, start, size):
    return jnp.concatenate([ref[half, pl.ds(start, size), :] for half in range(2)], axis=1)


def put_plane(ref, start, value):
    for half in range(2):
        ref[half, pl.ds(start, value.shape[0]), :] = value[:, half * LANES : (half + 1) * LANES]


def offsets(groups_y):
    sizes = (4, 2, 4) if groups_y == 32 else (4,)
    result = []
    for i in range(1, groups_y):
        moves, rest = [], i
        for size in sizes:
            moves.append((size, rest % size))
            rest //= size
        hops = sum(min(m, n - m) * (2 if n == 2 else 1) for n, m in moves)
        result.append((-hops, tuple(moves)))
    return [moves for _, moves in sorted(result)]


def iota(shape, axis):
    return lax.broadcasted_iota(jnp.int32, shape, axis)


def exchange_kernel(
    groups_y, groups_z, phases, cell_total,
    inp_hbm, pre_hbm, cot_hbm, wts_hbm, mix_hbm, coef_hbm, wx_hbm, wy_hbm, wyt_hbm, tw_hbm,
    lines_out, sten, spectral, red_sum,
    mix_ref, coef_ref, wx_ref, wy_ref, wyt_ref, tw_ref, inp4, pre4, cot4, wts, inp2, slo2, sbuf, rbuf, zsend, zrecv, zsend2, zrecv2, sbuf2,
    hy_send, hy_recv, hz_recv, hid, gram, hin, hsl, hslt, dual, red_send, red_recv,
    load_sem, s1, r1, s2, r2, sz, rz, sz2, rz2, hs_sem, hr_sem, sr, rr, out_sem,
):
    gz = lax.axis_index("gz")
    gy = lax.axis_index("gy")
    modes_x = wx_ref.shape[0] // 2

    def load(i, src, dst):
        return pltpu.make_async_copy(src, dst, load_sem.at[i])

    barrier = pltpu.get_barrier_semaphore()

    def partner(i):
        if isinstance(i, tuple):
            digits, stride, peer = gy, 1, 0
            for size, move in i:
                peer = peer + lax.rem(lax.rem(digits, size) + move, size) * stride
                digits, stride = digits // size, stride * size
            return peer
        return lax.rem(gy + i, groups_y)

    for i in offsets(groups_y):
        pl.semaphore_signal(barrier, inc=1, device_id=(gz, partner(i)), device_id_type=MESH)
    for i in range(1, groups_z):
        peer = lax.rem(gz + i, groups_z)
        pl.semaphore_signal(barrier, inc=1, device_id=(peer, gy), device_id_type=MESH)
    loads = [
        load(0, inp_hbm, inp4),
        load(6, wx_hbm, wx_ref),
        load(1, pre_hbm, pre4),
        load(2, cot_hbm, cot4),
    ]
    small = [
        load(4, mix_hbm, mix_ref),
        load(5, coef_hbm, coef_ref),
        load(7, wy_hbm, wy_ref),
        load(8, wyt_hbm, wyt_ref),
        load(9, tw_hbm, tw_ref),
    ]
    for copy in loads + small:
        copy.start()
    loads[1].wait()

    wx = split(wx_ref[...])

    def along_x(source, field):
        cells = jnp.concatenate(
            [
                jnp.concatenate(
                    [source[half, pl.ds(y, LANES, stride=YL), :] for half in range(2)], axis=1
                )
                for y in range(YL)
            ],
            axis=0,
        )
        result = dot3(wx, cells, NT)
        for y in range(YL):
            for part in range(2):
                sbuf[pl.ds((2 * field + part) * YL + y, modes_x, stride=4 * YL), :] = (
                    result[part * modes_x : (part + 1) * modes_x, y * LANES : (y + 1) * LANES]
                )

    loads[0].wait()
    for z in range(ZL):
        put_plane(inp2, z * 256, inp4[:, z].reshape(256, NX))
    along_x(inp2, 0)
    loads[2].wait()
    loads[3].wait()
    load(3, wts_hbm, wts).start()

    def slope_step(step, carry):
        z = step // 4
        c = lax.rem(step, 4) * 8
        pre = pre4[pl.ds(c, 8), z].reshape(64, NX)
        cot = cot4[pl.ds(c, 8), z].reshape(64, NX)
        put_plane(slo2, pl.multiple_of(step * 64, 64), cot * gelu_slope(pre))
        return carry

    lax.fori_loop(0, 16, slope_step, 0)
    along_x(slo2, 1)
    for z in range(ZL):
        for side, y in enumerate((YL - 1, 0)):
            for half in range(2):
                hy_send[side, half, pl.ds(z * C, C), :] = slo2[
                    half, pl.ds(z * 256 + y, C, stride=YL), :
                ]

    pl.semaphore_wait(barrier, groups_y - 1 + groups_z - 1)

    def rows(ref, index, size=YL):
        return ref.at[pl.ds(pl.multiple_of(index * size, size), size), :]

    def first(i):
        peer = partner(i)
        return pltpu.make_async_remote_copy(
            rows(sbuf, peer, 4 * YL), rows(rbuf, gy, 4 * YL), s1.at[peer], r1.at[gy],
            device_id=(gz, peer), device_id_type=MESH,
        )

    def first_in(i):
        peer = lax.rem(gy + i, groups_y)
        return pltpu.make_async_remote_copy(
            rows(sbuf, peer, 4 * YL), rows(rbuf, peer, 4 * YL), s1.at[peer], r1.at[peer],
            device_id=(gz, peer), device_id_type=MESH,
        )

    def second(i):
        peer = partner(i)
        return pltpu.make_async_remote_copy(
            rows(sbuf2, peer, 2 * YL), rows(lines_out, gy, 2 * YL), s2.at[peer], r2.at[gy],
            device_id=(gz, peer), device_id_type=MESH,
        )

    def second_in(i):
        peer = lax.rem(gy + i, groups_y)
        return pltpu.make_async_remote_copy(
            rows(sbuf2, peer, 2 * YL), rows(lines_out, peer, 2 * YL), s2.at[peer], r2.at[peer],
            device_id=(gz, peer), device_id_type=MESH,
        )

    def across(source, target, send, recv, i, inward):
        peer = lax.rem(gz + i, groups_z)
        slot = peer if inward else gz
        return pltpu.make_async_remote_copy(
            rows(source, peer), rows(target, slot), send.at[peer], recv.at[slot],
            device_id=(peer, gy), device_id_type=MESH,
        )

    def each_far(make):
        for i in offsets(groups_y):
            make(i).start()

    def each(make, action):
        def body(i, carry):
            getattr(make(i), action)()
            return carry

        lax.fori_loop(1, groups_y, body, 0)

    each_far(first)
    own_lines = pl.ds(pl.multiple_of(gy * 4 * YL, 4 * YL), 4 * YL)
    rbuf[own_lines, :] = sbuf[own_lines, :]

    next_z, prev_z = lax.rem(gz + 1, groups_z), lax.rem(gz + groups_z - 1, groups_z)
    next_y, prev_y = lax.rem(gy + 1, groups_y), lax.rem(gy + groups_y - 1, groups_y)
    halos = []
    for i, (source, target, device, sends, takes) in enumerate(
        (
            (slo2.at[:, pl.ds(3 * 256, 256), :], hz_recv.at[0], (next_z, gy),
             gz < groups_z - 1, gz > 0),
            (slo2.at[:, pl.ds(0, 256), :], hz_recv.at[1], (prev_z, gy),
             gz > 0, gz < groups_z - 1),
            (hy_send.at[0], hy_recv.at[0], (gz, next_y), gy < groups_y - 1, gy > 0),
            (hy_send.at[1], hy_recv.at[1], (gz, prev_y), gy > 0, gy < groups_y - 1),
        )
    ):
        copy = pltpu.make_async_remote_copy(
            source, target, hs_sem.at[i], hr_sem.at[i], device_id=device, device_id_type=MESH
        )
        halos.append((copy, sends, takes))
        pl.when(sends)(copy.start)

        @pl.when(jnp.logical_not(takes))
        def _():
            target[...] = jnp.zeros(target.shape, F32)

    for copy in small:
        copy.wait()
    mix = mix_ref[...]
    coef = coef_ref[...]
    expand = (lax.shift_right_logical(iota((256, C), 0), 3) == iota((256, C), 1)).astype(F32)
    gather = (lax.shift_right_logical(iota((C, 256), 1), 3) == iota((C, 256), 0)).astype(F32)
    row_y = lax.bitwise_and(iota((256, 256), 0), 7)
    col_y = lax.bitwise_and(iota((256, 256), 1), 7)

    def outside(which):
        if which < 2:
            return plane(hz_recv.at[which], 0, 256)
        return plane(hy_recv.at[which - 2], 0, ZL * C)

    def gram_of(left, z):
        return dot3(left, split(plane(inp2, z * 256, 256)), NT)

    same = row_y == col_y
    coef_rows = dot3(expand, coef, NT)
    coef_col = [coef_rows[:, j : j + 1] for j in range(5)]
    full = dot3(dot3(expand, mix, NT), expand, NT)
    weight = jnp.concatenate(
        [
            full
            * (
                jnp.where(same, coef_col[0], 0.0)
                + jnp.where(row_y == col_y + 1, coef_col[1], 0.0)
                + jnp.where(row_y == col_y - 1, coef_col[2], 0.0)
            ),
            jnp.where(same, full, 0.0),
        ],
        axis=0,
    )
    weight = split(weight)
    plain = (weight[0][256:512], weight[1][256:512])
    for z in range(ZL):
        both = dot3(weight, plane(slo2, z * 256, 256), NN)
        put_plane(sten, z * 256, both[0:256])
        hid[z + 1] = both[256:512]
    own = [split(plane(slo2, z * 256, 256)) for z in range(ZL)]
    for kind, shift in enumerate((0, -1, 1)):
        total = None
        for z in range(ZL):
            if 0 <= z + shift < ZL:
                term = gram_of(own[z + shift], z)
                total = term if total is None else total + term
        gram[kind] = total

    def moments():
        gram_0 = gram[0]
        gram_up = gram[1] + gram_of(outside(0), 0)
        gram_down = gram[2] + gram_of(outside(1), ZL - 1)
        before_y, after_y = outside(2), outside(3)
        edge = None
        for z in range(ZL):
            at = slice(z * C, (z + 1) * C)
            term = gram_of(jnp.concatenate([before_y[at], after_y[at]], axis=0), z)
            edge = term if z == 0 else edge + term
        pieces = jnp.concatenate(
            [
                jnp.where(same, gram_0, 0.0),
                jnp.where(col_y == row_y + 1, gram_0, 0.0),
                jnp.where(col_y == row_y - 1, gram_0, 0.0),
                jnp.where(same, gram_up, 0.0),
                jnp.where(same, gram_down, 0.0),
            ],
            axis=1,
        )
        summed = dot3(gather, pieces, NN)
        edge_y = col_y[0:C]
        sums = [summed[:, j * 256 : (j + 1) * 256] for j in range(5)]
        sums[1] = sums[1] + jnp.where(edge_y == 0, edge[0:C], 0.0)
        sums[2] = sums[2] + jnp.where(edge_y == YL - 1, edge[C : 2 * C], 0.0)
        every = dot3(jnp.concatenate(sums, axis=0), expand, NN)
        parts = [every[j * C : (j + 1) * C] for j in range(5)]
        local_mix = coef[0:1, :] * parts[0]
        for j in range(1, 5):
            local_mix = local_mix + coef[j : j + 1, :] * parts[j]
        red_send[0, 0:16, 0:C] = local_mix[0:16]
        red_send[0, 0:16, C : 2 * C] = local_mix[16:32]
        red_send[0, 0:16, 2 * C :] = jnp.zeros((16, 2 * C), F32)
        for j in range(5):
            red_send[0, j : j + 1, 2 * C : 3 * C] = jnp.sum(
                mix * parts[j], axis=0, keepdims=True
            )

    def place(phase):
        stride, size = phases[phase]
        if stride == 0:
            return size, gz
        return size, lax.rem(gy // stride, size)

    def piece(phase, i, inward):
        stride, _ = phases[phase]
        size, mine = place(phase)
        peer = lax.rem(mine + i, size)
        slot = peer if inward else mine
        device = (peer, gy) if stride == 0 else (gz, gy + (peer - mine) * stride)
        return pltpu.make_async_remote_copy(
            red_send.at[phase], red_recv.at[phase, slot], sr.at[phase, i], rr.at[phase, slot],
            device_id=device, device_id_type=MESH,
        )

    def tree_send(phase):
        size, mine = place(phase)
        for i in range(1, size):
            piece(phase, i, False).start()
        red_recv[phase, mine] = red_send[phase]

    def tree_take(phase):
        size, _ = place(phase)
        for i in range(1, size):
            piece(phase, i, True).wait_recv()
        total = red_recv[phase, 0]
        for j in range(1, size):
            total = total + red_recv[phase, j]
        if phase + 1 < len(phases):
            red_send[phase + 1] = total
        else:
            red_sum[...] = total * (1.0 / 1024.0)

    each(first_in, "wait_recv")
    received = rbuf[...].reshape(groups_y, 4, YL, LANES)
    received = jnp.concatenate(
        [received[:, part].reshape(groups_y * YL, LANES) for part in range(4)], axis=1
    )
    turned = dot3(wy_ref[...], received, NN)
    cos_part, sin_part = turned[0:32], turned[32:64]
    for field in range(2):
        re = slice(2 * field * LANES, (2 * field + 1) * LANES)
        im = slice((2 * field + 1) * LANES, (2 * field + 2) * LANES)
        zsend[:, re] = cos_part[:, re] + sin_part[:, im]
        zsend[:, im] = cos_part[:, im] - sin_part[:, re]
    for i in range(1, groups_z):
        across(zsend, zrecv, sz, rz, i, False).start()
    mine = pl.ds(pl.multiple_of(gz * 8, 8), 8)
    zrecv[mine, :] = zsend[mine, :]
    for i in range(1, groups_z):
        across(zsend, zrecv, sz, rz, i, True).wait_recv()

    cos_z = [tw_ref[2 * k : 2 * k + 1, :] for k in range(4)]
    sin_z = [tw_ref[2 * k + 1 : 2 * k + 2, :] for k in range(4)]
    for field in range(2):
        base = 2 * field * LANES
        re = [zrecv[q * 8 : q * 8 + 8, base : base + LANES] for q in range(4)]
        im = [zrecv[q * 8 : q * 8 + 8, base + LANES : base + 2 * LANES] for q in range(4)]
        re, im = dft4(re, im, -1)
        for k in range(4):
            t_re, t_im = re[k], im[k]
            if k:
                t_re, t_im = turn(t_re, t_im, cos_z[k], sin_z[k], -1)
            f_re, f_im = dft4(
                [t_re] + [pltpu.roll(t_re, LANES - 32 * s, 1) for s in range(1, 4)],
                [t_im] + [pltpu.roll(t_im, LANES - 32 * s, 1) for s in range(1, 4)],
                -1,
            )
            for m in range(4):
                at = pl.ds((k + 4 * m) * 8, 8)
                if field == 0:
                    hin[0, at, :] = f_re[m]
                    hin[1, at, :] = f_im[m]
                else:
                    hsl[0, at, :] = f_re[m] * (1.0 / cell_total)
                    hsl[1, at, :] = f_im[m] * (1.0 / cell_total)
    for part in range(2):
        hslt[part] = hsl[part].T[0:C, :]

    load(3, wts_hbm, wts).wait()

    def dual_step(step, carry):
        shift = lax.rem(NK - step * 32, NK)
        slope_re = pltpu.roll(hslt[0], shift, 1)
        slope_im = pltpu.roll(hslt[1], shift, 1)
        for j in range(32):
            k = step * 32 + j
            s_re = jnp.broadcast_to(slope_re[:, j : j + 1], (C, C))
            s_im = jnp.broadcast_to(slope_im[:, j : j + 1], (C, C))
            w_re, w_im = wts[0, k], wts[1, k]
            dual[0, pl.ds(k, 1), 0:C] = jnp.sum(w_re * s_re + w_im * s_im, axis=0, keepdims=True)
            dual[1, pl.ds(k, 1), 0:C] = jnp.sum(w_re * s_im - w_im * s_re, axis=0, keepdims=True)
        return carry

    lax.fori_loop(0, 4, dual_step, 0)

    block = lax.shift_right_logical(iota((8, LANES), 1), 5)
    v_re, v_im = [], []
    for k in range(4):
        u_re, u_im = dft4(
            [dual[0, pl.ds((k + 4 * m) * 8, 8), :] for m in range(4)],
            [dual[1, pl.ds((k + 4 * m) * 8, 8), :] for m in range(4)],
            1,
        )
        packed = []
        for u in (u_re, u_im):
            value = u[0]
            for s in range(1, 4):
                value = jnp.where(block == s, pltpu.roll(u[s], 32 * s, 1), value)
            packed.append(value)
        if k:
            packed = turn(packed[0], packed[1], cos_z[k], sin_z[k], 1)
        v_re.append(packed[0])
        v_im.append(packed[1])
    v_re, v_im = dft4(v_re, v_im, 1)
    for q in range(4):
        zsend2[q * 8 : q * 8 + 8, 0:LANES] = v_re[q]
        zsend2[q * 8 : q * 8 + 8, LANES : 2 * LANES] = v_im[q]
    for i in range(1, groups_z):
        across(zsend2, zrecv2, sz2, rz2, i, False).start()
    zrecv2[mine, :] = zsend2[mine, :]
    for copy, _, takes in halos:
        pl.when(takes)(copy.wait_recv)
    moments()
    tree_send(0)
    for i in range(1, groups_z):
        across(zsend2, zrecv2, sz2, rz2, i, True).wait_recv()

    upper = zrecv2[...]
    lower = jnp.concatenate([-upper[:, LANES:], upper[:, :LANES]], axis=1)
    back = dot3(wyt_ref[...], jnp.concatenate([upper, lower], axis=0), NN)
    sbuf2[...] = jnp.concatenate(
        [
            back[:, part * LANES : (part + 1) * LANES].reshape(groups_y, 1, YL, LANES)
            for part in range(2)
        ],
        axis=1,
    ).reshape(groups_y * 2 * YL, LANES)
    tree_take(0)
    tree_send(1)
    each_far(second)
    own_rows = pltpu.make_async_copy(rows(sbuf2, gy, 2 * YL), rows(lines_out, gy, 2 * YL), out_sem.at[0])
    own_rows.start()

    def outer_step(step, carry):
        shift = lax.rem(NK - step * 32, NK)
        slope_re = pltpu.roll(hslt[0], shift, 1)
        slope_im = pltpu.roll(hslt[1], shift, 1)
        for j in range(32):
            k = step * 32 + j
            s_re = jnp.broadcast_to(slope_re[:, j : j + 1], (C, C))
            s_im = jnp.broadcast_to(slope_im[:, j : j + 1], (C, C))
            i_re = hin[0, pl.ds(k, 1), 0:C]
            i_im = hin[1, pl.ds(k, 1), 0:C]
            spectral[0, k] = s_re * i_re + s_im * i_im
            spectral[1, k] = s_im * i_re - s_re * i_im
        return carry

    lax.fori_loop(0, 4, outer_step, 0)
    tree_take(1)
    if len(phases) > 2:
        tree_send(2)
    hid[0] = dot3(plain, outside(0), NN)
    hid[5] = dot3(plain, outside(1), NN)
    for z in range(ZL):
        total = plane(sten, z * 256, 256) + coef_col[3] * hid[z] + coef_col[4] * hid[z + 2]
        put_plane(sten, z * 256, total)
    coef_small = dot3((iota((C, C), 0) == iota((C, C), 1)).astype(F32), coef, NT)
    before_y, after_y = outside(2), outside(3)
    edges = jnp.concatenate(
        [side[z * C : (z + 1) * C] for side in (before_y, after_y) for z in range(ZL)], axis=1
    )
    edge_hidden = dot3(mix, edges, TN)
    for z in range(ZL):
        for side, y in enumerate((0, YL - 1)):
            at = pl.ds(z * 256 + y, C, stride=YL)
            for half in range(2):
                column = (side * ZL + z) * NX + half * LANES
                sten[half, at, :] = (
                    sten[half, at, :]
                    + coef_small[:, 1 + side : 2 + side]
                    * edge_hidden[:, column : column + LANES]
                )
    if len(phases) > 2:
        tree_take(2)

    each(second_in, "wait_recv")
    own_rows.wait()
    each(first, "wait_send")
    each(second, "wait_send")
    for copy, sends, _ in halos:
        pl.when(sends)(copy.wait_send)
    for i in range(1, groups_z):
        across(zsend, zrecv, sz, rz, i, False).wait_send()
        across(zsend2, zrecv2, sz2, rz2, i, False).wait_send()
    for phase in range(len(phases)):
        for i in range(1, place(phase)[0]):
            piece(phase, i, False).wait_send()


def result_kernel(
    lines, sten, spectral, red, wx_ref,
    grad_input, grad_spectral, grad_mix, grad_coef,
    cells, field, mix_out, coef_out, out_sem,
):
    modes_x = wx_ref.shape[0] // 2
    out = pltpu.make_async_copy(spectral, grad_spectral, out_sem.at[0])
    out.start()
    mix_out[0:16, :] = red[:, 0:C]
    mix_out[16:32, :] = red[:, C : 2 * C]
    coef_out[...] = red[0:5, 2 * C : 3 * C]
    small = [
        pltpu.make_async_copy(mix_out, grad_mix, out_sem.at[1]),
        pltpu.make_async_copy(coef_out, grad_coef, out_sem.at[2]),
    ]
    for copy in small:
        copy.start()
    spread = jnp.concatenate(
        [
            jnp.concatenate(
                [lines[pl.ds(part * YL + y, modes_x, stride=2 * YL), :] for y in range(YL)], axis=1
            )
            for part in range(2)
        ],
        axis=0,
    )
    result = dot3(spread, wx_ref[...], TN)
    for y in range(YL):
        for half in range(2):
            cells[half, pl.ds(y, LANES, stride=YL), :] = result[
                y * LANES : (y + 1) * LANES, half * LANES : (half + 1) * LANES
            ]
    planes = []
    for z in range(ZL):
        total = plane(cells, z * 256, 256) + plane(sten, z * 256, 256)
        field[z] = total.reshape(C, YL, NX)
        planes.append(pltpu.make_async_copy(field.at[z], grad_input.at[:, z], out_sem.at[3 + z]))
        planes[-1].start()
    for copy in planes + small + [out]:
        copy.wait()


def per_device(input_field, pre_activation, cotangent, spectral_weights, mix_weights, coefficients):
    groups_y = lax.axis_size("gy")
    groups_z = lax.axis_size("gz")
    grid_y = YL * groups_y
    modes_x = groups_y
    cell_total = NX * grid_y * ZL * groups_z
    phases = ((0, groups_z), (1, 8), (8, 4)) if groups_y == 32 else ((0, groups_z), (1, 4))
    rows_y = groups_y * YL
    cos_x, sin_x = table(NX, modes_x)
    cos_y, sin_y = table(grid_y, 32)
    wx = np.concatenate([cos_x, -sin_x]).astype(np.float32)
    wy = np.concatenate([cos_y, sin_y]).astype(np.float32)
    cell = np.arange(LANES) // C
    tw = np.stack(
        [fn(2.0 * math.pi * k * cell / 16.0) for k in range(4) for fn in (np.cos, np.sin)]
    ).astype(np.float32)
    weights = spectral_weights.reshape(2, NK, C, C)
    vmem = pl.BlockSpec(memory_space=pltpu.VMEM)
    hbm = pl.BlockSpec(memory_space=pltpu.HBM)
    sds = jax.ShapeDtypeStruct
    dma = pltpu.SemaphoreType.DMA
    lines, sten, spectral, red = pl.pallas_call(
        functools.partial(exchange_kernel, groups_y, groups_z, phases, cell_total),
        name="exchange",
        out_shape=(
            pltpu.VMEM((2 * rows_y, LANES), F32),
            pltpu.VMEM((2, ZL * 256, LANES), F32),
            pltpu.VMEM((2, NK, C, C), F32),
            pltpu.VMEM((16, LANES), F32),
        ),
        in_specs=[hbm] * 10,
        out_specs=(vmem,) * 4,
        scratch_shapes=[
            pltpu.VMEM((C, C), F32),
            pltpu.VMEM((5, C), F32),
            pltpu.VMEM(wx.shape, F32),
            pltpu.VMEM(wy.shape, F32),
            pltpu.VMEM(wy.T.shape, F32),
            pltpu.VMEM(tw.shape, F32),
            pltpu.VMEM((C, ZL, YL, NX), F32),
            pltpu.VMEM((C, ZL, YL, NX), F32),
            pltpu.VMEM((C, ZL, YL, NX), F32),
            pltpu.VMEM((2, NK, C, C), F32),
            pltpu.VMEM((2, ZL * 256, LANES), F32),
            pltpu.VMEM((2, ZL * 256, LANES), F32),
            pltpu.VMEM((4 * rows_y, LANES), F32),
            pltpu.VMEM((4 * rows_y, LANES), F32),
            pltpu.VMEM((32, 4 * LANES), F32),
            pltpu.VMEM((32, 4 * LANES), F32),
            pltpu.VMEM((32, 2 * LANES), F32),
            pltpu.VMEM((32, 2 * LANES), F32),
            pltpu.VMEM((2 * rows_y, LANES), F32),
            pltpu.VMEM((2, 2, ZL * C, LANES), F32),
            pltpu.VMEM((2, 2, ZL * C, LANES), F32),
            pltpu.VMEM((2, 2, 256, LANES), F32),
            pltpu.VMEM((6, 256, NX), F32),
            pltpu.VMEM((3, 256, 256), F32),
            pltpu.VMEM((2, NK, LANES), F32),
            pltpu.VMEM((2, NK, LANES), F32),
            pltpu.VMEM((2, C, NK), F32),
            pltpu.VMEM((2, NK, LANES), F32),
            pltpu.VMEM((len(phases), 16, LANES), F32),
            pltpu.VMEM((len(phases), 8, 16, LANES), F32),
            dma((10,)),
            dma((groups_y,)), dma((groups_y,)), dma((groups_y,)), dma((groups_y,)),
            dma((groups_z,)), dma((groups_z,)), dma((groups_z,)), dma((groups_z,)),
            dma((4,)), dma((4,)),
            dma((len(phases), 8)), dma((len(phases), 8)),
            dma((1,)),
        ],
        compiler_params=pltpu.CompilerParams(
            collective_id=0, has_side_effects=True, vmem_limit_bytes=40 << 20
        ),
    )(
        *(
            pltpu.with_memory_space_constraint(operand, pltpu.HBM)
            for operand in (
                input_field, pre_activation, cotangent, weights, mix_weights, coefficients,
                jnp.asarray(wx), jnp.asarray(wy), jnp.asarray(wy.T.copy()), jnp.asarray(tw),
            )
        )
    )
    grad_input, grad_spectral, grad_mix, grad_coef = pl.pallas_call(
        result_kernel,
        name="result",
        out_shape=(
            sds((C, ZL, YL, NX), F32),
            sds((2, NK, C, C), F32),
            sds((C, C), F32),
            sds((5, C), F32),
        ),
        in_specs=[vmem] * 5,
        out_specs=(hbm,) * 4,
        scratch_shapes=[
            pltpu.VMEM((2, ZL * 256, LANES), F32),
            pltpu.VMEM((ZL, C, YL, NX), F32),
            pltpu.VMEM((C, C), F32),
            pltpu.VMEM((5, C), F32),
            dma((3 + ZL,)),
        ],
        compiler_params=pltpu.CompilerParams(vmem_limit_bytes=24 << 20),
    )(lines, sten, spectral, red, jnp.asarray(wx))
    return (grad_input, grad_spectral.reshape(spectral_weights.shape), grad_mix, grad_coef)


def solution(mesh):
    in_specs = (
        P(None, "gz", "gy", None),
        P(None, "gz", "gy", None),
        P(None, "gz", "gy", None),
        P(None, None, "gz", "gy", None, None),
        P(),
        P(),
    )
    out_specs = (P(None, "gz", "gy", None), P(None, None, "gz", "gy", None, None), P(), P())
    return jax.shard_map(
        per_device, mesh=mesh, in_specs=in_specs, out_specs=out_specs, check_vma=False
    )
```

```python
import functools
import math

import jax
import jax.numpy as jnp
import numpy as np
from jax import lax
from jax.experimental import pallas as pl
from jax.experimental.pallas import tpu as pltpu
from jax.sharding import PartitionSpec as P

F32 = jnp.float32
BF16 = jnp.bfloat16
MESH = pl.DeviceIdType.MESH
C = 32
ZL = 4
YL = 8
NX = 256
LANES = 128
NK = 128


def mode_numbers(number):
    positions = np.arange(number)
    return np.where(positions < number // 2, positions, positions - number)


def table(cells, modes):
    product = np.remainder(np.outer(mode_numbers(modes), np.arange(cells)), cells)
    angles = product * (2.0 * math.pi / cells)
    return np.cos(angles), np.sin(angles)


def split(a):
    high = a.astype(BF16)
    return high, (a - high.astype(F32)).astype(BF16)


def dot1(a, b, dims):
    return lax.dot_general(a, b, (dims, ((), ())), preferred_element_type=F32)


def dot3(a, b, dims):
    a_high, a_low = a if isinstance(a, tuple) else split(a)
    b_high, b_low = b if isinstance(b, tuple) else split(b)
    return dot1(a_high, b_low, dims) + dot1(a_low, b_high, dims) + dot1(a_high, b_high, dims)


NN = ((1,), (0,))
NT = ((1,), (1,))
TN = ((0,), (0,))


def gelu_slope(values):
    normal_cdf = 0.5 * (1.0 + lax.erf(values * 0.7071067811865476))
    return normal_cdf + values * jnp.exp(-0.5 * values * values) * 0.3989422804014327


def dft4(re, im, sign):
    ar, ai = re[0] + re[2], im[0] + im[2]
    br, bi = re[0] - re[2], im[0] - im[2]
    cr, ci = re[1] + re[3], im[1] + im[3]
    dr, di = re[1] - re[3], im[1] - im[3]
    if sign < 0:
        return [ar + cr, br + di, ar - cr, br - di], [ai + ci, bi - dr, ai - ci, bi + dr]
    return [ar + cr, br - di, ar - cr, br + di], [ai + ci, bi + dr, ai - ci, bi - dr]


def turn(re, im, cos, sin, sign):
    if sign < 0:
        return re * cos + im * sin, im * cos - re * sin
    return re * cos - im * sin, im * cos + re * sin


def plane(ref, start, size):
    return jnp.concatenate([ref[half, pl.ds(start, size), :] for half in range(2)], axis=1)


def put_plane(ref, start, value):
    for half in range(2):
        ref[half, pl.ds(start, value.shape[0]), :] = value[:, half * LANES : (half + 1) * LANES]


def offsets(groups_y):
    sizes = (4, 2, 4) if groups_y == 32 else (4,)
    result = []
    for i in range(1, groups_y):
        moves, rest = [], i
        for size in sizes:
            moves.append((size, rest % size))
            rest //= size
        hops = sum(min(m, n - m) * (2 if n == 2 else 1) for n, m in moves)
        result.append((-hops, tuple(moves)))
    return [moves for _, moves in sorted(result)]


def iota(shape, axis):
    return lax.broadcasted_iota(jnp.int32, shape, axis)


def exchange_kernel(
    groups_y, groups_z, phases, cell_total,
    inp_hbm, pre_hbm, cot_hbm, wts_hbm, mix_hbm, coef_hbm, wx_hbm, wy_hbm, wyt_hbm, tw_hbm,
    lines_out, sten, spectral, red_sum,
    mix_ref, coef_ref, wx_ref, wy_ref, wyt_ref, tw_ref, inp4, pre4, cot4, wts, inp2, slo2, sbuf, rbuf, zsend, zrecv, zsend2, zrecv2, sbuf2,
    hy_send, hy_recv, hz_recv, hid, gram, packed, hin, hsl, hslt, dual, red_send, red_recv,
    load_sem, s1, r1, s2, r2, sz, rz, sz2, rz2, hs_sem, hr_sem, sr, rr, out_sem,
):
    gz = lax.axis_index("gz")
    gy = lax.axis_index("gy")
    modes_x = wx_ref.shape[0] // 2

    def load(i, src, dst):
        return pltpu.make_async_copy(src, dst, load_sem.at[i])

    barrier = pltpu.get_barrier_semaphore()

    def partner(i):
        if isinstance(i, tuple):
            digits, stride, peer = gy, 1, 0
            for size, move in i:
                peer = peer + lax.rem(lax.rem(digits, size) + move, size) * stride
                digits, stride = digits // size, stride * size
            return peer
        return lax.rem(gy + i, groups_y)

    for i in offsets(groups_y):
        pl.semaphore_signal(barrier, inc=1, device_id=(gz, partner(i)), device_id_type=MESH)
    for i in range(1, groups_z):
        peer = lax.rem(gz + i, groups_z)
        pl.semaphore_signal(barrier, inc=1, device_id=(peer, gy), device_id_type=MESH)
    loads = [
        load(0, inp_hbm, inp4),
        load(6, wx_hbm, wx_ref),
        load(1, pre_hbm, pre4),
        load(2, cot_hbm, cot4),
    ]
    small = [
        load(4, mix_hbm, mix_ref),
        load(5, coef_hbm, coef_ref),
        load(7, wy_hbm, wy_ref),
        load(8, wyt_hbm, wyt_ref),
        load(9, tw_hbm, tw_ref),
    ]
    for copy in loads + small:
        copy.start()
    loads[1].wait()

    wx = split(wx_ref[...])

    def along_x(source, field):
        cells = jnp.concatenate(
            [
                jnp.concatenate(
                    [source[half, pl.ds(y, LANES, stride=YL), :] for half in range(2)], axis=1
                )
                for y in range(YL)
            ],
            axis=0,
        )
        result = dot3(wx, cells, NT)
        for y in range(YL):
            for part in range(2):
                sbuf[pl.ds((2 * field + part) * YL + y, modes_x, stride=4 * YL), :] = (
                    result[part * modes_x : (part + 1) * modes_x, y * LANES : (y + 1) * LANES]
                )

    loads[0].wait()
    for z in range(ZL):
        put_plane(inp2, z * 256, inp4[:, z].reshape(256, NX))
    along_x(inp2, 0)
    loads[2].wait()
    loads[3].wait()
    load(3, wts_hbm, wts).start()

    def slope_step(step, carry):
        z = step // 4
        c = lax.rem(step, 4) * 8
        pre = pre4[pl.ds(c, 8), z].reshape(64, NX)
        cot = cot4[pl.ds(c, 8), z].reshape(64, NX)
        put_plane(slo2, pl.multiple_of(step * 64, 64), cot * gelu_slope(pre))
        return carry

    lax.fori_loop(0, 16, slope_step, 0)
    along_x(slo2, 1)
    for z in range(ZL):
        for side, y in enumerate((YL - 1, 0)):
            for half in range(2):
                hy_send[side, half, pl.ds(z * C, C), :] = slo2[
                    half, pl.ds(z * 256 + y, C, stride=YL), :
                ]

    pl.semaphore_wait(barrier, groups_y - 1 + groups_z - 1)

    def rows(ref, index, size=YL):
        return ref.at[pl.ds(pl.multiple_of(index * size, size), size), :]

    def first(i):
        peer = partner(i)
        return pltpu.make_async_remote_copy(
            rows(sbuf, peer, 4 * YL), rows(rbuf, gy, 4 * YL), s1.at[peer], r1.at[gy],
            device_id=(gz, peer), device_id_type=MESH,
        )

    def first_in(i):
        peer = lax.rem(gy + i, groups_y)
        return pltpu.make_async_remote_copy(
            rows(sbuf, peer, 4 * YL), rows(rbuf, peer, 4 * YL), s1.at[peer], r1.at[peer],
            device_id=(gz, peer), device_id_type=MESH,
        )

    def second(i):
        peer = partner(i)
        return pltpu.make_async_remote_copy(
            rows(sbuf2, peer, 2 * YL), rows(lines_out, gy, 2 * YL), s2.at[peer], r2.at[gy],
            device_id=(gz, peer), device_id_type=MESH,
        )

    def second_in(i):
        peer = lax.rem(gy + i, groups_y)
        return pltpu.make_async_remote_copy(
            rows(sbuf2, peer, 2 * YL), rows(lines_out, peer, 2 * YL), s2.at[peer], r2.at[peer],
            device_id=(gz, peer), device_id_type=MESH,
        )

    def across(source, target, send, recv, i, inward):
        peer = lax.rem(gz + i, groups_z)
        slot = peer if inward else gz
        return pltpu.make_async_remote_copy(
            rows(source, peer), rows(target, slot), send.at[peer], recv.at[slot],
            device_id=(peer, gy), device_id_type=MESH,
        )

    def each_far(make):
        for i in offsets(groups_y):
            make(i).start()

    def each(make, action):
        def body(i, carry):
            getattr(make(i), action)()
            return carry

        lax.fori_loop(1, groups_y, body, 0)

    each_far(first)
    own_lines = pl.ds(pl.multiple_of(gy * 4 * YL, 4 * YL), 4 * YL)
    rbuf[own_lines, :] = sbuf[own_lines, :]

    next_z, prev_z = lax.rem(gz + 1, groups_z), lax.rem(gz + groups_z - 1, groups_z)
    next_y, prev_y = lax.rem(gy + 1, groups_y), lax.rem(gy + groups_y - 1, groups_y)
    halos = []
    for i, (source, target, device, sends, takes) in enumerate(
        (
            (slo2.at[:, pl.ds(3 * 256, 256), :], hz_recv.at[0], (next_z, gy),
             gz < groups_z - 1, gz > 0),
            (slo2.at[:, pl.ds(0, 256), :], hz_recv.at[1], (prev_z, gy),
             gz > 0, gz < groups_z - 1),
            (hy_send.at[0], hy_recv.at[0], (gz, next_y), gy < groups_y - 1, gy > 0),
            (hy_send.at[1], hy_recv.at[1], (gz, prev_y), gy > 0, gy < groups_y - 1),
        )
    ):
        copy = pltpu.make_async_remote_copy(
            source, target, hs_sem.at[i], hr_sem.at[i], device_id=device, device_id_type=MESH
        )
        halos.append((copy, sends, takes))
        pl.when(sends)(copy.start)

        @pl.when(jnp.logical_not(takes))
        def _():
            target[...] = jnp.zeros(target.shape, F32)

    for copy in small:
        copy.wait()
    mix = mix_ref[...]
    coef = coef_ref[...]
    expand = (lax.shift_right_logical(iota((256, C), 0), 3) == iota((256, C), 1)).astype(F32)
    gather = (lax.shift_right_logical(iota((C, 256), 1), 3) == iota((C, 256), 0)).astype(F32)
    row_y = lax.bitwise_and(iota((256, 256), 0), 7)
    col_y = lax.bitwise_and(iota((256, 256), 1), 7)

    def outside(which):
        if which < 2:
            return plane(hz_recv.at[which], 0, 256)
        return plane(hy_recv.at[which - 2], 0, ZL * C)

    def gram_of(left, z):
        return dot3(left, split(plane(inp2, z * 256, 256)), NT)

    same = row_y == col_y
    coef_rows = dot3(expand, coef, NT)
    coef_col = [coef_rows[:, j : j + 1] for j in range(5)]
    full = dot3(dot3(expand, mix, NT), expand, NT)
    weight = jnp.concatenate(
        [
            full
            * (
                jnp.where(same, coef_col[0], 0.0)
                + jnp.where(row_y == col_y + 1, coef_col[1], 0.0)
                + jnp.where(row_y == col_y - 1, coef_col[2], 0.0)
            ),
            jnp.where(same, full, 0.0),
        ],
        axis=0,
    )
    weight = split(weight)
    plain = (weight[0][256:512], weight[1][256:512])
    for z in range(ZL):
        both = dot3(weight, plane(slo2, z * 256, 256), NN)
        put_plane(sten, z * 256, both[0:256])
        hid[z + 1] = both[256:512]
    own = [split(plane(slo2, z * 256, 256)) for z in range(ZL)]
    for kind, shift in enumerate((0, -1, 1)):
        total = None
        for z in range(ZL):
            if 0 <= z + shift < ZL:
                term = gram_of(own[z + shift], z)
                total = term if total is None else total + term
        gram[kind] = total

    def moments():
        gram_0 = gram[0]
        gram_up = gram[1] + gram_of(outside(0), 0)
        gram_down = gram[2] + gram_of(outside(1), ZL - 1)
        before_y, after_y = outside(2), outside(3)
        edge = None
        for z in range(ZL):
            at = slice(z * C, (z + 1) * C)
            term = gram_of(jnp.concatenate([before_y[at], after_y[at]], axis=0), z)
            edge = term if z == 0 else edge + term
        pieces = jnp.concatenate(
            [
                jnp.where(same, gram_0, 0.0),
                jnp.where(col_y == row_y + 1, gram_0, 0.0),
                jnp.where(col_y == row_y - 1, gram_0, 0.0),
                jnp.where(same, gram_up, 0.0),
                jnp.where(same, gram_down, 0.0),
            ],
            axis=1,
        )
        summed = dot3(gather, pieces, NN)
        edge_y = col_y[0:C]
        sums = [summed[:, j * 256 : (j + 1) * 256] for j in range(5)]
        sums[1] = sums[1] + jnp.where(edge_y == 0, edge[0:C], 0.0)
        sums[2] = sums[2] + jnp.where(edge_y == YL - 1, edge[C : 2 * C], 0.0)
        every = dot3(jnp.concatenate(sums, axis=0), expand, NN)
        parts = [every[j * C : (j + 1) * C] for j in range(5)]
        local_mix = coef[0:1, :] * parts[0]
        for j in range(1, 5):
            local_mix = local_mix + coef[j : j + 1, :] * parts[j]
        red_send[0, 0:16, 0:C] = local_mix[0:16]
        red_send[0, 0:16, C : 2 * C] = local_mix[16:32]
        red_send[0, 0:16, 2 * C :] = jnp.zeros((16, 2 * C), F32)
        for j in range(5):
            red_send[0, j : j + 1, 2 * C : 3 * C] = jnp.sum(
                mix * parts[j], axis=0, keepdims=True
            )

    def place(phase):
        stride, size = phases[phase]
        if stride == 0:
            return size, gz
        return size, lax.rem(gy // stride, size)

    def piece(phase, i, inward):
        stride, _ = phases[phase]
        size, mine = place(phase)
        peer = lax.rem(mine + i, size)
        slot = peer if inward else mine
        device = (peer, gy) if stride == 0 else (gz, gy + (peer - mine) * stride)
        return pltpu.make_async_remote_copy(
            red_send.at[phase], red_recv.at[phase, slot], sr.at[phase, i], rr.at[phase, slot],
            device_id=device, device_id_type=MESH,
        )

    def tree_send(phase):
        size, mine = place(phase)
        for i in range(1, size):
            piece(phase, i, False).start()
        red_recv[phase, mine] = red_send[phase]

    def tree_take(phase):
        size, _ = place(phase)
        for i in range(1, size):
            piece(phase, i, True).wait_recv()
        total = red_recv[phase, 0]
        for j in range(1, size):
            total = total + red_recv[phase, j]
        if phase + 1 < len(phases):
            red_send[phase + 1] = total
        else:
            red_sum[...] = total * (1.0 / 1024.0)

    load(3, wts_hbm, wts).wait()

    def pack_step(group, carry):
        q, j = group // 8, lax.rem(group, 8)
        for part in range(2):
            for m in range(4):
                packed[part, group, :, m * C : (m + 1) * C] = wts[part, (q + 4 * m) * 8 + j]
        return carry

    lax.fori_loop(0, 32, pack_step, 0)

    each(first_in, "wait_recv")
    received = rbuf[...].reshape(groups_y, 4, YL, LANES)
    received = jnp.concatenate(
        [received[:, part].reshape(groups_y * YL, LANES) for part in range(4)], axis=1
    )
    turned = dot3(wy_ref[...], received, NN)
    cos_part, sin_part = turned[0:32], turned[32:64]
    for field in range(2):
        re = slice(2 * field * LANES, (2 * field + 1) * LANES)
        im = slice((2 * field + 1) * LANES, (2 * field + 2) * LANES)
        zsend[:, re] = cos_part[:, re] + sin_part[:, im]
        zsend[:, im] = cos_part[:, im] - sin_part[:, re]
    for i in range(1, groups_z):
        across(zsend, zrecv, sz, rz, i, False).start()
    mine = pl.ds(pl.multiple_of(gz * 8, 8), 8)
    zrecv[mine, :] = zsend[mine, :]
    for i in range(1, groups_z):
        across(zsend, zrecv, sz, rz, i, True).wait_recv()

    cos_z = [tw_ref[2 * k : 2 * k + 1, :] for k in range(4)]
    sin_z = [tw_ref[2 * k + 1 : 2 * k + 2, :] for k in range(4)]
    for field in range(2):
        base = 2 * field * LANES
        re = [zrecv[q * 8 : q * 8 + 8, base : base + LANES] for q in range(4)]
        im = [zrecv[q * 8 : q * 8 + 8, base + LANES : base + 2 * LANES] for q in range(4)]
        re, im = dft4(re, im, -1)
        for k in range(4):
            t_re, t_im = re[k], im[k]
            if k:
                t_re, t_im = turn(t_re, t_im, cos_z[k], sin_z[k], -1)
            f_re, f_im = dft4(
                [t_re] + [pltpu.roll(t_re, LANES - 32 * s, 1) for s in range(1, 4)],
                [t_im] + [pltpu.roll(t_im, LANES - 32 * s, 1) for s in range(1, 4)],
                -1,
            )
            for m in range(4):
                at = pl.ds((k + 4 * m) * 8, 8)
                if field == 0:
                    hin[0, at, :] = f_re[m]
                    hin[1, at, :] = f_im[m]
                else:
                    hsl[0, at, :] = f_re[m] * (1.0 / cell_total)
                    hsl[1, at, :] = f_im[m] * (1.0 / cell_total)
    for part in range(2):
        hslt[part] = hsl[part].T[0:C, :]

    for copy, _, takes in halos:
        pl.when(takes)(copy.wait_recv)
    moments()
    tree_send(0)

    lane = iota((C, LANES), 1)

    def dual_step(q, carry):
        shift = lax.rem(NK - q * 8, NK)
        slope_re = pltpu.roll(hslt[0], shift, 1)
        slope_im = pltpu.roll(hslt[1], shift, 1)
        for j in range(8):
            group = q * 8 + j
            spread = lax.bitwise_and(lane, 96) + j
            s_re = jnp.take_along_axis(slope_re, spread, axis=1)
            s_im = jnp.take_along_axis(slope_im, spread, axis=1)
            w_re, w_im = packed[0, group], packed[1, group]
            dual[0, pl.ds(group, 1), :] = jnp.sum(w_re * s_re + w_im * s_im, axis=0, keepdims=True)
            dual[1, pl.ds(group, 1), :] = jnp.sum(w_re * s_im - w_im * s_re, axis=0, keepdims=True)
        return carry

    lax.fori_loop(0, 4, dual_step, 0)

    block = lax.shift_right_logical(iota((8, LANES), 1), 5)
    v_re, v_im = [], []
    for k in range(4):
        u_re, u_im = dft4(
            *(
                [dual[part, k * 8 : k * 8 + 8, :]]
                + [
                    pltpu.roll(dual[part, k * 8 : k * 8 + 8, :], LANES - 32 * m, 1)
                    for m in range(1, 4)
                ]
                for part in range(2)
            ),
            1,
        )
        turned = []
        for u in (u_re, u_im):
            value = u[0]
            for s in range(1, 4):
                value = jnp.where(block == s, pltpu.roll(u[s], 32 * s, 1), value)
            turned.append(value)
        if k:
            turned = turn(turned[0], turned[1], cos_z[k], sin_z[k], 1)
        v_re.append(turned[0])
        v_im.append(turned[1])
    v_re, v_im = dft4(v_re, v_im, 1)
    for q in range(4):
        zsend2[q * 8 : q * 8 + 8, 0:LANES] = v_re[q]
        zsend2[q * 8 : q * 8 + 8, LANES : 2 * LANES] = v_im[q]
    for i in range(1, groups_z):
        across(zsend2, zrecv2, sz2, rz2, i, False).start()
    zrecv2[mine, :] = zsend2[mine, :]
    tree_take(0)
    tree_send(1)
    for i in range(1, groups_z):
        across(zsend2, zrecv2, sz2, rz2, i, True).wait_recv()

    upper = zrecv2[...]
    lower = jnp.concatenate([-upper[:, LANES:], upper[:, :LANES]], axis=1)
    back = dot3(wyt_ref[...], jnp.concatenate([upper, lower], axis=0), NN)
    sbuf2[...] = jnp.concatenate(
        [
            back[:, part * LANES : (part + 1) * LANES].reshape(groups_y, 1, YL, LANES)
            for part in range(2)
        ],
        axis=1,
    ).reshape(groups_y * 2 * YL, LANES)
    each_far(second)
    own_rows = pltpu.make_async_copy(rows(sbuf2, gy, 2 * YL), rows(lines_out, gy, 2 * YL), out_sem.at[0])
    own_rows.start()

    def outer_step(step, carry):
        shift = lax.rem(NK - step * 32, NK)
        slope_re = pltpu.roll(hslt[0], shift, 1)
        slope_im = pltpu.roll(hslt[1], shift, 1)
        for j in range(32):
            k = step * 32 + j
            s_re = jnp.broadcast_to(slope_re[:, j : j + 1], (C, C))
            s_im = jnp.broadcast_to(slope_im[:, j : j + 1], (C, C))
            i_re = hin[0, pl.ds(k, 1), 0:C]
            i_im = hin[1, pl.ds(k, 1), 0:C]
            spectral[0, k] = s_re * i_re + s_im * i_im
            spectral[1, k] = s_im * i_re - s_re * i_im
        return carry

    lax.fori_loop(0, 4, outer_step, 0)
    tree_take(1)
    if len(phases) > 2:
        tree_send(2)
    hid[0] = dot3(plain, outside(0), NN)
    hid[5] = dot3(plain, outside(1), NN)
    for z in range(ZL):
        total = plane(sten, z * 256, 256) + coef_col[3] * hid[z] + coef_col[4] * hid[z + 2]
        put_plane(sten, z * 256, total)
    coef_small = dot3((iota((C, C), 0) == iota((C, C), 1)).astype(F32), coef, NT)
    before_y, after_y = outside(2), outside(3)
    edges = jnp.concatenate(
        [side[z * C : (z + 1) * C] for side in (before_y, after_y) for z in range(ZL)], axis=1
    )
    edge_hidden = dot3(mix, edges, TN)
    for z in range(ZL):
        for side, y in enumerate((0, YL - 1)):
            at = pl.ds(z * 256 + y, C, stride=YL)
            for half in range(2):
                column = (side * ZL + z) * NX + half * LANES
                sten[half, at, :] = (
                    sten[half, at, :]
                    + coef_small[:, 1 + side : 2 + side]
                    * edge_hidden[:, column : column + LANES]
                )
    if len(phases) > 2:
        tree_take(2)

    each(second_in, "wait_recv")
    own_rows.wait()
    each(first, "wait_send")
    each(second, "wait_send")
    for copy, sends, _ in halos:
        pl.when(sends)(copy.wait_send)
    for i in range(1, groups_z):
        across(zsend, zrecv, sz, rz, i, False).wait_send()
        across(zsend2, zrecv2, sz2, rz2, i, False).wait_send()
    for phase in range(len(phases)):
        for i in range(1, place(phase)[0]):
            piece(phase, i, False).wait_send()


def result_kernel(
    lines, sten, spectral, red, wx_ref,
    grad_input, grad_spectral, grad_mix, grad_coef,
    cells, field, mix_out, coef_out, out_sem,
):
    modes_x = wx_ref.shape[0] // 2
    out = pltpu.make_async_copy(spectral, grad_spectral, out_sem.at[0])
    out.start()
    mix_out[0:16, :] = red[:, 0:C]
    mix_out[16:32, :] = red[:, C : 2 * C]
    coef_out[...] = red[0:5, 2 * C : 3 * C]
    small = [
        pltpu.make_async_copy(mix_out, grad_mix, out_sem.at[1]),
        pltpu.make_async_copy(coef_out, grad_coef, out_sem.at[2]),
    ]
    for copy in small:
        copy.start()
    spread = jnp.concatenate(
        [
            jnp.concatenate(
                [lines[pl.ds(part * YL + y, modes_x, stride=2 * YL), :] for y in range(YL)], axis=1
            )
            for part in range(2)
        ],
        axis=0,
    )
    result = dot3(spread, wx_ref[...], TN)
    for y in range(YL):
        for half in range(2):
            cells[half, pl.ds(y, LANES, stride=YL), :] = result[
                y * LANES : (y + 1) * LANES, half * LANES : (half + 1) * LANES
            ]
    planes = []
    for z in range(ZL):
        total = plane(cells, z * 256, 256) + plane(sten, z * 256, 256)
        field[z] = total.reshape(C, YL, NX)
        planes.append(pltpu.make_async_copy(field.at[z], grad_input.at[:, z], out_sem.at[3 + z]))
        planes[-1].start()
    for copy in planes + small + [out]:
        copy.wait()


def per_device(input_field, pre_activation, cotangent, spectral_weights, mix_weights, coefficients):
    groups_y = lax.axis_size("gy")
    groups_z = lax.axis_size("gz")
    grid_y = YL * groups_y
    modes_x = groups_y
    cell_total = NX * grid_y * ZL * groups_z
    phases = ((0, groups_z), (1, 8), (8, 4)) if groups_y == 32 else ((0, groups_z), (1, 4))
    rows_y = groups_y * YL
    cos_x, sin_x = table(NX, modes_x)
    cos_y, sin_y = table(grid_y, 32)
    wx = np.concatenate([cos_x, -sin_x]).astype(np.float32)
    wy = np.concatenate([cos_y, sin_y]).astype(np.float32)
    cell = np.arange(LANES) // C
    tw = np.stack(
        [fn(2.0 * math.pi * k * cell / 16.0) for k in range(4) for fn in (np.cos, np.sin)]
    ).astype(np.float32)
    weights = spectral_weights.reshape(2, NK, C, C)
    vmem = pl.BlockSpec(memory_space=pltpu.VMEM)
    hbm = pl.BlockSpec(memory_space=pltpu.HBM)
    sds = jax.ShapeDtypeStruct
    dma = pltpu.SemaphoreType.DMA
    lines, sten, spectral, red = pl.pallas_call(
        functools.partial(exchange_kernel, groups_y, groups_z, phases, cell_total),
        name="exchange",
        out_shape=(
            pltpu.VMEM((2 * rows_y, LANES), F32),
            pltpu.VMEM((2, ZL * 256, LANES), F32),
            pltpu.VMEM((2, NK, C, C), F32),
            pltpu.VMEM((16, LANES), F32),
        ),
        in_specs=[hbm] * 10,
        out_specs=(vmem,) * 4,
        scratch_shapes=[
            pltpu.VMEM((C, C), F32),
            pltpu.VMEM((5, C), F32),
            pltpu.VMEM(wx.shape, F32),
            pltpu.VMEM(wy.shape, F32),
            pltpu.VMEM(wy.T.shape, F32),
            pltpu.VMEM(tw.shape, F32),
            pltpu.VMEM((C, ZL, YL, NX), F32),
            pltpu.VMEM((C, ZL, YL, NX), F32),
            pltpu.VMEM((C, ZL, YL, NX), F32),
            pltpu.VMEM((2, NK, C, C), F32),
            pltpu.VMEM((2, ZL * 256, LANES), F32),
            pltpu.VMEM((2, ZL * 256, LANES), F32),
            pltpu.VMEM((4 * rows_y, LANES), F32),
            pltpu.VMEM((4 * rows_y, LANES), F32),
            pltpu.VMEM((32, 4 * LANES), F32),
            pltpu.VMEM((32, 4 * LANES), F32),
            pltpu.VMEM((32, 2 * LANES), F32),
            pltpu.VMEM((32, 2 * LANES), F32),
            pltpu.VMEM((2 * rows_y, LANES), F32),
            pltpu.VMEM((2, 2, ZL * C, LANES), F32),
            pltpu.VMEM((2, 2, ZL * C, LANES), F32),
            pltpu.VMEM((2, 2, 256, LANES), F32),
            pltpu.VMEM((6, 256, NX), F32),
            pltpu.VMEM((3, 256, 256), F32),
            pltpu.VMEM((2, 32, C, LANES), F32),
            pltpu.VMEM((2, NK, LANES), F32),
            pltpu.VMEM((2, NK, LANES), F32),
            pltpu.VMEM((2, C, NK), F32),
            pltpu.VMEM((2, 32, LANES), F32),
            pltpu.VMEM((len(phases), 16, LANES), F32),
            pltpu.VMEM((len(phases), 8, 16, LANES), F32),
            dma((10,)),
            dma((groups_y,)), dma((groups_y,)), dma((groups_y,)), dma((groups_y,)),
            dma((groups_z,)), dma((groups_z,)), dma((groups_z,)), dma((groups_z,)),
            dma((4,)), dma((4,)),
            dma((len(phases), 8)), dma((len(phases), 8)),
            dma((1,)),
        ],
        compiler_params=pltpu.CompilerParams(
            collective_id=0, has_side_effects=True, vmem_limit_bytes=40 << 20
        ),
    )(
        *(
            pltpu.with_memory_space_constraint(operand, pltpu.HBM)
            for operand in (
                input_field, pre_activation, cotangent, weights, mix_weights, coefficients,
                jnp.asarray(wx), jnp.asarray(wy), jnp.asarray(wy.T.copy()), jnp.asarray(tw),
            )
        )
    )
    grad_input, grad_spectral, grad_mix, grad_coef = pl.pallas_call(
        result_kernel,
        name="result",
        out_shape=(
            sds((C, ZL, YL, NX), F32),
            sds((2, NK, C, C), F32),
            sds((C, C), F32),
            sds((5, C), F32),
        ),
        in_specs=[vmem] * 5,
        out_specs=(hbm,) * 4,
        scratch_shapes=[
            pltpu.VMEM((2, ZL * 256, LANES), F32),
            pltpu.VMEM((ZL, C, YL, NX), F32),
            pltpu.VMEM((C, C), F32),
            pltpu.VMEM((5, C), F32),
            dma((3 + ZL,)),
        ],
        compiler_params=pltpu.CompilerParams(vmem_limit_bytes=24 << 20),
    )(lines, sten, spectral, red, jnp.asarray(wx))
    return (grad_input, grad_spectral.reshape(spectral_weights.shape), grad_mix, grad_coef)


def solution(mesh):
    in_specs = (
        P(None, "gz", "gy", None),
        P(None, "gz", "gy", None),
        P(None, "gz", "gy", None),
        P(None, None, "gz", "gy", None, None),
        P(),
        P(),
    )
    out_specs = (P(None, "gz", "gy", None), P(None, None, "gz", "gy", None, None), P(), P())
    return jax.shard_map(
        per_device, mesh=mesh, in_specs=in_specs, out_specs=out_specs, check_vma=False
    )
```

```python
import functools
import math

import jax
import jax.numpy as jnp
import numpy as np
from jax import lax
from jax.experimental import pallas as pl
from jax.experimental.pallas import tpu as pltpu
from jax.sharding import PartitionSpec as P

F32 = jnp.float32
BF16 = jnp.bfloat16
MESH = pl.DeviceIdType.MESH
C = 32
ZL = 4
YL = 8
NX = 256
LANES = 128
NK = 128


def mode_numbers(number):
    positions = np.arange(number)
    return np.where(positions < number // 2, positions, positions - number)


def table(cells, modes):
    product = np.remainder(np.outer(mode_numbers(modes), np.arange(cells)), cells)
    angles = product * (2.0 * math.pi / cells)
    return np.cos(angles), np.sin(angles)


def split(a):
    high = a.astype(BF16)
    return high, (a - high.astype(F32)).astype(BF16)


def dot1(a, b, dims):
    return lax.dot_general(a, b, (dims, ((), ())), preferred_element_type=F32)


def dot3(a, b, dims):
    a_high, a_low = a if isinstance(a, tuple) else split(a)
    b_high, b_low = b if isinstance(b, tuple) else split(b)
    return dot1(a_high, b_low, dims) + dot1(a_low, b_high, dims) + dot1(a_high, b_high, dims)


NN = ((1,), (0,))
NT = ((1,), (1,))
TN = ((0,), (0,))


def gelu_slope(values):
    normal_cdf = 0.5 * (1.0 + lax.erf(values * 0.7071067811865476))
    return normal_cdf + values * jnp.exp(-0.5 * values * values) * 0.3989422804014327


def dft4(re, im, sign):
    ar, ai = re[0] + re[2], im[0] + im[2]
    br, bi = re[0] - re[2], im[0] - im[2]
    cr, ci = re[1] + re[3], im[1] + im[3]
    dr, di = re[1] - re[3], im[1] - im[3]
    if sign < 0:
        return [ar + cr, br + di, ar - cr, br - di], [ai + ci, bi - dr, ai - ci, bi + dr]
    return [ar + cr, br - di, ar - cr, br + di], [ai + ci, bi + dr, ai - ci, bi - dr]


def turn(re, im, cos, sin, sign):
    if sign < 0:
        return re * cos + im * sin, im * cos - re * sin
    return re * cos - im * sin, im * cos + re * sin


def plane(ref, start, size):
    return jnp.concatenate([ref[half, pl.ds(start, size), :] for half in range(2)], axis=1)


def put_plane(ref, start, value):
    for half in range(2):
        ref[half, pl.ds(start, value.shape[0]), :] = value[:, half * LANES : (half + 1) * LANES]


def offsets(groups_y):
    sizes = (4, 2, 4) if groups_y == 32 else (4,)
    result = []
    for i in range(1, groups_y):
        moves, rest = [], i
        for size in sizes:
            moves.append((size, rest % size))
            rest //= size
        hops = sum(min(m, n - m) * (2 if n == 2 else 1) for n, m in moves)
        result.append((-hops, tuple(moves)))
    return [moves for _, moves in sorted(result)]


def iota(shape, axis):
    return lax.broadcasted_iota(jnp.int32, shape, axis)


def exchange_kernel(
    groups_y, groups_z, phases, cell_total,
    inp_hbm, pre_hbm, cot_hbm, wts_hbm, mix_hbm, coef_hbm, wx_hbm, wy_hbm, wyt_hbm, tw_hbm,
    lines_out, sten, spectral, red_sum,
    mix_ref, coef_ref, wx_ref, wy_ref, wyt_ref, tw_ref, inp4, pre4, cot4, wts, inp2, slo2, sbuf, rbuf, zsend, zrecv, zsend2, zrecv2, sbuf2,
    hy_send, hy_recv, hz_recv, hid, inner, packed, hin, hsl, hslt, dual, red_send, red_recv,
    load_sem, s1, r1, s2, r2, sz, rz, sz2, rz2, hs_sem, hr_sem, sr, rr, out_sem,
):
    gz = lax.axis_index("gz")
    gy = lax.axis_index("gy")
    modes_x = wx_ref.shape[0] // 2

    def load(i, src, dst):
        return pltpu.make_async_copy(src, dst, load_sem.at[i])

    barrier = pltpu.get_barrier_semaphore()

    def partner(i):
        if isinstance(i, tuple):
            digits, stride, peer = gy, 1, 0
            for size, move in i:
                peer = peer + lax.rem(lax.rem(digits, size) + move, size) * stride
                digits, stride = digits // size, stride * size
            return peer
        return lax.rem(gy + i, groups_y)

    for i in offsets(groups_y):
        pl.semaphore_signal(barrier, inc=1, device_id=(gz, partner(i)), device_id_type=MESH)
    for i in range(1, groups_z):
        peer = lax.rem(gz + i, groups_z)
        pl.semaphore_signal(barrier, inc=1, device_id=(peer, gy), device_id_type=MESH)
    loads = [
        load(0, inp_hbm, inp4),
        load(6, wx_hbm, wx_ref),
        load(1, pre_hbm, pre4),
        load(2, cot_hbm, cot4),
    ]
    small = [
        load(4, mix_hbm, mix_ref),
        load(5, coef_hbm, coef_ref),
        load(7, wy_hbm, wy_ref),
        load(8, wyt_hbm, wyt_ref),
        load(9, tw_hbm, tw_ref),
    ]
    for copy in loads + small:
        copy.start()
    loads[1].wait()

    wx = split(wx_ref[...])

    def along_x(source, field):
        cells = jnp.concatenate(
            [
                jnp.concatenate(
                    [source[half, pl.ds(y, LANES, stride=YL), :] for half in range(2)], axis=1
                )
                for y in range(YL)
            ],
            axis=0,
        )
        result = dot3(wx, cells, NT)
        for y in range(YL):
            for part in range(2):
                sbuf[pl.ds((2 * field + part) * YL + y, modes_x, stride=4 * YL), :] = (
                    result[part * modes_x : (part + 1) * modes_x, y * LANES : (y + 1) * LANES]
                )

    loads[0].wait()
    for z in range(ZL):
        put_plane(inp2, z * 256, inp4[:, z].reshape(256, NX))
    along_x(inp2, 0)
    loads[2].wait()
    loads[3].wait()
    load(3, wts_hbm, wts).start()

    def slope_step(step, carry):
        z = step // 4
        c = lax.rem(step, 4) * 8
        pre = pre4[pl.ds(c, 8), z].reshape(64, NX)
        cot = cot4[pl.ds(c, 8), z].reshape(64, NX)
        put_plane(slo2, pl.multiple_of(step * 64, 64), cot * gelu_slope(pre))
        return carry

    lax.fori_loop(0, 16, slope_step, 0)
    along_x(slo2, 1)
    for z in range(ZL):
        for side, y in enumerate((YL - 1, 0)):
            for half in range(2):
                hy_send[side, half, pl.ds(z * C, C), :] = slo2[
                    half, pl.ds(z * 256 + y, C, stride=YL), :
                ]

    pl.semaphore_wait(barrier, groups_y - 1 + groups_z - 1)

    def rows(ref, index, size=YL):
        return ref.at[pl.ds(pl.multiple_of(index * size, size), size), :]

    def first(i):
        peer = partner(i)
        return pltpu.make_async_remote_copy(
            rows(sbuf, peer, 4 * YL), rows(rbuf, gy, 4 * YL), s1.at[peer], r1.at[gy],
            device_id=(gz, peer), device_id_type=MESH,
        )

    def first_in(i):
        peer = lax.rem(gy + i, groups_y)
        return pltpu.make_async_remote_copy(
            rows(sbuf, peer, 4 * YL), rows(rbuf, peer, 4 * YL), s1.at[peer], r1.at[peer],
            device_id=(gz, peer), device_id_type=MESH,
        )

    def second(i):
        peer = partner(i)
        return pltpu.make_async_remote_copy(
            rows(sbuf2, peer, 2 * YL), rows(lines_out, gy, 2 * YL), s2.at[peer], r2.at[gy],
            device_id=(gz, peer), device_id_type=MESH,
        )

    def second_in(i):
        peer = lax.rem(gy + i, groups_y)
        return pltpu.make_async_remote_copy(
            rows(sbuf2, peer, 2 * YL), rows(lines_out, peer, 2 * YL), s2.at[peer], r2.at[peer],
            device_id=(gz, peer), device_id_type=MESH,
        )

    def across(source, target, send, recv, i, inward):
        peer = lax.rem(gz + i, groups_z)
        slot = peer if inward else gz
        return pltpu.make_async_remote_copy(
            rows(source, peer), rows(target, slot), send.at[peer], recv.at[slot],
            device_id=(peer, gy), device_id_type=MESH,
        )

    def each_far(make):
        for i in offsets(groups_y):
            make(i).start()

    def each(make, action):
        def body(i, carry):
            getattr(make(i), action)()
            return carry

        lax.fori_loop(1, groups_y, body, 0)

    each_far(first)
    own_lines = pl.ds(pl.multiple_of(gy * 4 * YL, 4 * YL), 4 * YL)
    rbuf[own_lines, :] = sbuf[own_lines, :]

    next_z, prev_z = lax.rem(gz + 1, groups_z), lax.rem(gz + groups_z - 1, groups_z)
    next_y, prev_y = lax.rem(gy + 1, groups_y), lax.rem(gy + groups_y - 1, groups_y)
    halos = []
    for i, (source, target, device, sends, takes) in enumerate(
        (
            (slo2.at[:, pl.ds(3 * 256, 256), :], hz_recv.at[0], (next_z, gy),
             gz < groups_z - 1, gz > 0),
            (slo2.at[:, pl.ds(0, 256), :], hz_recv.at[1], (prev_z, gy),
             gz > 0, gz < groups_z - 1),
            (hy_send.at[0], hy_recv.at[0], (gz, next_y), gy < groups_y - 1, gy > 0),
            (hy_send.at[1], hy_recv.at[1], (gz, prev_y), gy > 0, gy < groups_y - 1),
        )
    ):
        copy = pltpu.make_async_remote_copy(
            source, target, hs_sem.at[i], hr_sem.at[i], device_id=device, device_id_type=MESH
        )
        halos.append((copy, sends, takes))
        pl.when(sends)(copy.start)

        @pl.when(jnp.logical_not(takes))
        def _():
            target[...] = jnp.zeros(target.shape, F32)

    for copy in small:
        copy.wait()
    mix = mix_ref[...]
    coef = coef_ref[...]
    expand = (lax.shift_right_logical(iota((256, C), 0), 3) == iota((256, C), 1)).astype(F32)
    gather = (lax.shift_right_logical(iota((C, 256), 1), 3) == iota((C, 256), 0)).astype(F32)
    row_y = lax.bitwise_and(iota((256, 256), 0), 7)
    col_y = lax.bitwise_and(iota((256, 256), 1), 7)

    def outside(which):
        if which < 2:
            return plane(hz_recv.at[which], 0, 256)
        return plane(hy_recv.at[which - 2], 0, ZL * C)

    def gram_of(left, z):
        return dot3(left, split(plane(inp2, z * 256, 256)), NT)

    same = row_y == col_y
    coef_rows = dot3(expand, coef, NT)
    coef_col = [coef_rows[:, j : j + 1] for j in range(5)]
    full = dot3(dot3(expand, mix, NT), expand, NT)
    weight = jnp.concatenate(
        [
            full
            * (
                jnp.where(same, coef_col[0], 0.0)
                + jnp.where(row_y == col_y + 1, coef_col[1], 0.0)
                + jnp.where(row_y == col_y - 1, coef_col[2], 0.0)
            ),
            jnp.where(same, full, 0.0),
        ],
        axis=0,
    )
    weight = split(weight)
    plain = (weight[0][256:512], weight[1][256:512])
    for z in range(ZL):
        both = dot3(weight, plane(slo2, z * 256, 256), NN)
        put_plane(sten, z * 256, both[0:256])
        hid[z + 1] = both[256:512]
    own = [split(plane(slo2, z * 256, 256)) for z in range(ZL)]
    grams = []
    for shift in (0, -1, 1):
        total = None
        for z in range(ZL):
            if 0 <= z + shift < ZL:
                term = gram_of(own[z + shift], z)
                total = term if total is None else total + term
        grams.append(total)
    pieces = jnp.concatenate(
        [
            jnp.where(same, grams[0], 0.0),
            jnp.where(col_y == row_y + 1, grams[0], 0.0),
            jnp.where(col_y == row_y - 1, grams[0], 0.0),
            jnp.where(same, grams[1], 0.0),
            jnp.where(same, grams[2], 0.0),
        ],
        axis=1,
    )
    summed = dot3(gather, pieces, NN)
    sums = [summed[:, j * 256 : (j + 1) * 256] for j in range(5)]
    inner[...] = dot3(jnp.concatenate(sums, axis=0), expand, NN)

    def along(ref, starts, stride):
        return jnp.concatenate(
            [
                ref[half, pl.ds(start, C, stride=stride), :]
                for start in starts
                for half in range(2)
            ],
            axis=1,
        )

    def moments():
        planes_y = [z * 256 for z in range(ZL)]
        rows_z = [z * C for z in range(ZL)]
        lines_y = list(range(YL))
        last = (ZL - 1) * 256
        outer = {
            1: (along(hy_recv.at[0], rows_z, 1), along(inp2, planes_y, YL)),
            2: (
                along(hy_recv.at[1], rows_z, 1),
                along(inp2, [start + YL - 1 for start in planes_y], YL),
            ),
            3: (along(hz_recv.at[0], lines_y, YL), along(inp2, lines_y, YL)),
            4: (
                along(hz_recv.at[1], lines_y, YL),
                along(inp2, [last + y for y in lines_y], YL),
            ),
        }
        parts = [inner[j * C : (j + 1) * C, :] for j in range(5)]
        for j, (left, right) in outer.items():
            parts[j] = parts[j] + dot3(left, right, NT)
        local_mix = coef[0:1, :] * parts[0]
        for j in range(1, 5):
            local_mix = local_mix + coef[j : j + 1, :] * parts[j]
        red_send[0, 0:16, 0:C] = local_mix[0:16]
        red_send[0, 0:16, C : 2 * C] = local_mix[16:32]
        red_send[0, 0:16, 2 * C :] = jnp.zeros((16, 2 * C), F32)
        for j in range(5):
            red_send[0, j : j + 1, 2 * C : 3 * C] = jnp.sum(
                mix * parts[j], axis=0, keepdims=True
            )

    def place(phase):
        stride, size = phases[phase]
        if stride == 0:
            return size, gz
        return size, lax.rem(gy // stride, size)

    def piece(phase, i, inward):
        stride, _ = phases[phase]
        size, mine = place(phase)
        peer = lax.rem(mine + i, size)
        slot = peer if inward else mine
        device = (peer, gy) if stride == 0 else (gz, gy + (peer - mine) * stride)
        return pltpu.make_async_remote_copy(
            red_send.at[phase], red_recv.at[phase, slot], sr.at[phase, i], rr.at[phase, slot],
            device_id=device, device_id_type=MESH,
        )

    def tree_send(phase):
        size, mine = place(phase)
        for i in range(1, size):
            piece(phase, i, False).start()
        red_recv[phase, mine] = red_send[phase]

    def tree_take(phase):
        size, _ = place(phase)
        for i in range(1, size):
            piece(phase, i, True).wait_recv()
        total = red_recv[phase, 0]
        for j in range(1, size):
            total = total + red_recv[phase, j]
        if phase + 1 < len(phases):
            red_send[phase + 1] = total
        else:
            red_sum[...] = total * (1.0 / 1024.0)

    load(3, wts_hbm, wts).wait()

    def pack_step(group, carry):
        q, j = group // 8, lax.rem(group, 8)
        for part in range(2):
            for m in range(4):
                packed[part, group, :, m * C : (m + 1) * C] = wts[part, (q + 4 * m) * 8 + j]
        return carry

    lax.fori_loop(0, 32, pack_step, 0)

    each(first_in, "wait_recv")
    received = rbuf[...].reshape(groups_y, 4, YL, LANES)
    received = jnp.concatenate(
        [received[:, part].reshape(groups_y * YL, LANES) for part in range(4)], axis=1
    )
    turned = dot3(wy_ref[...], received, NN)
    cos_part, sin_part = turned[0:32], turned[32:64]
    for field in range(2):
        re = slice(2 * field * LANES, (2 * field + 1) * LANES)
        im = slice((2 * field + 1) * LANES, (2 * field + 2) * LANES)
        zsend[:, re] = cos_part[:, re] + sin_part[:, im]
        zsend[:, im] = cos_part[:, im] - sin_part[:, re]
    for i in range(1, groups_z):
        across(zsend, zrecv, sz, rz, i, False).start()
    mine = pl.ds(pl.multiple_of(gz * 8, 8), 8)
    zrecv[mine, :] = zsend[mine, :]
    for i in range(1, groups_z):
        across(zsend, zrecv, sz, rz, i, True).wait_recv()

    cos_z = [tw_ref[2 * k : 2 * k + 1, :] for k in range(4)]
    sin_z = [tw_ref[2 * k + 1 : 2 * k + 2, :] for k in range(4)]
    for field in range(2):
        base = 2 * field * LANES
        re = [zrecv[q * 8 : q * 8 + 8, base : base + LANES] for q in range(4)]
        im = [zrecv[q * 8 : q * 8 + 8, base + LANES : base + 2 * LANES] for q in range(4)]
        re, im = dft4(re, im, -1)
        for k in range(4):
            t_re, t_im = re[k], im[k]
            if k:
                t_re, t_im = turn(t_re, t_im, cos_z[k], sin_z[k], -1)
            f_re, f_im = dft4(
                [t_re] + [pltpu.roll(t_re, LANES - 32 * s, 1) for s in range(1, 4)],
                [t_im] + [pltpu.roll(t_im, LANES - 32 * s, 1) for s in range(1, 4)],
                -1,
            )
            for m in range(4):
                at = pl.ds((k + 4 * m) * 8, 8)
                if field == 0:
                    hin[0, at, :] = f_re[m]
                    hin[1, at, :] = f_im[m]
                else:
                    hsl[0, at, :] = f_re[m] * (1.0 / cell_total)
                    hsl[1, at, :] = f_im[m] * (1.0 / cell_total)
    for part in range(2):
        hslt[part] = hsl[part].T[0:C, :]

    for copy, _, takes in halos:
        pl.when(takes)(copy.wait_recv)
    moments()
    tree_send(0)

    lane = iota((C, LANES), 1)

    def dual_step(q, carry):
        shift = lax.rem(NK - q * 8, NK)
        slope_re = pltpu.roll(hslt[0], shift, 1)
        slope_im = pltpu.roll(hslt[1], shift, 1)
        for j in range(8):
            group = q * 8 + j
            spread = lax.bitwise_and(lane, 96) + j
            s_re = jnp.take_along_axis(slope_re, spread, axis=1)
            s_im = jnp.take_along_axis(slope_im, spread, axis=1)
            w_re, w_im = packed[0, group], packed[1, group]
            dual[0, pl.ds(group, 1), :] = jnp.sum(w_re * s_re + w_im * s_im, axis=0, keepdims=True)
            dual[1, pl.ds(group, 1), :] = jnp.sum(w_re * s_im - w_im * s_re, axis=0, keepdims=True)
        return carry

    lax.fori_loop(0, 4, dual_step, 0)

    block = lax.shift_right_logical(iota((8, LANES), 1), 5)
    v_re, v_im = [], []
    for k in range(4):
        u_re, u_im = dft4(
            *(
                [dual[part, k * 8 : k * 8 + 8, :]]
                + [
                    pltpu.roll(dual[part, k * 8 : k * 8 + 8, :], LANES - 32 * m, 1)
                    for m in range(1, 4)
                ]
                for part in range(2)
            ),
            1,
        )
        turned = []
        for u in (u_re, u_im):
            value = u[0]
            for s in range(1, 4):
                value = jnp.where(block == s, pltpu.roll(u[s], 32 * s, 1), value)
            turned.append(value)
        if k:
            turned = turn(turned[0], turned[1], cos_z[k], sin_z[k], 1)
        v_re.append(turned[0])
        v_im.append(turned[1])
    v_re, v_im = dft4(v_re, v_im, 1)
    for q in range(4):
        zsend2[q * 8 : q * 8 + 8, 0:LANES] = v_re[q]
        zsend2[q * 8 : q * 8 + 8, LANES : 2 * LANES] = v_im[q]
    for i in range(1, groups_z):
        across(zsend2, zrecv2, sz2, rz2, i, False).start()
    zrecv2[mine, :] = zsend2[mine, :]
    tree_take(0)
    tree_send(1)
    for i in range(1, groups_z):
        across(zsend2, zrecv2, sz2, rz2, i, True).wait_recv()

    upper = zrecv2[...]
    lower = jnp.concatenate([-upper[:, LANES:], upper[:, :LANES]], axis=1)
    back = dot3(wyt_ref[...], jnp.concatenate([upper, lower], axis=0), NN)
    sbuf2[...] = jnp.concatenate(
        [
            back[:, part * LANES : (part + 1) * LANES].reshape(groups_y, 1, YL, LANES)
            for part in range(2)
        ],
        axis=1,
    ).reshape(groups_y * 2 * YL, LANES)
    each_far(second)
    own_rows = pltpu.make_async_copy(rows(sbuf2, gy, 2 * YL), rows(lines_out, gy, 2 * YL), out_sem.at[0])
    own_rows.start()

    def outer_step(step, carry):
        shift = lax.rem(NK - step * 32, NK)
        slope_re = pltpu.roll(hslt[0], shift, 1)
        slope_im = pltpu.roll(hslt[1], shift, 1)
        for j in range(32):
            k = step * 32 + j
            s_re = jnp.broadcast_to(slope_re[:, j : j + 1], (C, C))
            s_im = jnp.broadcast_to(slope_im[:, j : j + 1], (C, C))
            i_re = hin[0, pl.ds(k, 1), 0:C]
            i_im = hin[1, pl.ds(k, 1), 0:C]
            spectral[0, k] = s_re * i_re + s_im * i_im
            spectral[1, k] = s_im * i_re - s_re * i_im
        return carry

    lax.fori_loop(0, 4, outer_step, 0)
    tree_take(1)
    if len(phases) > 2:
        tree_send(2)
    hid[0] = dot3(plain, outside(0), NN)
    hid[5] = dot3(plain, outside(1), NN)
    for z in range(ZL):
        total = plane(sten, z * 256, 256) + coef_col[3] * hid[z] + coef_col[4] * hid[z + 2]
        put_plane(sten, z * 256, total)
    coef_small = dot3((iota((C, C), 0) == iota((C, C), 1)).astype(F32), coef, NT)
    before_y, after_y = outside(2), outside(3)
    edges = jnp.concatenate(
        [side[z * C : (z + 1) * C] for side in (before_y, after_y) for z in range(ZL)], axis=1
    )
    edge_hidden = dot3(mix, edges, TN)
    for z in range(ZL):
        for side, y in enumerate((0, YL - 1)):
            at = pl.ds(z * 256 + y, C, stride=YL)
            for half in range(2):
                column = (side * ZL + z) * NX + half * LANES
                sten[half, at, :] = (
                    sten[half, at, :]
                    + coef_small[:, 1 + side : 2 + side]
                    * edge_hidden[:, column : column + LANES]
                )
    if len(phases) > 2:
        tree_take(2)

    each(second_in, "wait_recv")
    own_rows.wait()
    each(first, "wait_send")
    each(second, "wait_send")
    for copy, sends, _ in halos:
        pl.when(sends)(copy.wait_send)
    for i in range(1, groups_z):
        across(zsend, zrecv, sz, rz, i, False).wait_send()
        across(zsend2, zrecv2, sz2, rz2, i, False).wait_send()
    for phase in range(len(phases)):
        for i in range(1, place(phase)[0]):
            piece(phase, i, False).wait_send()


def result_kernel(
    lines, sten, spectral, red, wx_ref,
    grad_input, grad_spectral, grad_mix, grad_coef,
    cells, field, mix_out, coef_out, out_sem,
):
    modes_x = wx_ref.shape[0] // 2
    out = pltpu.make_async_copy(spectral, grad_spectral, out_sem.at[0])
    out.start()
    mix_out[0:16, :] = red[:, 0:C]
    mix_out[16:32, :] = red[:, C : 2 * C]
    coef_out[...] = red[0:5, 2 * C : 3 * C]
    small = [
        pltpu.make_async_copy(mix_out, grad_mix, out_sem.at[1]),
        pltpu.make_async_copy(coef_out, grad_coef, out_sem.at[2]),
    ]
    for copy in small:
        copy.start()
    spread = jnp.concatenate(
        [
            jnp.concatenate(
                [lines[pl.ds(part * YL + y, modes_x, stride=2 * YL), :] for y in range(YL)], axis=1
            )
            for part in range(2)
        ],
        axis=0,
    )
    result = dot3(spread, wx_ref[...], TN)
    for y in range(YL):
        for half in range(2):
            cells[half, pl.ds(y, LANES, stride=YL), :] = result[
                y * LANES : (y + 1) * LANES, half * LANES : (half + 1) * LANES
            ]
    planes = []
    for z in range(ZL):
        total = plane(cells, z * 256, 256) + plane(sten, z * 256, 256)
        field[z] = total.reshape(C, YL, NX)
        planes.append(pltpu.make_async_copy(field.at[z], grad_input.at[:, z], out_sem.at[3 + z]))
        planes[-1].start()
    for copy in planes + small + [out]:
        copy.wait()


def per_device(input_field, pre_activation, cotangent, spectral_weights, mix_weights, coefficients):
    groups_y = lax.axis_size("gy")
    groups_z = lax.axis_size("gz")
    grid_y = YL * groups_y
    modes_x = groups_y
    cell_total = NX * grid_y * ZL * groups_z
    phases = ((0, groups_z), (1, 8), (8, 4)) if groups_y == 32 else ((0, groups_z), (1, 4))
    rows_y = groups_y * YL
    cos_x, sin_x = table(NX, modes_x)
    cos_y, sin_y = table(grid_y, 32)
    wx = np.concatenate([cos_x, -sin_x]).astype(np.float32)
    wy = np.concatenate([cos_y, sin_y]).astype(np.float32)
    cell = np.arange(LANES) // C
    tw = np.stack(
        [fn(2.0 * math.pi * k * cell / 16.0) for k in range(4) for fn in (np.cos, np.sin)]
    ).astype(np.float32)
    weights = spectral_weights.reshape(2, NK, C, C)
    vmem = pl.BlockSpec(memory_space=pltpu.VMEM)
    hbm = pl.BlockSpec(memory_space=pltpu.HBM)
    sds = jax.ShapeDtypeStruct
    dma = pltpu.SemaphoreType.DMA
    lines, sten, spectral, red = pl.pallas_call(
        functools.partial(exchange_kernel, groups_y, groups_z, phases, cell_total),
        name="exchange",
        out_shape=(
            pltpu.VMEM((2 * rows_y, LANES), F32),
            pltpu.VMEM((2, ZL * 256, LANES), F32),
            pltpu.VMEM((2, NK, C, C), F32),
            pltpu.VMEM((16, LANES), F32),
        ),
        in_specs=[hbm] * 10,
        out_specs=(vmem,) * 4,
        scratch_shapes=[
            pltpu.VMEM((C, C), F32),
            pltpu.VMEM((5, C), F32),
            pltpu.VMEM(wx.shape, F32),
            pltpu.VMEM(wy.shape, F32),
            pltpu.VMEM(wy.T.shape, F32),
            pltpu.VMEM(tw.shape, F32),
            pltpu.VMEM((C, ZL, YL, NX), F32),
            pltpu.VMEM((C, ZL, YL, NX), F32),
            pltpu.VMEM((C, ZL, YL, NX), F32),
            pltpu.VMEM((2, NK, C, C), F32),
            pltpu.VMEM((2, ZL * 256, LANES), F32),
            pltpu.VMEM((2, ZL * 256, LANES), F32),
            pltpu.VMEM((4 * rows_y, LANES), F32),
            pltpu.VMEM((4 * rows_y, LANES), F32),
            pltpu.VMEM((32, 4 * LANES), F32),
            pltpu.VMEM((32, 4 * LANES), F32),
            pltpu.VMEM((32, 2 * LANES), F32),
            pltpu.VMEM((32, 2 * LANES), F32),
            pltpu.VMEM((2 * rows_y, LANES), F32),
            pltpu.VMEM((2, 2, ZL * C, LANES), F32),
            pltpu.VMEM((2, 2, ZL * C, LANES), F32),
            pltpu.VMEM((2, 2, 256, LANES), F32),
            pltpu.VMEM((6, 256, NX), F32),
            pltpu.VMEM((5 * C, C), F32),
            pltpu.VMEM((2, 32, C, LANES), F32),
            pltpu.VMEM((2, NK, LANES), F32),
            pltpu.VMEM((2, NK, LANES), F32),
            pltpu.VMEM((2, C, NK), F32),
            pltpu.VMEM((2, 32, LANES), F32),
            pltpu.VMEM((len(phases), 16, LANES), F32),
            pltpu.VMEM((len(phases), 8, 16, LANES), F32),
            dma((10,)),
            dma((groups_y,)), dma((groups_y,)), dma((groups_y,)), dma((groups_y,)),
            dma((groups_z,)), dma((groups_z,)), dma((groups_z,)), dma((groups_z,)),
            dma((4,)), dma((4,)),
            dma((len(phases), 8)), dma((len(phases), 8)),
            dma((1,)),
        ],
        compiler_params=pltpu.CompilerParams(
            collective_id=0, has_side_effects=True, vmem_limit_bytes=40 << 20
        ),
    )(
        *(
            pltpu.with_memory_space_constraint(operand, pltpu.HBM)
            for operand in (
                input_field, pre_activation, cotangent, weights, mix_weights, coefficients,
                jnp.asarray(wx), jnp.asarray(wy), jnp.asarray(wy.T.copy()), jnp.asarray(tw),
            )
        )
    )
    grad_input, grad_spectral, grad_mix, grad_coef = pl.pallas_call(
        result_kernel,
        name="result",
        out_shape=(
            sds((C, ZL, YL, NX), F32),
            sds((2, NK, C, C), F32),
            sds((C, C), F32),
            sds((5, C), F32),
        ),
        in_specs=[vmem] * 5,
        out_specs=(hbm,) * 4,
        scratch_shapes=[
            pltpu.VMEM((2, ZL * 256, LANES), F32),
            pltpu.VMEM((ZL, C, YL, NX), F32),
            pltpu.VMEM((C, C), F32),
            pltpu.VMEM((5, C), F32),
            dma((3 + ZL,)),
        ],
        compiler_params=pltpu.CompilerParams(vmem_limit_bytes=24 << 20),
    )(lines, sten, spectral, red, jnp.asarray(wx))
    return (grad_input, grad_spectral.reshape(spectral_weights.shape), grad_mix, grad_coef)


def solution(mesh):
    in_specs = (
        P(None, "gz", "gy", None),
        P(None, "gz", "gy", None),
        P(None, "gz", "gy", None),
        P(None, None, "gz", "gy", None, None),
        P(),
        P(),
    )
    out_specs = (P(None, "gz", "gy", None), P(None, None, "gz", "gy", None, None), P(), P())
    return jax.shard_map(
        per_device, mesh=mesh, in_specs=in_specs, out_specs=out_specs, check_vma=False
    )
```

```python
import functools
import math

import jax
import jax.numpy as jnp
import numpy as np
from jax import lax
from jax.experimental import pallas as pl
from jax.experimental.pallas import tpu as pltpu
from jax.sharding import PartitionSpec as P

F32 = jnp.float32
BF16 = jnp.bfloat16
MESH = pl.DeviceIdType.MESH
C = 32
ZL = 4
YL = 8
NX = 256
LANES = 128
NK = 128


def mode_numbers(number):
    positions = np.arange(number)
    return np.where(positions < number // 2, positions, positions - number)


def table(cells, modes):
    product = np.remainder(np.outer(mode_numbers(modes), np.arange(cells)), cells)
    angles = product * (2.0 * math.pi / cells)
    return np.cos(angles), np.sin(angles)


def split(a):
    high = a.astype(BF16)
    return high, (a - high.astype(F32)).astype(BF16)


def dot1(a, b, dims):
    return lax.dot_general(a, b, (dims, ((), ())), preferred_element_type=F32)


def dot3(a, b, dims):
    a_high, a_low = a if isinstance(a, tuple) else split(a)
    b_high, b_low = b if isinstance(b, tuple) else split(b)
    return dot1(a_high, b_low, dims) + dot1(a_low, b_high, dims) + dot1(a_high, b_high, dims)


NN = ((1,), (0,))
NT = ((1,), (1,))
TN = ((0,), (0,))


def gelu_slope(values):
    normal_cdf = 0.5 * (1.0 + lax.erf(values * 0.7071067811865476))
    return normal_cdf + values * jnp.exp(-0.5 * values * values) * 0.3989422804014327


def dft4(re, im, sign):
    ar, ai = re[0] + re[2], im[0] + im[2]
    br, bi = re[0] - re[2], im[0] - im[2]
    cr, ci = re[1] + re[3], im[1] + im[3]
    dr, di = re[1] - re[3], im[1] - im[3]
    if sign < 0:
        return [ar + cr, br + di, ar - cr, br - di], [ai + ci, bi - dr, ai - ci, bi + dr]
    return [ar + cr, br - di, ar - cr, br + di], [ai + ci, bi + dr, ai - ci, bi - dr]


def turn(re, im, cos, sin, sign):
    if sign < 0:
        return re * cos + im * sin, im * cos - re * sin
    return re * cos - im * sin, im * cos + re * sin


def plane(ref, start, size):
    return jnp.concatenate([ref[half, pl.ds(start, size), :] for half in range(2)], axis=1)


def put_plane(ref, start, value):
    for half in range(2):
        ref[half, pl.ds(start, value.shape[0]), :] = value[:, half * LANES : (half + 1) * LANES]


def offsets(groups_y):
    sizes = (4, 2, 4) if groups_y == 32 else (4,)
    result = []
    for i in range(1, groups_y):
        moves, rest = [], i
        for size in sizes:
            moves.append((size, rest % size))
            rest //= size
        hops = sum(min(m, n - m) * (2 if n == 2 else 1) for n, m in moves)
        result.append((-hops, tuple(moves)))
    return [moves for _, moves in sorted(result)]


def iota(shape, axis):
    return lax.broadcasted_iota(jnp.int32, shape, axis)


def exchange_kernel(
    groups_y, groups_z, phases, cell_total,
    inp_hbm, pre_hbm, cot_hbm, wts_hbm, mix_hbm, coef_hbm, wx_hbm, wy_hbm, wyt_hbm, tw_hbm,
    lines_out, sten, spectral, red_sum,
    mix_ref, coef_ref, wx_ref, wy_ref, wyt_ref, tw_ref, inp4, pre4, cot4, wts, inp2, slo2, sbuf, rbuf, zsend, zrecv, zsend2, zrecv2, sbuf2,
    hy_send, hy_recv, hz_recv, hid, inner, packed, hin, hsl, hslt, dual, red_send, red_recv,
    load_sem, s1, r1, s2, r2, sz, rz, sz2, rz2, hs_sem, hr_sem, sr, rr, out_sem,
):
    gz = lax.axis_index("gz")
    gy = lax.axis_index("gy")
    modes_x = wx_ref.shape[0] // 2

    def load(i, src, dst):
        return pltpu.make_async_copy(src, dst, load_sem.at[i])

    barrier = pltpu.get_barrier_semaphore()

    def partner(i):
        if isinstance(i, tuple):
            digits, stride, peer = gy, 1, 0
            for size, move in i:
                peer = peer + lax.rem(lax.rem(digits, size) + move, size) * stride
                digits, stride = digits // size, stride * size
            return peer
        return lax.rem(gy + i, groups_y)

    for i in offsets(groups_y):
        pl.semaphore_signal(barrier, inc=1, device_id=(gz, partner(i)), device_id_type=MESH)
    for i in range(1, groups_z):
        peer = lax.rem(gz + i, groups_z)
        pl.semaphore_signal(barrier, inc=1, device_id=(peer, gy), device_id_type=MESH)
    loads = [
        load(0, inp_hbm, inp4),
        load(6, wx_hbm, wx_ref),
        load(1, pre_hbm, pre4),
        load(2, cot_hbm, cot4),
    ]
    small = [
        load(4, mix_hbm, mix_ref),
        load(5, coef_hbm, coef_ref),
        load(7, wy_hbm, wy_ref),
        load(8, wyt_hbm, wyt_ref),
        load(9, tw_hbm, tw_ref),
    ]
    for copy in loads + small:
        copy.start()
    loads[1].wait()

    wx = split(wx_ref[...])

    def along_x(source, field):
        cells = jnp.concatenate(
            [
                jnp.concatenate(
                    [source[half, pl.ds(y, LANES, stride=YL), :] for half in range(2)], axis=1
                )
                for y in range(YL)
            ],
            axis=0,
        )
        result = dot3(wx, cells, NT)
        for y in range(YL):
            for part in range(2):
                sbuf[pl.ds((2 * field + part) * YL + y, modes_x, stride=4 * YL), :] = (
                    result[part * modes_x : (part + 1) * modes_x, y * LANES : (y + 1) * LANES]
                )

    loads[0].wait()
    for z in range(ZL):
        put_plane(inp2, z * 256, inp4[:, z].reshape(256, NX))
    along_x(inp2, 0)
    loads[2].wait()
    loads[3].wait()
    load(3, wts_hbm, wts).start()

    def slope_step(step, carry):
        z = step // 4
        c = lax.rem(step, 4) * 8
        pre = pre4[pl.ds(c, 8), z].reshape(64, NX)
        cot = cot4[pl.ds(c, 8), z].reshape(64, NX)
        put_plane(slo2, pl.multiple_of(step * 64, 64), cot * gelu_slope(pre))
        return carry

    lax.fori_loop(0, 16, slope_step, 0)
    along_x(slo2, 1)
    for z in range(ZL):
        for side, y in enumerate((YL - 1, 0)):
            for half in range(2):
                hy_send[side, half, pl.ds(z * C, C), :] = slo2[
                    half, pl.ds(z * 256 + y, C, stride=YL), :
                ]

    pl.semaphore_wait(barrier, groups_y - 1 + groups_z - 1)

    def rows(ref, index, size=YL):
        return ref.at[pl.ds(pl.multiple_of(index * size, size), size), :]

    def first(i):
        peer = partner(i)
        return pltpu.make_async_remote_copy(
            rows(sbuf, peer, 4 * YL), rows(rbuf, gy, 4 * YL), s1.at[peer], r1.at[gy],
            device_id=(gz, peer), device_id_type=MESH,
        )

    def first_in(i):
        peer = lax.rem(gy + i, groups_y)
        return pltpu.make_async_remote_copy(
            rows(sbuf, peer, 4 * YL), rows(rbuf, peer, 4 * YL), s1.at[peer], r1.at[peer],
            device_id=(gz, peer), device_id_type=MESH,
        )

    def second(i):
        peer = partner(i)
        return pltpu.make_async_remote_copy(
            rows(sbuf2, peer, 2 * YL), rows(lines_out, gy, 2 * YL), s2.at[peer], r2.at[gy],
            device_id=(gz, peer), device_id_type=MESH,
        )

    def second_in(i):
        peer = lax.rem(gy + i, groups_y)
        return pltpu.make_async_remote_copy(
            rows(sbuf2, peer, 2 * YL), rows(lines_out, peer, 2 * YL), s2.at[peer], r2.at[peer],
            device_id=(gz, peer), device_id_type=MESH,
        )

    def across(source, target, send, recv, i, inward):
        peer = lax.rem(gz + i, groups_z)
        slot = peer if inward else gz
        return pltpu.make_async_remote_copy(
            rows(source, peer), rows(target, slot), send.at[peer], recv.at[slot],
            device_id=(peer, gy), device_id_type=MESH,
        )

    def each_far(make):
        for i in offsets(groups_y):
            make(i).start()

    def each(make, action):
        def body(i, carry):
            getattr(make(i), action)()
            return carry

        lax.fori_loop(1, groups_y, body, 0)

    each_far(first)
    own_lines = pl.ds(pl.multiple_of(gy * 4 * YL, 4 * YL), 4 * YL)
    rbuf[own_lines, :] = sbuf[own_lines, :]

    next_z, prev_z = lax.rem(gz + 1, groups_z), lax.rem(gz + groups_z - 1, groups_z)
    next_y, prev_y = lax.rem(gy + 1, groups_y), lax.rem(gy + groups_y - 1, groups_y)
    halos = []
    for i, (source, target, device, sends, takes) in enumerate(
        (
            (slo2.at[:, pl.ds(3 * 256, 256), :], hz_recv.at[0], (next_z, gy),
             gz < groups_z - 1, gz > 0),
            (slo2.at[:, pl.ds(0, 256), :], hz_recv.at[1], (prev_z, gy),
             gz > 0, gz < groups_z - 1),
            (hy_send.at[0], hy_recv.at[0], (gz, next_y), gy < groups_y - 1, gy > 0),
            (hy_send.at[1], hy_recv.at[1], (gz, prev_y), gy > 0, gy < groups_y - 1),
        )
    ):
        copy = pltpu.make_async_remote_copy(
            source, target, hs_sem.at[i], hr_sem.at[i], device_id=device, device_id_type=MESH
        )
        halos.append((copy, sends, takes))
        pl.when(sends)(copy.start)

        @pl.when(jnp.logical_not(takes))
        def _():
            target[...] = jnp.zeros(target.shape, F32)

    for copy in small:
        copy.wait()
    mix = mix_ref[...]
    coef = coef_ref[...]
    expand = (lax.shift_right_logical(iota((256, C), 0), 3) == iota((256, C), 1)).astype(F32)
    gather = (lax.shift_right_logical(iota((C, 256), 1), 3) == iota((C, 256), 0)).astype(F32)
    row_y = lax.bitwise_and(iota((256, 256), 0), 7)
    col_y = lax.bitwise_and(iota((256, 256), 1), 7)

    def outside(which):
        if which < 2:
            return plane(hz_recv.at[which], 0, 256)
        return plane(hy_recv.at[which - 2], 0, ZL * C)

    def gram_of(left, z):
        return dot3(left, split(plane(inp2, z * 256, 256)), NT)

    same = row_y == col_y
    coef_rows = dot3(expand, coef, NT)
    coef_col = [coef_rows[:, j : j + 1] for j in range(5)]
    full = dot3(dot3(expand, mix, NT), expand, NT)
    weight = jnp.concatenate(
        [
            full
            * (
                jnp.where(same, coef_col[0], 0.0)
                + jnp.where(row_y == col_y + 1, coef_col[1], 0.0)
                + jnp.where(row_y == col_y - 1, coef_col[2], 0.0)
            ),
            jnp.where(same, full, 0.0),
        ],
        axis=0,
    )
    weight = split(weight)
    plain = (weight[0][256:512], weight[1][256:512])
    for z in range(ZL):
        both = dot3(weight, plane(slo2, z * 256, 256), NN)
        put_plane(sten, z * 256, both[0:256])
        hid[z + 1] = both[256:512]
    own = [split(plane(slo2, z * 256, 256)) for z in range(ZL)]
    grams = []
    for shift in (0, -1, 1):
        total = None
        for z in range(ZL):
            if 0 <= z + shift < ZL:
                term = gram_of(own[z + shift], z)
                total = term if total is None else total + term
        grams.append(total)
    pieces = jnp.concatenate(
        [
            jnp.where(same, grams[0], 0.0),
            jnp.where(col_y == row_y + 1, grams[0], 0.0),
            jnp.where(col_y == row_y - 1, grams[0], 0.0),
            jnp.where(same, grams[1], 0.0),
            jnp.where(same, grams[2], 0.0),
        ],
        axis=1,
    )
    summed = dot3(gather, pieces, NN)
    sums = [summed[:, j * 256 : (j + 1) * 256] for j in range(5)]
    inner[...] = dot3(jnp.concatenate(sums, axis=0), expand, NN)

    def along(ref, starts, stride):
        return jnp.concatenate(
            [
                ref[half, pl.ds(start, C, stride=stride), :]
                for start in starts
                for half in range(2)
            ],
            axis=1,
        )

    def moments():
        planes_y = [z * 256 for z in range(ZL)]
        rows_z = [z * C for z in range(ZL)]
        lines_y = list(range(YL))
        last = (ZL - 1) * 256
        outer = {
            1: (along(hy_recv.at[0], rows_z, 1), along(inp2, planes_y, YL)),
            2: (
                along(hy_recv.at[1], rows_z, 1),
                along(inp2, [start + YL - 1 for start in planes_y], YL),
            ),
            3: (along(hz_recv.at[0], lines_y, YL), along(inp2, lines_y, YL)),
            4: (
                along(hz_recv.at[1], lines_y, YL),
                along(inp2, [last + y for y in lines_y], YL),
            ),
        }
        parts = [inner[j * C : (j + 1) * C, :] for j in range(5)]
        for j, (left, right) in outer.items():
            parts[j] = parts[j] + dot3(left, right, NT)
        local_mix = coef[0:1, :] * parts[0]
        for j in range(1, 5):
            local_mix = local_mix + coef[j : j + 1, :] * parts[j]
        red_send[0, 0:16, 0:C] = local_mix[0:16]
        red_send[0, 0:16, C : 2 * C] = local_mix[16:32]
        red_send[0, 0:16, 2 * C :] = jnp.zeros((16, 2 * C), F32)
        for j in range(5):
            red_send[0, j : j + 1, 2 * C : 3 * C] = jnp.sum(
                mix * parts[j], axis=0, keepdims=True
            )

    def place(phase):
        stride, size = phases[phase]
        if stride == 0:
            return size, gz
        return size, lax.rem(gy // stride, size)

    def piece(phase, i, inward):
        stride, _ = phases[phase]
        size, mine = place(phase)
        peer = lax.rem(mine + i, size)
        slot = peer if inward else mine
        device = (peer, gy) if stride == 0 else (gz, gy + (peer - mine) * stride)
        return pltpu.make_async_remote_copy(
            red_send.at[phase], red_recv.at[phase, slot], sr.at[phase, i], rr.at[phase, slot],
            device_id=device, device_id_type=MESH,
        )

    def tree_send(phase):
        size, mine = place(phase)
        for i in range(1, size):
            piece(phase, i, False).start()
        red_recv[phase, mine] = red_send[phase]

    def tree_take(phase):
        size, _ = place(phase)
        for i in range(1, size):
            piece(phase, i, True).wait_recv()
        total = red_recv[phase, 0]
        for j in range(1, size):
            total = total + red_recv[phase, j]
        if phase + 1 < len(phases):
            red_send[phase + 1] = total
        else:
            red_sum[...] = total * (1.0 / 1024.0)

    load(3, wts_hbm, wts).wait()

    def pack_step(group, carry):
        q, j = group // 8, lax.rem(group, 8)
        for part in range(2):
            for m in range(4):
                packed[part, group, :, m * C : (m + 1) * C] = wts[part, (q + 4 * m) * 8 + j]
        return carry

    lax.fori_loop(0, 32, pack_step, 0)

    each(first_in, "wait_recv")
    received = rbuf[...].reshape(groups_y, 4, YL, LANES)
    received = jnp.concatenate(
        [received[:, part].reshape(groups_y * YL, LANES) for part in range(4)], axis=1
    )
    turned = dot3(wy_ref[...], received, NN)
    cos_part, sin_part = turned[0:32], turned[32:64]
    for field in range(2):
        re = slice(2 * field * LANES, (2 * field + 1) * LANES)
        im = slice((2 * field + 1) * LANES, (2 * field + 2) * LANES)
        zsend[:, re] = cos_part[:, re] + sin_part[:, im]
        zsend[:, im] = cos_part[:, im] - sin_part[:, re]
    for i in range(1, groups_z):
        across(zsend, zrecv, sz, rz, i, False).start()
    mine = pl.ds(pl.multiple_of(gz * 8, 8), 8)
    zrecv[mine, :] = zsend[mine, :]
    for copy, _, takes in halos:
        pl.when(takes)(copy.wait_recv)
    moments()
    tree_send(0)
    for i in range(1, groups_z):
        across(zsend, zrecv, sz, rz, i, True).wait_recv()

    cos_z = [tw_ref[2 * k : 2 * k + 1, :] for k in range(4)]
    sin_z = [tw_ref[2 * k + 1 : 2 * k + 2, :] for k in range(4)]
    for field in range(2):
        base = 2 * field * LANES
        re = [zrecv[q * 8 : q * 8 + 8, base : base + LANES] for q in range(4)]
        im = [zrecv[q * 8 : q * 8 + 8, base + LANES : base + 2 * LANES] for q in range(4)]
        re, im = dft4(re, im, -1)
        for k in range(4):
            t_re, t_im = re[k], im[k]
            if k:
                t_re, t_im = turn(t_re, t_im, cos_z[k], sin_z[k], -1)
            f_re, f_im = dft4(
                [t_re] + [pltpu.roll(t_re, LANES - 32 * s, 1) for s in range(1, 4)],
                [t_im] + [pltpu.roll(t_im, LANES - 32 * s, 1) for s in range(1, 4)],
                -1,
            )
            for m in range(4):
                at = pl.ds((k + 4 * m) * 8, 8)
                if field == 0:
                    hin[0, at, :] = f_re[m]
                    hin[1, at, :] = f_im[m]
                else:
                    hsl[0, at, :] = f_re[m] * (1.0 / cell_total)
                    hsl[1, at, :] = f_im[m] * (1.0 / cell_total)
    for part in range(2):
        hslt[part] = hsl[part].T[0:C, :]

    lane = iota((C, LANES), 1)

    def dual_step(q, carry):
        shift = lax.rem(NK - q * 8, NK)
        slope_re = pltpu.roll(hslt[0], shift, 1)
        slope_im = pltpu.roll(hslt[1], shift, 1)
        for j in range(8):
            group = q * 8 + j
            spread = lax.bitwise_and(lane, 96) + j
            s_re = jnp.take_along_axis(slope_re, spread, axis=1)
            s_im = jnp.take_along_axis(slope_im, spread, axis=1)
            w_re, w_im = packed[0, group], packed[1, group]
            dual[0, pl.ds(group, 1), :] = jnp.sum(w_re * s_re + w_im * s_im, axis=0, keepdims=True)
            dual[1, pl.ds(group, 1), :] = jnp.sum(w_re * s_im - w_im * s_re, axis=0, keepdims=True)
        return carry

    lax.fori_loop(0, 4, dual_step, 0)

    block = lax.shift_right_logical(iota((8, LANES), 1), 5)
    v_re, v_im = [], []
    for k in range(4):
        u_re, u_im = dft4(
            *(
                [dual[part, k * 8 : k * 8 + 8, :]]
                + [
                    pltpu.roll(dual[part, k * 8 : k * 8 + 8, :], LANES - 32 * m, 1)
                    for m in range(1, 4)
                ]
                for part in range(2)
            ),
            1,
        )
        turned = []
        for u in (u_re, u_im):
            value = u[0]
            for s in range(1, 4):
                value = jnp.where(block == s, pltpu.roll(u[s], 32 * s, 1), value)
            turned.append(value)
        if k:
            turned = turn(turned[0], turned[1], cos_z[k], sin_z[k], 1)
        v_re.append(turned[0])
        v_im.append(turned[1])
    v_re, v_im = dft4(v_re, v_im, 1)
    for q in range(4):
        zsend2[q * 8 : q * 8 + 8, 0:LANES] = v_re[q]
        zsend2[q * 8 : q * 8 + 8, LANES : 2 * LANES] = v_im[q]
    for i in range(1, groups_z):
        across(zsend2, zrecv2, sz2, rz2, i, False).start()
    zrecv2[mine, :] = zsend2[mine, :]
    tree_take(0)
    tree_send(1)
    for i in range(1, groups_z):
        across(zsend2, zrecv2, sz2, rz2, i, True).wait_recv()

    upper = zrecv2[...]
    lower = jnp.concatenate([-upper[:, LANES:], upper[:, :LANES]], axis=1)
    back = dot3(wyt_ref[...], jnp.concatenate([upper, lower], axis=0), NN)
    sbuf2[...] = jnp.concatenate(
        [
            back[:, part * LANES : (part + 1) * LANES].reshape(groups_y, 1, YL, LANES)
            for part in range(2)
        ],
        axis=1,
    ).reshape(groups_y * 2 * YL, LANES)
    each_far(second)
    tree_take(1)
    if len(phases) > 2:
        tree_send(2)
    own_rows = pltpu.make_async_copy(rows(sbuf2, gy, 2 * YL), rows(lines_out, gy, 2 * YL), out_sem.at[0])
    own_rows.start()

    def outer_step(step, carry):
        shift = lax.rem(NK - step * 32, NK)
        slope_re = pltpu.roll(hslt[0], shift, 1)
        slope_im = pltpu.roll(hslt[1], shift, 1)
        for j in range(32):
            k = step * 32 + j
            s_re = jnp.broadcast_to(slope_re[:, j : j + 1], (C, C))
            s_im = jnp.broadcast_to(slope_im[:, j : j + 1], (C, C))
            i_re = hin[0, pl.ds(k, 1), 0:C]
            i_im = hin[1, pl.ds(k, 1), 0:C]
            spectral[0, k] = s_re * i_re + s_im * i_im
            spectral[1, k] = s_im * i_re - s_re * i_im
        return carry

    lax.fori_loop(0, 4, outer_step, 0)
    hid[0] = dot3(plain, outside(0), NN)
    hid[5] = dot3(plain, outside(1), NN)
    for z in range(ZL):
        total = plane(sten, z * 256, 256) + coef_col[3] * hid[z] + coef_col[4] * hid[z + 2]
        put_plane(sten, z * 256, total)
    coef_small = dot3((iota((C, C), 0) == iota((C, C), 1)).astype(F32), coef, NT)
    before_y, after_y = outside(2), outside(3)
    edges = jnp.concatenate(
        [side[z * C : (z + 1) * C] for side in (before_y, after_y) for z in range(ZL)], axis=1
    )
    edge_hidden = dot3(mix, edges, TN)
    for z in range(ZL):
        for side, y in enumerate((0, YL - 1)):
            at = pl.ds(z * 256 + y, C, stride=YL)
            for half in range(2):
                column = (side * ZL + z) * NX + half * LANES
                sten[half, at, :] = (
                    sten[half, at, :]
                    + coef_small[:, 1 + side : 2 + side]
                    * edge_hidden[:, column : column + LANES]
                )
    if len(phases) > 2:
        tree_take(2)

    each(second_in, "wait_recv")
    own_rows.wait()
    each(first, "wait_send")
    each(second, "wait_send")
    for copy, sends, _ in halos:
        pl.when(sends)(copy.wait_send)
    for i in range(1, groups_z):
        across(zsend, zrecv, sz, rz, i, False).wait_send()
        across(zsend2, zrecv2, sz2, rz2, i, False).wait_send()
    for phase in range(len(phases)):
        for i in range(1, place(phase)[0]):
            piece(phase, i, False).wait_send()


def result_kernel(
    lines, sten, spectral, red, wx_ref,
    grad_input, grad_spectral, grad_mix, grad_coef,
    cells, field, mix_out, coef_out, out_sem,
):
    modes_x = wx_ref.shape[0] // 2
    out = pltpu.make_async_copy(spectral, grad_spectral, out_sem.at[0])
    out.start()
    mix_out[0:16, :] = red[:, 0:C]
    mix_out[16:32, :] = red[:, C : 2 * C]
    coef_out[...] = red[0:5, 2 * C : 3 * C]
    small = [
        pltpu.make_async_copy(mix_out, grad_mix, out_sem.at[1]),
        pltpu.make_async_copy(coef_out, grad_coef, out_sem.at[2]),
    ]
    for copy in small:
        copy.start()
    spread = jnp.concatenate(
        [
            jnp.concatenate(
                [lines[pl.ds(part * YL + y, modes_x, stride=2 * YL), :] for y in range(YL)], axis=1
            )
            for part in range(2)
        ],
        axis=0,
    )
    result = dot3(spread, wx_ref[...], TN)
    for y in range(YL):
        for half in range(2):
            cells[half, pl.ds(y, LANES, stride=YL), :] = result[
                y * LANES : (y + 1) * LANES, half * LANES : (half + 1) * LANES
            ]
    planes = []
    for z in range(ZL):
        total = plane(cells, z * 256, 256) + plane(sten, z * 256, 256)
        field[z] = total.reshape(C, YL, NX)
        planes.append(pltpu.make_async_copy(field.at[z], grad_input.at[:, z], out_sem.at[3 + z]))
        planes[-1].start()
    for copy in planes + small + [out]:
        copy.wait()


def per_device(input_field, pre_activation, cotangent, spectral_weights, mix_weights, coefficients):
    groups_y = lax.axis_size("gy")
    groups_z = lax.axis_size("gz")
    grid_y = YL * groups_y
    modes_x = groups_y
    cell_total = NX * grid_y * ZL * groups_z
    phases = ((0, groups_z), (1, 8), (8, 4)) if groups_y == 32 else ((0, groups_z), (1, 4))
    rows_y = groups_y * YL
    cos_x, sin_x = table(NX, modes_x)
    cos_y, sin_y = table(grid_y, 32)
    wx = np.concatenate([cos_x, -sin_x]).astype(np.float32)
    wy = np.concatenate([cos_y, sin_y]).astype(np.float32)
    cell = np.arange(LANES) // C
    tw = np.stack(
        [fn(2.0 * math.pi * k * cell / 16.0) for k in range(4) for fn in (np.cos, np.sin)]
    ).astype(np.float32)
    weights = spectral_weights.reshape(2, NK, C, C)
    vmem = pl.BlockSpec(memory_space=pltpu.VMEM)
    hbm = pl.BlockSpec(memory_space=pltpu.HBM)
    sds = jax.ShapeDtypeStruct
    dma = pltpu.SemaphoreType.DMA
    lines, sten, spectral, red = pl.pallas_call(
        functools.partial(exchange_kernel, groups_y, groups_z, phases, cell_total),
        name="exchange",
        out_shape=(
            pltpu.VMEM((2 * rows_y, LANES), F32),
            pltpu.VMEM((2, ZL * 256, LANES), F32),
            pltpu.VMEM((2, NK, C, C), F32),
            pltpu.VMEM((16, LANES), F32),
        ),
        in_specs=[hbm] * 10,
        out_specs=(vmem,) * 4,
        scratch_shapes=[
            pltpu.VMEM((C, C), F32),
            pltpu.VMEM((5, C), F32),
            pltpu.VMEM(wx.shape, F32),
            pltpu.VMEM(wy.shape, F32),
            pltpu.VMEM(wy.T.shape, F32),
            pltpu.VMEM(tw.shape, F32),
            pltpu.VMEM((C, ZL, YL, NX), F32),
            pltpu.VMEM((C, ZL, YL, NX), F32),
            pltpu.VMEM((C, ZL, YL, NX), F32),
            pltpu.VMEM((2, NK, C, C), F32),
            pltpu.VMEM((2, ZL * 256, LANES), F32),
            pltpu.VMEM((2, ZL * 256, LANES), F32),
            pltpu.VMEM((4 * rows_y, LANES), F32),
            pltpu.VMEM((4 * rows_y, LANES), F32),
            pltpu.VMEM((32, 4 * LANES), F32),
            pltpu.VMEM((32, 4 * LANES), F32),
            pltpu.VMEM((32, 2 * LANES), F32),
            pltpu.VMEM((32, 2 * LANES), F32),
            pltpu.VMEM((2 * rows_y, LANES), F32),
            pltpu.VMEM((2, 2, ZL * C, LANES), F32),
            pltpu.VMEM((2, 2, ZL * C, LANES), F32),
            pltpu.VMEM((2, 2, 256, LANES), F32),
            pltpu.VMEM((6, 256, NX), F32),
            pltpu.VMEM((5 * C, C), F32),
            pltpu.VMEM((2, 32, C, LANES), F32),
            pltpu.VMEM((2, NK, LANES), F32),
            pltpu.VMEM((2, NK, LANES), F32),
            pltpu.VMEM((2, C, NK), F32),
            pltpu.VMEM((2, 32, LANES), F32),
            pltpu.VMEM((len(phases), 16, LANES), F32),
            pltpu.VMEM((len(phases), 8, 16, LANES), F32),
            dma((10,)),
            dma((groups_y,)), dma((groups_y,)), dma((groups_y,)), dma((groups_y,)),
            dma((groups_z,)), dma((groups_z,)), dma((groups_z,)), dma((groups_z,)),
            dma((4,)), dma((4,)),
            dma((len(phases), 8)), dma((len(phases), 8)),
            dma((1,)),
        ],
        compiler_params=pltpu.CompilerParams(
            collective_id=0, has_side_effects=True, vmem_limit_bytes=40 << 20
        ),
    )(
        *(
            pltpu.with_memory_space_constraint(operand, pltpu.HBM)
            for operand in (
                input_field, pre_activation, cotangent, weights, mix_weights, coefficients,
                jnp.asarray(wx), jnp.asarray(wy), jnp.asarray(wy.T.copy()), jnp.asarray(tw),
            )
        )
    )
    grad_input, grad_spectral, grad_mix, grad_coef = pl.pallas_call(
        result_kernel,
        name="result",
        out_shape=(
            sds((C, ZL, YL, NX), F32),
            sds((2, NK, C, C), F32),
            sds((C, C), F32),
            sds((5, C), F32),
        ),
        in_specs=[vmem] * 5,
        out_specs=(hbm,) * 4,
        scratch_shapes=[
            pltpu.VMEM((2, ZL * 256, LANES), F32),
            pltpu.VMEM((ZL, C, YL, NX), F32),
            pltpu.VMEM((C, C), F32),
            pltpu.VMEM((5, C), F32),
            dma((3 + ZL,)),
        ],
        compiler_params=pltpu.CompilerParams(vmem_limit_bytes=24 << 20),
    )(lines, sten, spectral, red, jnp.asarray(wx))
    return (grad_input, grad_spectral.reshape(spectral_weights.shape), grad_mix, grad_coef)


def solution(mesh):
    in_specs = (
        P(None, "gz", "gy", None),
        P(None, "gz", "gy", None),
        P(None, "gz", "gy", None),
        P(None, None, "gz", "gy", None, None),
        P(),
        P(),
    )
    out_specs = (P(None, "gz", "gy", None), P(None, None, "gz", "gy", None, None), P(), P())
    return jax.shard_map(
        per_device, mesh=mesh, in_specs=in_specs, out_specs=out_specs, check_vma=False
    )
```

```python
import functools
import math

import jax
import jax.numpy as jnp
import numpy as np
from jax import lax
from jax.experimental import pallas as pl
from jax.experimental.pallas import tpu as pltpu
from jax.sharding import PartitionSpec as P

F32 = jnp.float32
BF16 = jnp.bfloat16
MESH = pl.DeviceIdType.MESH
C = 32
ZL = 4
YL = 8
NX = 256
LANES = 128
NK = 128


def mode_numbers(number):
    positions = np.arange(number)
    return np.where(positions < number // 2, positions, positions - number)


def table(cells, modes):
    product = np.remainder(np.outer(mode_numbers(modes), np.arange(cells)), cells)
    angles = product * (2.0 * math.pi / cells)
    return np.cos(angles), np.sin(angles)


def split(a):
    high = a.astype(BF16)
    return high, (a - high.astype(F32)).astype(BF16)


def dot1(a, b, dims):
    return lax.dot_general(a, b, (dims, ((), ())), preferred_element_type=F32)


def dot3(a, b, dims):
    a_high, a_low = a if isinstance(a, tuple) else split(a)
    b_high, b_low = b if isinstance(b, tuple) else split(b)
    return dot1(a_high, b_low, dims) + dot1(a_low, b_high, dims) + dot1(a_high, b_high, dims)


NN = ((1,), (0,))
NT = ((1,), (1,))
TN = ((0,), (0,))


def gelu_slope(values):
    normal_cdf = 0.5 * (1.0 + lax.erf(values * 0.7071067811865476))
    return normal_cdf + values * jnp.exp(-0.5 * values * values) * 0.3989422804014327


def dft4(re, im, sign):
    ar, ai = re[0] + re[2], im[0] + im[2]
    br, bi = re[0] - re[2], im[0] - im[2]
    cr, ci = re[1] + re[3], im[1] + im[3]
    dr, di = re[1] - re[3], im[1] - im[3]
    if sign < 0:
        return [ar + cr, br + di, ar - cr, br - di], [ai + ci, bi - dr, ai - ci, bi + dr]
    return [ar + cr, br - di, ar - cr, br + di], [ai + ci, bi + dr, ai - ci, bi - dr]


def turn(re, im, cos, sin, sign):
    if sign < 0:
        return re * cos + im * sin, im * cos - re * sin
    return re * cos - im * sin, im * cos + re * sin


def plane(ref, start, size):
    return jnp.concatenate([ref[half, pl.ds(start, size), :] for half in range(2)], axis=1)


def put_plane(ref, start, value):
    for half in range(2):
        ref[half, pl.ds(start, value.shape[0]), :] = value[:, half * LANES : (half + 1) * LANES]


def offsets(groups_y):
    sizes = (4, 2, 4) if groups_y == 32 else (4,)
    result = []
    for i in range(1, groups_y):
        moves, rest = [], i
        for size in sizes:
            moves.append((size, rest % size))
            rest //= size
        hops = sum(min(m, n - m) * (2 if n == 2 else 1) for n, m in moves)
        result.append((-hops, tuple(moves)))
    return [moves for _, moves in sorted(result)]


def iota(shape, axis):
    return lax.broadcasted_iota(jnp.int32, shape, axis)


def exchange_kernel(
    groups_y, groups_z, phases, cell_total,
    inp_hbm, pre_hbm, cot_hbm, wts_hbm, mix_hbm, coef_hbm, wx_hbm, wy_hbm, wyt_hbm, tw_hbm,
    lines_out, sten, spectral, red_sum,
    mix_ref, coef_ref, wx_ref, wy_ref, wyt_ref, tw_ref, inp4, pre4, cot4, wts, inp2, slo2, sbuf, rbuf, zsend, zrecv, zsend2, zrecv2, sbuf2,
    hy_send, hy_recv, hz_recv, hid, inner, packed, hin, hsl, hslt, dual, red_send, red_recv,
    load_sem, s1, r1, s2, r2, sz, rz, sz2, rz2, hs_sem, hr_sem, sr, rr, out_sem,
):
    gz = lax.axis_index("gz")
    gy = lax.axis_index("gy")
    modes_x = wx_ref.shape[0] // 2

    def load(i, src, dst):
        return pltpu.make_async_copy(src, dst, load_sem.at[i])

    barrier = pltpu.get_barrier_semaphore()

    def partner(i):
        if isinstance(i, tuple):
            digits, stride, peer = gy, 1, 0
            for size, move in i:
                peer = peer + lax.rem(lax.rem(digits, size) + move, size) * stride
                digits, stride = digits // size, stride * size
            return peer
        return lax.rem(gy + i, groups_y)

    for i in offsets(groups_y):
        pl.semaphore_signal(barrier, inc=1, device_id=(gz, partner(i)), device_id_type=MESH)
    for i in range(1, groups_z):
        peer = lax.rem(gz + i, groups_z)
        pl.semaphore_signal(barrier, inc=1, device_id=(peer, gy), device_id_type=MESH)
    loads = [
        load(0, inp_hbm, inp4),
        load(6, wx_hbm, wx_ref),
        load(1, pre_hbm, pre4),
        load(2, cot_hbm, cot4),
    ]
    small = [
        load(4, mix_hbm, mix_ref),
        load(5, coef_hbm, coef_ref),
        load(7, wy_hbm, wy_ref),
        load(8, wyt_hbm, wyt_ref),
        load(9, tw_hbm, tw_ref),
    ]
    for copy in loads + small:
        copy.start()
    loads[1].wait()

    wx = split(wx_ref[...])

    def along_x(source, field):
        cells = jnp.concatenate(
            [
                jnp.concatenate(
                    [source[half, pl.ds(y, LANES, stride=YL), :] for half in range(2)], axis=1
                )
                for y in range(YL)
            ],
            axis=0,
        )
        result = dot3(wx, cells, NT)
        for y in range(YL):
            for part in range(2):
                sbuf[pl.ds((2 * field + part) * YL + y, modes_x, stride=4 * YL), :] = (
                    result[part * modes_x : (part + 1) * modes_x, y * LANES : (y + 1) * LANES]
                )

    loads[0].wait()
    for z in range(ZL):
        put_plane(inp2, z * 256, inp4[:, z].reshape(256, NX))
    along_x(inp2, 0)
    loads[2].wait()
    loads[3].wait()
    load(3, wts_hbm, wts).start()

    def slope_step(step, carry):
        z = step // 4
        c = lax.rem(step, 4) * 8
        pre = pre4[pl.ds(c, 8), z].reshape(64, NX)
        cot = cot4[pl.ds(c, 8), z].reshape(64, NX)
        put_plane(slo2, pl.multiple_of(step * 64, 64), cot * gelu_slope(pre))
        return carry

    lax.fori_loop(0, 16, slope_step, 0)
    along_x(slo2, 1)
    for z in range(ZL):
        for side, y in enumerate((YL - 1, 0)):
            for half in range(2):
                hy_send[side, half, pl.ds(z * C, C), :] = slo2[
                    half, pl.ds(z * 256 + y, C, stride=YL), :
                ]

    pl.semaphore_wait(barrier, groups_y - 1 + groups_z - 1)

    def rows(ref, index, size=YL):
        return ref.at[pl.ds(pl.multiple_of(index * size, size), size), :]

    def first(i):
        peer = partner(i)
        return pltpu.make_async_remote_copy(
            rows(sbuf, peer, 4 * YL), rows(rbuf, gy, 4 * YL), s1.at[peer], r1.at[gy],
            device_id=(gz, peer), device_id_type=MESH,
        )

    def first_in(i):
        peer = lax.rem(gy + i, groups_y)
        return pltpu.make_async_remote_copy(
            rows(sbuf, peer, 4 * YL), rows(rbuf, peer, 4 * YL), s1.at[peer], r1.at[peer],
            device_id=(gz, peer), device_id_type=MESH,
        )

    def second(i):
        peer = partner(i)
        return pltpu.make_async_remote_copy(
            rows(sbuf2, peer, 2 * YL), rows(lines_out, gy, 2 * YL), s2.at[peer], r2.at[gy],
            device_id=(gz, peer), device_id_type=MESH,
        )

    def second_in(i):
        peer = lax.rem(gy + i, groups_y)
        return pltpu.make_async_remote_copy(
            rows(sbuf2, peer, 2 * YL), rows(lines_out, peer, 2 * YL), s2.at[peer], r2.at[peer],
            device_id=(gz, peer), device_id_type=MESH,
        )

    def across(source, target, send, recv, i, inward):
        peer = lax.rem(gz + i, groups_z)
        slot = peer if inward else gz
        return pltpu.make_async_remote_copy(
            rows(source, peer), rows(target, slot), send.at[peer], recv.at[slot],
            device_id=(peer, gy), device_id_type=MESH,
        )

    def each_far(make):
        for i in offsets(groups_y):
            make(i).start()

    def each(make, action):
        def body(i, carry):
            getattr(make(i), action)()
            return carry

        lax.fori_loop(1, groups_y, body, 0)

    each_far(first)
    own_lines = pl.ds(pl.multiple_of(gy * 4 * YL, 4 * YL), 4 * YL)
    rbuf[own_lines, :] = sbuf[own_lines, :]

    next_z, prev_z = lax.rem(gz + 1, groups_z), lax.rem(gz + groups_z - 1, groups_z)
    next_y, prev_y = lax.rem(gy + 1, groups_y), lax.rem(gy + groups_y - 1, groups_y)
    halos = []
    for i, (source, target, device, sends, takes) in enumerate(
        (
            (slo2.at[:, pl.ds(3 * 256, 256), :], hz_recv.at[0], (next_z, gy),
             gz < groups_z - 1, gz > 0),
            (slo2.at[:, pl.ds(0, 256), :], hz_recv.at[1], (prev_z, gy),
             gz > 0, gz < groups_z - 1),
            (hy_send.at[0], hy_recv.at[0], (gz, next_y), gy < groups_y - 1, gy > 0),
            (hy_send.at[1], hy_recv.at[1], (gz, prev_y), gy > 0, gy < groups_y - 1),
        )
    ):
        copy = pltpu.make_async_remote_copy(
            source, target, hs_sem.at[i], hr_sem.at[i], device_id=device, device_id_type=MESH
        )
        halos.append((copy, sends, takes))
        pl.when(sends)(copy.start)

        @pl.when(jnp.logical_not(takes))
        def _():
            target[...] = jnp.zeros(target.shape, F32)

    for copy in small:
        copy.wait()
    mix = mix_ref[...]
    coef = coef_ref[...]
    expand = (lax.shift_right_logical(iota((256, C), 0), 3) == iota((256, C), 1)).astype(F32)
    gather = (lax.shift_right_logical(iota((C, 256), 1), 3) == iota((C, 256), 0)).astype(F32)
    row_y = lax.bitwise_and(iota((256, 256), 0), 7)
    col_y = lax.bitwise_and(iota((256, 256), 1), 7)

    def outside(which):
        if which < 2:
            return plane(hz_recv.at[which], 0, 256)
        return plane(hy_recv.at[which - 2], 0, ZL * C)

    def gram_of(left, z):
        return dot3(left, split(plane(inp2, z * 256, 256)), NT)

    same = row_y == col_y
    coef_rows = dot3(expand, coef, NT)
    coef_col = [coef_rows[:, j : j + 1] for j in range(5)]
    full = dot3(dot3(expand, mix, NT), expand, NT)
    weight = jnp.concatenate(
        [
            full
            * (
                jnp.where(same, coef_col[0], 0.0)
                + jnp.where(row_y == col_y + 1, coef_col[1], 0.0)
                + jnp.where(row_y == col_y - 1, coef_col[2], 0.0)
            ),
            jnp.where(same, full, 0.0),
        ],
        axis=0,
    )
    weight = split(weight)
    plain = (weight[0][256:512], weight[1][256:512])
    for z in range(ZL):
        both = dot3(weight, plane(slo2, z * 256, 256), NN)
        put_plane(sten, z * 256, both[0:256])
        hid[z + 1] = both[256:512]
    own = [split(plane(slo2, z * 256, 256)) for z in range(ZL)]
    grams = []
    for shift in (0, -1, 1):
        total = None
        for z in range(ZL):
            if 0 <= z + shift < ZL:
                term = gram_of(own[z + shift], z)
                total = term if total is None else total + term
        grams.append(total)
    pieces = jnp.concatenate(
        [
            jnp.where(same, grams[0], 0.0),
            jnp.where(col_y == row_y + 1, grams[0], 0.0),
            jnp.where(col_y == row_y - 1, grams[0], 0.0),
            jnp.where(same, grams[1], 0.0),
            jnp.where(same, grams[2], 0.0),
        ],
        axis=1,
    )
    summed = dot3(gather, pieces, NN)
    sums = [summed[:, j * 256 : (j + 1) * 256] for j in range(5)]
    inner[...] = dot3(jnp.concatenate(sums, axis=0), expand, NN)

    def along(ref, starts, stride):
        return jnp.concatenate(
            [
                ref[half, pl.ds(start, C, stride=stride), :]
                for start in starts
                for half in range(2)
            ],
            axis=1,
        )

    def moments():
        planes_y = [z * 256 for z in range(ZL)]
        rows_z = [z * C for z in range(ZL)]
        lines_y = list(range(YL))
        last = (ZL - 1) * 256
        outer = {
            1: (along(hy_recv.at[0], rows_z, 1), along(inp2, planes_y, YL)),
            2: (
                along(hy_recv.at[1], rows_z, 1),
                along(inp2, [start + YL - 1 for start in planes_y], YL),
            ),
            3: (along(hz_recv.at[0], lines_y, YL), along(inp2, lines_y, YL)),
            4: (
                along(hz_recv.at[1], lines_y, YL),
                along(inp2, [last + y for y in lines_y], YL),
            ),
        }
        parts = [inner[j * C : (j + 1) * C, :] for j in range(5)]
        for j, (left, right) in outer.items():
            parts[j] = parts[j] + dot3(left, right, NT)
        local_mix = coef[0:1, :] * parts[0]
        for j in range(1, 5):
            local_mix = local_mix + coef[j : j + 1, :] * parts[j]
        red_send[0, 0:16, 0:C] = local_mix[0:16]
        red_send[0, 0:16, C : 2 * C] = local_mix[16:32]
        red_send[0, 0:16, 2 * C :] = jnp.zeros((16, 2 * C), F32)
        for j in range(5):
            red_send[0, j : j + 1, 2 * C : 3 * C] = jnp.sum(
                mix * parts[j], axis=0, keepdims=True
            )

    def place(phase):
        stride, size = phases[phase]
        if stride == 0:
            return size, gz
        return size, lax.rem(gy // stride, size)

    def piece(phase, i, inward):
        stride, _ = phases[phase]
        size, mine = place(phase)
        peer = lax.rem(mine + i, size)
        slot = peer if inward else mine
        device = (peer, gy) if stride == 0 else (gz, gy + (peer - mine) * stride)
        return pltpu.make_async_remote_copy(
            red_send.at[phase], red_recv.at[phase, slot], sr.at[phase, i], rr.at[phase, slot],
            device_id=device, device_id_type=MESH,
        )

    def tree_send(phase):
        size, mine = place(phase)
        for i in range(1, size):
            piece(phase, i, False).start()
        red_recv[phase, mine] = red_send[phase]

    def tree_take(phase):
        size, _ = place(phase)
        for i in range(1, size):
            piece(phase, i, True).wait_recv()
        total = red_recv[phase, 0]
        for j in range(1, size):
            total = total + red_recv[phase, j]
        if phase + 1 < len(phases):
            red_send[phase + 1] = total
        else:
            red_sum[...] = total * (1.0 / 1024.0)

    load(3, wts_hbm, wts).wait()

    def pack_step(group, carry):
        q, j = group // 8, lax.rem(group, 8)
        for part in range(2):
            for m in range(4):
                packed[part, group, :, m * C : (m + 1) * C] = wts[part, (q + 4 * m) * 8 + j]
        return carry

    lax.fori_loop(0, 32, pack_step, 0)

    each(first_in, "wait_recv")
    received = rbuf[...].reshape(groups_y, 4, YL, LANES)
    received = jnp.concatenate(
        [received[:, part].reshape(groups_y * YL, LANES) for part in range(4)], axis=1
    )
    turned = dot3(wy_ref[...], received, NN)
    cos_part, sin_part = turned[0:32], turned[32:64]
    for field in range(2):
        re = slice(2 * field * LANES, (2 * field + 1) * LANES)
        im = slice((2 * field + 1) * LANES, (2 * field + 2) * LANES)
        zsend[:, re] = cos_part[:, re] + sin_part[:, im]
        zsend[:, im] = cos_part[:, im] - sin_part[:, re]
    for i in range(1, groups_z):
        across(zsend, zrecv, sz, rz, i, False).start()
    mine = pl.ds(pl.multiple_of(gz * 8, 8), 8)
    zrecv[mine, :] = zsend[mine, :]
    for copy, _, takes in halos:
        pl.when(takes)(copy.wait_recv)
    moments()
    tree_send(0)
    for i in range(1, groups_z):
        across(zsend, zrecv, sz, rz, i, True).wait_recv()

    cos_z = [tw_ref[2 * k : 2 * k + 1, :] for k in range(4)]
    sin_z = [tw_ref[2 * k + 1 : 2 * k + 2, :] for k in range(4)]
    for field in range(2):
        base = 2 * field * LANES
        re = [zrecv[q * 8 : q * 8 + 8, base : base + LANES] for q in range(4)]
        im = [zrecv[q * 8 : q * 8 + 8, base + LANES : base + 2 * LANES] for q in range(4)]
        re, im = dft4(re, im, -1)
        for k in range(4):
            t_re, t_im = re[k], im[k]
            if k:
                t_re, t_im = turn(t_re, t_im, cos_z[k], sin_z[k], -1)
            f_re, f_im = dft4(
                [t_re] + [pltpu.roll(t_re, LANES - 32 * s, 1) for s in range(1, 4)],
                [t_im] + [pltpu.roll(t_im, LANES - 32 * s, 1) for s in range(1, 4)],
                -1,
            )
            for m in range(4):
                at = pl.ds((k + 4 * m) * 8, 8)
                if field == 0:
                    hin[0, at, :] = f_re[m]
                    hin[1, at, :] = f_im[m]
                else:
                    hsl[0, at, :] = f_re[m] * (1.0 / cell_total)
                    hsl[1, at, :] = f_im[m] * (1.0 / cell_total)
    for part in range(2):
        hslt[part] = hsl[part].T[0:C, :]

    lane = iota((C, LANES), 1)

    def dual_step(q, carry):
        shift = lax.rem(NK - q * 8, NK)
        slope_re = pltpu.roll(hslt[0], shift, 1)
        slope_im = pltpu.roll(hslt[1], shift, 1)
        for j in range(8):
            group = q * 8 + j
            spread = lax.bitwise_and(lane, 96) + j
            s_re = jnp.take_along_axis(slope_re, spread, axis=1)
            s_im = jnp.take_along_axis(slope_im, spread, axis=1)
            w_re, w_im = packed[0, group], packed[1, group]
            dual[0, pl.ds(group, 1), :] = jnp.sum(w_re * s_re + w_im * s_im, axis=0, keepdims=True)
            dual[1, pl.ds(group, 1), :] = jnp.sum(w_re * s_im - w_im * s_re, axis=0, keepdims=True)
        return carry

    lax.fori_loop(0, 4, dual_step, 0)

    block = lax.shift_right_logical(iota((8, LANES), 1), 5)
    v_re, v_im = [], []
    for k in range(4):
        u_re, u_im = dft4(
            *(
                [dual[part, k * 8 : k * 8 + 8, :]]
                + [
                    pltpu.roll(dual[part, k * 8 : k * 8 + 8, :], LANES - 32 * m, 1)
                    for m in range(1, 4)
                ]
                for part in range(2)
            ),
            1,
        )
        turned = []
        for u in (u_re, u_im):
            value = u[0]
            for s in range(1, 4):
                value = jnp.where(block == s, pltpu.roll(u[s], 32 * s, 1), value)
            turned.append(value)
        if k:
            turned = turn(turned[0], turned[1], cos_z[k], sin_z[k], 1)
        v_re.append(turned[0])
        v_im.append(turned[1])
    v_re, v_im = dft4(v_re, v_im, 1)
    for q in range(4):
        zsend2[q * 8 : q * 8 + 8, 0:LANES] = v_re[q]
        zsend2[q * 8 : q * 8 + 8, LANES : 2 * LANES] = v_im[q]
    for i in range(1, groups_z):
        across(zsend2, zrecv2, sz2, rz2, i, False).start()
    zrecv2[mine, :] = zsend2[mine, :]
    tree_take(0)
    tree_send(1)
    for i in range(1, groups_z):
        across(zsend2, zrecv2, sz2, rz2, i, True).wait_recv()

    upper = zrecv2[...]
    lower = jnp.concatenate([-upper[:, LANES:], upper[:, :LANES]], axis=1)
    back = dot3(wyt_ref[...], jnp.concatenate([upper, lower], axis=0), NN)
    sbuf2[...] = jnp.concatenate(
        [
            back[:, part * LANES : (part + 1) * LANES].reshape(groups_y, 1, YL, LANES)
            for part in range(2)
        ],
        axis=1,
    ).reshape(groups_y * 2 * YL, LANES)
    each_far(second)
    tree_take(1)
    if len(phases) > 2:
        tree_send(2)
    own_rows = pltpu.make_async_copy(rows(sbuf2, gy, 2 * YL), rows(lines_out, gy, 2 * YL), out_sem.at[0])
    own_rows.start()

    def outer_step(step, carry):
        shift = lax.rem(NK - step * 32, NK)
        slope_re = pltpu.roll(hslt[0], shift, 1)
        slope_im = pltpu.roll(hslt[1], shift, 1)
        for j in range(32):
            k = step * 32 + j
            s_re = jnp.broadcast_to(slope_re[:, j : j + 1], (C, C))
            s_im = jnp.broadcast_to(slope_im[:, j : j + 1], (C, C))
            i_re = hin[0, pl.ds(k, 1), 0:C]
            i_im = hin[1, pl.ds(k, 1), 0:C]
            spectral[0, k] = s_re * i_re + s_im * i_im
            spectral[1, k] = s_im * i_re - s_re * i_im
        return carry

    lax.fori_loop(0, 4, outer_step, 0)
    hid[0] = dot3(plain, outside(0), NN)
    hid[5] = dot3(plain, outside(1), NN)
    for z in range(ZL):
        total = plane(sten, z * 256, 256) + coef_col[3] * hid[z] + coef_col[4] * hid[z + 2]
        put_plane(sten, z * 256, total)
    coef_small = dot3((iota((C, C), 0) == iota((C, C), 1)).astype(F32), coef, NT)
    before_y, after_y = outside(2), outside(3)
    edges = jnp.concatenate(
        [side[z * C : (z + 1) * C] for side in (before_y, after_y) for z in range(ZL)], axis=1
    )
    edge_hidden = dot3(mix, edges, TN)
    for z in range(ZL):
        for side, y in enumerate((0, YL - 1)):
            at = pl.ds(z * 256 + y, C, stride=YL)
            for half in range(2):
                column = (side * ZL + z) * NX + half * LANES
                sten[half, at, :] = (
                    sten[half, at, :]
                    + coef_small[:, 1 + side : 2 + side]
                    * edge_hidden[:, column : column + LANES]
                )
    if len(phases) > 2:
        tree_take(2)

    each(first, "wait_send")
    each(second, "wait_send")
    for copy, sends, _ in halos:
        pl.when(sends)(copy.wait_send)
    for i in range(1, groups_z):
        across(zsend, zrecv, sz, rz, i, False).wait_send()
        across(zsend2, zrecv2, sz2, rz2, i, False).wait_send()
    for phase in range(len(phases)):
        for i in range(1, place(phase)[0]):
            piece(phase, i, False).wait_send()
    each(second_in, "wait_recv")
    own_rows.wait()


def result_kernel(
    lines, sten, spectral, red, wx_ref,
    grad_input, grad_spectral, grad_mix, grad_coef,
    cells, field, mix_out, coef_out, out_sem,
):
    modes_x = wx_ref.shape[0] // 2
    out = pltpu.make_async_copy(spectral, grad_spectral, out_sem.at[0])
    out.start()
    mix_out[0:16, :] = red[:, 0:C]
    mix_out[16:32, :] = red[:, C : 2 * C]
    coef_out[...] = red[0:5, 2 * C : 3 * C]
    small = [
        pltpu.make_async_copy(mix_out, grad_mix, out_sem.at[1]),
        pltpu.make_async_copy(coef_out, grad_coef, out_sem.at[2]),
    ]
    for copy in small:
        copy.start()
    spread = jnp.concatenate(
        [
            jnp.concatenate(
                [lines[pl.ds(part * YL + y, modes_x, stride=2 * YL), :] for y in range(YL)], axis=1
            )
            for part in range(2)
        ],
        axis=0,
    )
    result = dot3(spread, wx_ref[...], TN)
    for y in range(YL):
        for half in range(2):
            cells[half, pl.ds(y, LANES, stride=YL), :] = result[
                y * LANES : (y + 1) * LANES, half * LANES : (half + 1) * LANES
            ]
    planes = []
    for z in range(ZL):
        total = plane(cells, z * 256, 256) + plane(sten, z * 256, 256)
        field[z] = total.reshape(C, YL, NX)
        planes.append(pltpu.make_async_copy(field.at[z], grad_input.at[:, z], out_sem.at[3 + z]))
        planes[-1].start()
    for copy in planes + small + [out]:
        copy.wait()


def per_device(input_field, pre_activation, cotangent, spectral_weights, mix_weights, coefficients):
    groups_y = lax.axis_size("gy")
    groups_z = lax.axis_size("gz")
    grid_y = YL * groups_y
    modes_x = groups_y
    cell_total = NX * grid_y * ZL * groups_z
    phases = ((0, groups_z), (1, 8), (8, 4)) if groups_y == 32 else ((0, groups_z), (1, 4))
    rows_y = groups_y * YL
    cos_x, sin_x = table(NX, modes_x)
    cos_y, sin_y = table(grid_y, 32)
    wx = np.concatenate([cos_x, -sin_x]).astype(np.float32)
    wy = np.concatenate([cos_y, sin_y]).astype(np.float32)
    cell = np.arange(LANES) // C
    tw = np.stack(
        [fn(2.0 * math.pi * k * cell / 16.0) for k in range(4) for fn in (np.cos, np.sin)]
    ).astype(np.float32)
    weights = spectral_weights.reshape(2, NK, C, C)
    vmem = pl.BlockSpec(memory_space=pltpu.VMEM)
    hbm = pl.BlockSpec(memory_space=pltpu.HBM)
    sds = jax.ShapeDtypeStruct
    dma = pltpu.SemaphoreType.DMA
    lines, sten, spectral, red = pl.pallas_call(
        functools.partial(exchange_kernel, groups_y, groups_z, phases, cell_total),
        name="exchange",
        out_shape=(
            pltpu.VMEM((2 * rows_y, LANES), F32),
            pltpu.VMEM((2, ZL * 256, LANES), F32),
            pltpu.VMEM((2, NK, C, C), F32),
            pltpu.VMEM((16, LANES), F32),
        ),
        in_specs=[hbm] * 10,
        out_specs=(vmem,) * 4,
        scratch_shapes=[
            pltpu.VMEM((C, C), F32),
            pltpu.VMEM((5, C), F32),
            pltpu.VMEM(wx.shape, F32),
            pltpu.VMEM(wy.shape, F32),
            pltpu.VMEM(wy.T.shape, F32),
            pltpu.VMEM(tw.shape, F32),
            pltpu.VMEM((C, ZL, YL, NX), F32),
            pltpu.VMEM((C, ZL, YL, NX), F32),
            pltpu.VMEM((C, ZL, YL, NX), F32),
            pltpu.VMEM((2, NK, C, C), F32),
            pltpu.VMEM((2, ZL * 256, LANES), F32),
            pltpu.VMEM((2, ZL * 256, LANES), F32),
            pltpu.VMEM((4 * rows_y, LANES), F32),
            pltpu.VMEM((4 * rows_y, LANES), F32),
            pltpu.VMEM((32, 4 * LANES), F32),
            pltpu.VMEM((32, 4 * LANES), F32),
            pltpu.VMEM((32, 2 * LANES), F32),
            pltpu.VMEM((32, 2 * LANES), F32),
            pltpu.VMEM((2 * rows_y, LANES), F32),
            pltpu.VMEM((2, 2, ZL * C, LANES), F32),
            pltpu.VMEM((2, 2, ZL * C, LANES), F32),
            pltpu.VMEM((2, 2, 256, LANES), F32),
            pltpu.VMEM((6, 256, NX), F32),
            pltpu.VMEM((5 * C, C), F32),
            pltpu.VMEM((2, 32, C, LANES), F32),
            pltpu.VMEM((2, NK, LANES), F32),
            pltpu.VMEM((2, NK, LANES), F32),
            pltpu.VMEM((2, C, NK), F32),
            pltpu.VMEM((2, 32, LANES), F32),
            pltpu.VMEM((len(phases), 16, LANES), F32),
            pltpu.VMEM((len(phases), 8, 16, LANES), F32),
            dma((10,)),
            dma((groups_y,)), dma((groups_y,)), dma((groups_y,)), dma((groups_y,)),
            dma((groups_z,)), dma((groups_z,)), dma((groups_z,)), dma((groups_z,)),
            dma((4,)), dma((4,)),
            dma((len(phases), 8)), dma((len(phases), 8)),
            dma((1,)),
        ],
        compiler_params=pltpu.CompilerParams(
            collective_id=0, has_side_effects=True, vmem_limit_bytes=40 << 20
        ),
    )(
        *(
            pltpu.with_memory_space_constraint(operand, pltpu.HBM)
            for operand in (
                input_field, pre_activation, cotangent, weights, mix_weights, coefficients,
                jnp.asarray(wx), jnp.asarray(wy), jnp.asarray(wy.T.copy()), jnp.asarray(tw),
            )
        )
    )
    grad_input, grad_spectral, grad_mix, grad_coef = pl.pallas_call(
        result_kernel,
        name="result",
        out_shape=(
            sds((C, ZL, YL, NX), F32),
            sds((2, NK, C, C), F32),
            sds((C, C), F32),
            sds((5, C), F32),
        ),
        in_specs=[vmem] * 5,
        out_specs=(hbm,) * 4,
        scratch_shapes=[
            pltpu.VMEM((2, ZL * 256, LANES), F32),
            pltpu.VMEM((ZL, C, YL, NX), F32),
            pltpu.VMEM((C, C), F32),
            pltpu.VMEM((5, C), F32),
            dma((3 + ZL,)),
        ],
        compiler_params=pltpu.CompilerParams(vmem_limit_bytes=24 << 20),
    )(lines, sten, spectral, red, jnp.asarray(wx))
    return (grad_input, grad_spectral.reshape(spectral_weights.shape), grad_mix, grad_coef)


def solution(mesh):
    in_specs = (
        P(None, "gz", "gy", None),
        P(None, "gz", "gy", None),
        P(None, "gz", "gy", None),
        P(None, None, "gz", "gy", None, None),
        P(),
        P(),
    )
    out_specs = (P(None, "gz", "gy", None), P(None, None, "gz", "gy", None, None), P(), P())
    return jax.shard_map(
        per_device, mesh=mesh, in_specs=in_specs, out_specs=out_specs, check_vma=False
    )
```
